32 devices in a mesh: section: 4 (over y, x), member: 8 (over z, core).
Axes of the slice: x: 2, y: 2, z: 4, core: 2. Of those that a mesh axis runs over, the one named last changes fastest.
Arguments:
- populations: float32 [64, 19, 4096], P(('section', 'member'))
- fluid_mask: int32 [64, 4096], P(('section', 'member')), may hold values 0 or 1
- section_level: int32 [4], replicated, may hold values from 0 to 2, as said below
- neighbours: int32 [64, 18], P(('section', 'member')), may hold values from -1 to 63, as said below
- interface: int32 [64, 6, 4], P(('section', 'member')), may hold values from -1 to 63, as said below
Outputs:
- final_populations: float32 [64, 19, 4096], P(('section', 'member'))
The draws below stay inside these ranges and needn't reach their ends.
Inputs may be any that keep to these rules, and one draw needn't show every extreme that they name: `section_level`: levels never fall along the section axis and each of 0, 1, 2 is held by some section. `neighbours`: A neighbour lies in the same section as the block, on the same member index or one beside it. `interface`: entries stand only on faces whose neighbour is -1; the named blocks lie in a section whose level differs from the block's by one, on the same member index or one beside it. Where that level is below the block's, exactly one quadrant of the face is named, else all four.
All inputs are finite; a program needn't handle non-finite values. No bound on the sum of `fluid_mask` on one device may be relied on, other than what follows from the above.
Results may differ from the reference program's by a relative error of at most 0.0003.
Values sent between devices are 32-bit elements; how exact they have to be, the bound alone decides.
No kernel may reach another device: no remote copies, remote signals or barrier semaphores. Data moves between devices by JAX's collectives and lax.ppermute only.
A program may use at most 64 MiB of HBM per device.

```python
import jax
import jax.numpy as jnp
from jax import lax

EDGE = 16
CELLS = 4096
BLK_DEV = 2
BLOCKS = 64
PACK = 7936
N_SECTION = 4
N_MEMBER = 8


VELOCITY_TABLE = ((0, 0, 0), (1, 0, 0), (-1, 0, 0), (0, 1, 0), (0, -1, 0), (0, 0, 1), (0, 0, -1), (1, 1, 0), (-1, -1, 0), (1, -1, 0), (-1, 1, 0), (1, 0, 1), (-1, 0, -1), (1, 0, -1), (-1, 0, 1), (0, 1, 1), (0, -1, -1), (0, 1, -1), (0, -1, 1))


WEIGHT_TABLE = (1.0 / 3.0,) + (1.0 / 18.0,) * 6 + (1.0 / 36.0,) * 12


def geometry(key):
    sections = jnp.arange(N_SECTION)
    cut_one = jax.random.randint(jax.random.fold_in(key, 11), (), 1, N_SECTION - 1)
    cut_two = jax.random.randint(jax.random.fold_in(key, 12), (), cut_one + 1, N_SECTION)
    levels = (sections >= cut_one).astype(jnp.int32) + (sections >= cut_two).astype(jnp.int32)
    blocks = jnp.arange(BLOCKS)
    block_section = blocks // (N_MEMBER * BLK_DEV)
    block_member = blocks // BLK_DEV % N_MEMBER
    step = jax.random.randint(jax.random.fold_in(key, 13), (BLOCKS, 18), -1, 2)
    member_next = jnp.clip(block_member[:, None] + step, 0, N_MEMBER - 1)
    within = jax.random.randint(jax.random.fold_in(key, 14), (BLOCKS, 18), 0, BLK_DEV)
    present = jax.random.randint(jax.random.fold_in(key, 15), (BLOCKS, 18), 0, 8) < 6
    block_ids = jnp.where(present, (block_section[:, None] * N_MEMBER + member_next) * BLK_DEV + within, -1)
    special = cut_two * N_MEMBER * BLK_DEV - 1
    block_ids = block_ids.at[0, 0].set(-1).at[BLOCKS - 1, 0].set(BLOCKS - 1).at[special, 0].set(-1).astype(jnp.int32)
    own_level = levels[block_section]
    scores = jax.random.randint(jax.random.fold_in(key, 16), (BLOCKS, 6, N_SECTION), 0, 1000) * N_SECTION + sections
    valid = jnp.abs(levels[None, None, :] - own_level[:, None, None]) == 1
    chosen = jnp.argmax(jnp.where(valid, scores, -1), axis=2)
    coarser = levels[chosen] < own_level[:, None]
    quadrant = jax.random.randint(jax.random.fold_in(key, 17), (BLOCKS, 6), 0, 4)
    step_four = jax.random.randint(jax.random.fold_in(key, 18), (BLOCKS, 6, 4), -1, 2)
    member_four = jnp.clip(block_member[:, None, None] + step_four, 0, N_MEMBER - 1)
    within_four = jax.random.randint(jax.random.fold_in(key, 19), (BLOCKS, 6, 4), 0, BLK_DEV)
    source = (chosen[:, :, None] * N_MEMBER + member_four) * BLK_DEV + within_four
    used = (block_ids[:, :6] == -1) & (jax.random.randint(jax.random.fold_in(key, 20), (BLOCKS, 6), 0, 4) < 3)
    keep = jnp.where(coarser[:, :, None], jnp.arange(4)[None, None, :] == quadrant[:, :, None], True)
    links = jnp.where(used[:, :, None] & keep, source, -1)
    links = links.at[special, 0].set(jnp.full((4,), BLOCKS - 1, links.dtype)).astype(jnp.int32)
    return (levels, block_ids, links)


def draw_section_level(key, part):
    return geometry(key)[0]


def draw_neighbours(key, part):
    return geometry(key)[1]


def draw_interface(key, part):
    return geometry(key)[2]


def draw_populations(key, part):
    lattice = jnp.array(VELOCITY_TABLE, jnp.float32)
    weight_vector = jnp.array(WEIGHT_TABLE, jnp.float32)
    flow = jax.random.uniform(jax.random.fold_in(key, 1), (BLOCKS, 3, CELLS), jnp.float32, -0.05, 0.05)
    along = lattice[None, :, 0, None] * flow[:, None, 0, :] + lattice[None, :, 1, None] * flow[:, None, 1, :] + lattice[None, :, 2, None] * flow[:, None, 2, :]
    noise = 0.25 * jnp.clip(jax.random.normal(jax.random.fold_in(key, 2), (BLOCKS, 19, CELLS), jnp.float32), -2.5, 2.5)
    values = weight_vector[None, :, None] * (1.0 + 3.0 * along + noise)
    return values.astype(jnp.float32)


def place_ends(drawn, own_key, low, top_value):
    place = [jax.random.randint(jax.random.fold_in(own_key, axis), (), 0, length) for axis, length in enumerate(drawn.shape)]
    main_axis = drawn.shape.index(max(drawn.shape))
    beside = place[:main_axis] + [(place[main_axis] + 1) % drawn.shape[main_axis]] + place[main_axis + 1:]
    return drawn.at[tuple(place)].set(low).at[tuple(beside)].set(top_value)


def setup_inputs(seed: int = 0) -> dict:
    key_list = jax.random.split(jax.random.key(seed), 6)
    populations = draw_populations(jax.random.fold_in(key_list[5], 71), 0)
    fluid_mask = place_ends((jax.random.randint(key_list[1], (BLOCKS, CELLS), 0, 8) < 7).astype(jnp.int32), jax.random.fold_in(key_list[1], 1), 0, 1)
    section_level = draw_section_level(jax.random.fold_in(key_list[5], 71), 0)
    neighbours = draw_neighbours(jax.random.fold_in(key_list[5], 71), 0)
    interface = draw_interface(jax.random.fold_in(key_list[5], 71), 0)
    return dict(populations=populations, fluid_mask=fluid_mask, section_level=section_level, neighbours=neighbours, interface=interface)


VELOCITIES = ((0, 0, 0), (1, 0, 0), (-1, 0, 0), (0, 1, 0), (0, -1, 0), (0, 0, 1), (0, 0, -1),
              (1, 1, 0), (-1, -1, 0), (1, -1, 0), (-1, 1, 0), (1, 0, 1), (-1, 0, -1), (1, 0, -1),
              (-1, 0, 1), (0, 1, 1), (0, -1, -1), (0, 1, -1), (0, -1, 1))
WEIGHTS = (1.0 / 3.0,) + (1.0 / 18.0,) * 6 + (1.0 / 36.0,) * 12
OPPOSITE = (0, 2, 1, 4, 3, 6, 5, 8, 7, 10, 9, 12, 11, 14, 13, 16, 15, 18, 17)
HIGH = lax.Precision.HIGHEST


def export_lists():
    result = []
    for j in range(6):
        side = VELOCITIES[1 + j]
        result.append([q for q in range(19) if sum(a * b for a, b in zip(VELOCITIES[q], side)) == 1])
    return result


def relax_rate(level):
    return jnp.where(level == 0, 1.0 / 0.55, jnp.where(level == 1, 1.0 / 0.6, 1.0 / 0.7)).astype(jnp.float32)


def collide(current, fluid, rate):
    lattice = jnp.array(VELOCITIES, jnp.float32)
    weight_vector = jnp.array(WEIGHTS, jnp.float32)
    density = jnp.sum(current, axis=1)
    momentum = jnp.einsum('nqc,qd->ndc', current, lattice, precision=HIGH)
    velocity = momentum / density[:, None, :]
    along = jnp.einsum('qd,ndc->nqc', lattice, velocity, precision=HIGH)
    speed_square = jnp.sum(velocity * velocity, axis=1)
    equilibrium = weight_vector[None, :, None] * density[:, None, :] * (
        1.0 + 3.0 * along + 4.5 * along * along - 1.5 * speed_square[:, None, :])
    relaxed = current - rate * (current - equilibrium)
    bounced = jnp.stack([current[:, o] for o in OPPOSITE], axis=1)
    return jnp.where(fluid[:, None, :] == 1, relaxed, bounced)


def export(current):
    count = current.shape[0]
    blocks_view = current.reshape(count, 19, EDGE, EDGE, EDGE)
    lists = export_lists()
    pieces = []
    for j in range(6):
        layer_index = EDGE - 1 if j % 2 == 0 else 0
        chosen = jnp.stack([blocks_view[:, q] for q in lists[j]], axis=1)
        plane_data = jnp.take(chosen, layer_index, axis=2 + j // 2)
        pieces.append(plane_data.reshape(count, 5 * EDGE * EDGE))
    for j in range(12):
        direction = VELOCITIES[7 + j]
        index_list = [slice(None)]
        for a in range(3):
            if direction[a] > 0:
                index_list.append(EDGE - 1)
            elif direction[a] < 0:
                index_list.append(0)
            else:
                index_list.append(slice(None))
        pieces.append(blocks_view[:, 7 + j][tuple(index_list)])
    flat = jnp.concatenate(pieces, axis=1)
    return jnp.pad(flat, ((0, 0), (0, PACK - flat.shape[1])))


def quadrant_tables():
    half = EDGE // 2
    places = jnp.arange(EDGE)
    tables = []
    for k in range(4):
        first = (places[None, :] == half * (k // 2) + places[:, None] // 2).astype(jnp.float32)
        second = (places[None, :] == half * (k % 2) + places[:, None] // 2).astype(jnp.float32)
        tables.append(jnp.einsum('ai,bj->ijab', first, second, precision=HIGH).reshape(EDGE * EDGE, EDGE * EDGE))
    prolong = jnp.stack(tables, axis=0)
    restrict = 0.25 * jnp.transpose(prolong, (0, 2, 1))
    return prolong, restrict


def boundary_data(neighbour_rows, neighbour_ok, link_rows, link_ok, coarse_source):
    count = neighbour_rows.shape[0]
    area = EDGE * EDGE
    face_size = 5 * area
    lists = export_lists()
    face_list = []
    link_list = []
    edge_list = []
    for j in range(6):
        start = (j ^ 1) * face_size
        face_list.append(neighbour_rows[:, j, start:start + face_size].reshape(count, 5, area))
        link_list.append(link_rows[:, j, :, start:start + face_size].reshape(count, 4, 5, area))
    for j in range(12):
        start = 30 * area + (j ^ 1) * EDGE
        edge_list.append(neighbour_rows[:, 6 + j, start:start + EDGE])
    face_planes = jnp.stack(face_list, axis=1)
    link_planes = jnp.stack(link_list, axis=1)
    edge_planes = jnp.stack(edge_list, axis=1)
    prolong, restrict = quadrant_tables()
    upward = jnp.einsum('njkpi,kio->njkpo', link_planes, prolong, precision=HIGH)
    downward = jnp.einsum('njkpi,kio->njkpo', link_planes, restrict, precision=HIGH)
    mapped = jnp.where(link_ok[:, :, :, None, None],
                       jnp.where(coarse_source[:, :, :, None, None], upward, downward), 0.0)
    link_sum = jnp.sum(mapped, axis=2)
    has_link = jnp.any(link_ok, axis=2)
    rest_faces = jnp.array([[WEIGHTS[q] for q in lists[j ^ 1]] for j in range(6)], jnp.float32)
    faces_out = jnp.where(neighbour_ok[:, :6, None, None], face_planes,
                          jnp.where(has_link[:, :, None, None], link_sum, rest_faces[None, :, :, None]))
    edges_out = jnp.where(neighbour_ok[:, 6:, None], edge_planes, jnp.float32(1.0 / 36.0))
    return faces_out, edges_out


def stream(current, face_planes, edge_lines):
    count = current.shape[0]
    blocks_view = current.reshape(count, 19, EDGE, EDGE, EDGE)
    lists = export_lists()
    outputs = []
    for q in range(19):
        direction = VELOCITIES[q]
        padded = jnp.pad(blocks_view[:, q], ((0, 0), (1, 1), (1, 1), (1, 1)))
        moving = [a for a in range(3) if direction[a] != 0]
        for a in moving:
            toward = -direction[a]
            slot = 2 * a + (0 if toward > 0 else 1)
            position = lists[slot ^ 1].index(q)
            index_list = [slice(None)] + [slice(1, EDGE + 1)] * 3
            index_list[1 + a] = EDGE + 1 if toward > 0 else 0
            padded = padded.at[tuple(index_list)].set(face_planes[:, slot, position].reshape(count, EDGE, EDGE))
        if len(moving) == 2:
            slot = VELOCITIES.index(tuple(-v for v in direction)) - 7
            index_list = [slice(None)] + [slice(1, EDGE + 1)] * 3
            for a in moving:
                index_list[1 + a] = EDGE + 1 if direction[a] < 0 else 0
            padded = padded.at[tuple(index_list)].set(edge_lines[:, slot])
        shifted = padded[:, 1 - direction[0]:1 - direction[0] + EDGE,
                         1 - direction[1]:1 - direction[1] + EDGE,
                         1 - direction[2]:1 - direction[2] + EDGE]
        outputs.append(shifted.reshape(count, CELLS))
    return jnp.stack(outputs, axis=1)


def reference(populations, fluid_mask, section_level, neighbours, interface):
    groups = BLOCKS // BLK_DEV
    group_level = section_level[jnp.arange(groups) // N_MEMBER]
    fluid_groups = fluid_mask.reshape(groups, BLK_DEV, CELLS)
    neighbour_groups = neighbours.reshape(groups, BLK_DEV, 18)
    link_groups = interface.reshape(groups, BLK_DEV, 6, 4)
    current = populations.reshape(groups, BLK_DEV, 19, CELLS)
    for k in range(2):
        if k == 0:
            advances = group_level >= 1
        else:
            advances = group_level == 2

        def post_collision(inputs):
            block_pops, block_fluid, level_here, moves = inputs
            starred = collide(block_pops, block_fluid, relax_rate(level_here))
            return jnp.where(moves, starred, block_pops)

        starred = lax.map(post_collision, (current, fluid_groups, group_level, advances))
        exports = lax.map(export, starred).reshape(BLOCKS, PACK)

        def advance_group(inputs):
            block_star, block_old, block_ids, link_ids, level_here, moves = inputs
            neighbour_rows = exports[jnp.maximum(block_ids, 0)]
            link_rows = exports[jnp.maximum(link_ids, 0)]
            source_level = section_level[jnp.maximum(link_ids, 0) // (N_MEMBER * BLK_DEV)]
            face_planes, edge_lines = boundary_data(neighbour_rows, block_ids >= 0, link_rows, link_ids >= 0,
                                                    source_level < level_here)
            moved = stream(block_star, face_planes, edge_lines)
            return jnp.where(moves, moved, block_old)

        current = lax.map(advance_group, (starred, current, neighbour_groups, link_groups, group_level, advances))
    return current.reshape(BLOCKS, 19, CELLS)
```

```python
import functools

import jax
import jax.numpy as jnp
from jax import lax
from jax.experimental import pallas as pl
from jax.experimental.pallas import tpu as pltpu
from jax.sharding import PartitionSpec as P

VELOCITIES = (
    (0, 0, 0), (1, 0, 0), (-1, 0, 0), (0, 1, 0), (0, -1, 0), (0, 0, 1), (0, 0, -1),
    (1, 1, 0), (-1, -1, 0), (1, -1, 0), (-1, 1, 0), (1, 0, 1), (-1, 0, -1), (1, 0, -1),
    (-1, 0, 1), (0, 1, 1), (0, -1, -1), (0, 1, -1), (0, -1, 1),
)
WEIGHTS = (1.0 / 3.0,) + (1.0 / 18.0,) * 6 + (1.0 / 36.0,) * 12
OPPOSITE = (0, 2, 1, 4, 3, 6, 5, 8, 7, 10, 9, 12, 11, 14, 13, 16, 15, 18, 17)
LISTS = [
    [q for q in range(19) if sum(a * b for a, b in zip(VELOCITIES[q], VELOCITIES[1 + j])) == 1]
    for j in range(6)
]
ROWS = 64
TILES = 8


def iotas():
    sub = lax.broadcasted_iota(jnp.int32, (8, 128), 0)
    lane = lax.broadcasted_iota(jnp.int32, (8, 128), 1)
    return sub, lane


def pick(x, index):
    return jnp.take_along_axis(x, index, axis=1, mode="promise_in_bounds")


def lanes(x, shift):
    return pltpu.roll(x, shift % 128, 1)


def subs(x, shift):
    return pltpu.roll(x, shift % 8, 0)


def tile(ref, q, t):
    return ref[q, 8 * t : 8 * t + 8, :]


def bulk(ref, row):
    return jnp.broadcast_to(ref[row : row + 1, :], (8, 128))


def relax_rate(level):
    return jnp.where(
        level == 0, jnp.float32(1.0 / 0.55), jnp.where(level == 1, jnp.float32(1.0 / 0.6), jnp.float32(1.0 / 0.7))
    )


def collide(src, dst, mask, rate):
    for t in range(TILES):
        f = [tile(src, q, t) for q in range(19)]
        density = f[0]
        for q in range(1, 19):
            density = density + f[q]
        velocity = []
        for a in range(3):
            plus = [q for q in range(19) if VELOCITIES[q][a] > 0]
            total = f[plus[0]] - f[OPPOSITE[plus[0]]]
            for q in plus[1:]:
                total = total + (f[q] - f[OPPOSITE[q]])
            velocity.append(total / density)
        speed = velocity[0] * velocity[0] + velocity[1] * velocity[1] + velocity[2] * velocity[2]
        base = 1.0 - 1.5 * speed
        fluid = mask[8 * t : 8 * t + 8, :] == 1
        keep = 1.0 - rate
        scaled = [rate * jnp.float32(w) * density for w in (WEIGHTS[0], WEIGHTS[1], WEIGHTS[7])]
        out = keep * f[0] + scaled[0] * base
        dst[0, 8 * t : 8 * t + 8, :] = jnp.where(fluid, out, f[0])
        for q in range(1, 19, 2):
            o = OPPOSITE[q]
            along = None
            for a in range(3):
                c = VELOCITIES[q][a]
                if c:
                    term = velocity[a] if c > 0 else -velocity[a]
                    along = term if along is None else along + term
            weight = scaled[1] if q < 7 else scaled[2]
            even = base + 4.5 * along * along
            odd = 3.0 * along
            dst[q, 8 * t : 8 * t + 8, :] = jnp.where(fluid, keep * f[q] + weight * (even + odd), f[o])
            dst[o, 8 * t : 8 * t + 8, :] = jnp.where(fluid, keep * f[o] + weight * (even - odd), f[q])


def export(src, out):
    sub, lane = iotas()
    xl, yh = sub // 4, (sub // 2) % 2
    for j in range(6):
        axis, high = j // 2, j % 2 == 0
        for i, q in enumerate(LISTS[j]):
            if axis == 0:
                v = tile(src, q, TILES - 1 if high else 0)
                first = 4 if high else 0
                for h in range(2):
                    for b in range(2):
                        s = first + 2 * h + b
                        r = 10 * j + 5 * h + i
                        out[b, r : r + 1, :] = v[s : s + 1, :]
                continue
            for h in range(2):
                total = jnp.zeros((8, 128), jnp.float32)
                for k in range(4):
                    if axis == 1:
                        index = (lane & 15) + (112 if high else 0)
                        here = (lane >> 4 == 2 * k + xl) & (yh == (1 if high else 0))
                    else:
                        index = (lane & 7) * 16 + (15 if high else 0)
                        here = lane >> 3 == (2 * k + xl) * 2 + yh
                    total = jnp.where(here, pick(tile(src, q, 4 * h + k), index), total)
                total = total + subs(total, 4)
                total = total + subs(total, 2)
                for b in range(2):
                    r = 10 * j + 5 * h + i
                    out[b, r : r + 1, :] = total[b : b + 1, :]


def slots(block_id, me, sections, members, blocks):
    safe = jnp.maximum(block_id, 0)
    section = safe // (members * blocks)
    member = (safe // blocks) % members
    offset = member - me[1]
    chip = jnp.where(me[1] % 2 == 0, 1, -1)
    which = jnp.where(offset == 0, 0, jnp.where(offset == chip, 1, 2))
    if sections & (sections - 1) == 0:
        apart = section ^ me[0]
    else:
        apart = (me[0] + sections - section) % sections
    slot = (which * sections + apart) * blocks + safe % blocks
    return jnp.where(block_id >= 0, slot, 0), section


def arrived(level_ref, near_ref, link_ref, table, halo, me, sizes):
    sections, members, blocks = sizes
    sub, lane = iotas()
    level = level_ref[me[0]]
    for block in range(blocks):
        for j in range(6):
            first = 10 * (j ^ 1)

            def rows(slot, part):
                return table[slot, first + 5 * part : first + 5 * part + 5, :]

            near_id = near_ref[block, j]
            near, _ = slots(near_id, me, sections, members, blocks)
            ids = [link_ref[block, k, j] for k in range(4)]
            placed = [slots(i, me, sections, members, blocks) for i in ids]
            coarse = [(ids[k] >= 0) & (level_ref[placed[k][1]] < level) for k in range(4)]
            fine = [(ids[k] >= 0) & (level_ref[placed[k][1]] >= level) for k in range(4)]
            any_coarse = coarse[0] | coarse[1] | coarse[2] | coarse[3]
            any_fine = fine[0] | fine[1] | fine[2] | fine[3]
            rest = [WEIGHTS[q] for q in LISTS[j ^ 1]]

            @pl.when(near_id >= 0)
            def _():
                halo[block, 10 * j : 10 * j + 10, :] = table[near, first : first + 10, :]

            @pl.when((near_id < 0) & any_coarse)
            def _():
                slot = jnp.where(
                    coarse[0], placed[0][0], jnp.where(coarse[1], placed[1][0], jnp.where(coarse[2], placed[2][0], placed[3][0]))
                )
                a = jnp.where(coarse[0] | coarse[1], 0, 1)
                b = jnp.where(coarse[0] | (coarse[2] & jnp.logical_not(coarse[1])), 0, 1)
                source = jnp.where(a == 0, rows(slot, 0), rows(slot, 1))
                for h in range(2):
                    index = (4 * h + (lane[:5] >> 5)) * 16 + 8 * b + ((lane[:5] & 15) >> 1)
                    halo[block, 10 * j + 5 * h : 10 * j + 5 * h + 5, :] = pick(source, index)

            @pl.when((near_id < 0) & jnp.logical_not(any_coarse) & any_fine)
            def _():
                index = (lane[:5] >> 4) % 4 * 32 + 2 * (lane[:5] & 7)
                quads = []
                for k in range(4):
                    parts = []
                    for h in range(2):
                        v = rows(placed[k][0], h)
                        v = v + lanes(v, -1)
                        v = v + lanes(v, -16)
                        parts.append(pick(v, index))
                    quad = jnp.where(lane[:5] >= 64, parts[1], parts[0])
                    quads.append(quad * jnp.where(fine[k], jnp.float32(0.25), jnp.float32(0.0)))
                for a in range(2):
                    halo[block, 10 * j + 5 * a : 10 * j + 5 * a + 5, :] = jnp.where(
                        lane[:5] & 8 == 0, quads[2 * a], quads[2 * a + 1]
                    )

            @pl.when((near_id < 0) & jnp.logical_not(any_coarse | any_fine))
            def _():
                for h in range(2):
                    for i in range(5):
                        r = 10 * j + 5 * h + i
                        halo[block, r : r + 1, :] = jnp.full((1, 128), rest[i], jnp.float32)


def stream(src, dst, near_ref, table, halo, me, sizes):
    sections, members, blocks = sizes
    sub, lane = iotas()
    odd = (sub & 1) == 1
    xl, yh = sub // 4, (sub // 2) % 2
    z = lane & 15
    bases = [(2 * k + xl) * 16 for k in range(4)]

    def plane(j, i, h):
        return jnp.where(odd, bulk(halo.at[1], 10 * j + 5 * h + i), bulk(halo.at[0], 10 * j + 5 * h + i))

    for q in range(19):
        c = VELOCITIES[q]
        moving = [a for a in range(3) if c[a]]
        values = [tile(src, q, t) for t in range(TILES)]
        planes = {}
        for a in moving:
            j = 2 * a + (0 if c[a] < 0 else 1)
            i = LISTS[j ^ 1].index(q)
            planes[a] = [plane(j, i, h) for h in range(2)]
        line = None
        if len(moving) == 2:
            e = VELOCITIES.index(tuple(-v for v in c)) - 1
            j = 2 * moving[0] + (0 if c[moving[0]] > 0 else 1)
            i = LISTS[j].index(q)
            found = []
            for block in range(blocks):
                block_id = near_ref[block, e]
                slot, _ = slots(block_id, me, sections, members, blocks)
                good = jnp.full((8, 128), block_id, jnp.int32) >= 0
                found.append(
                    [jnp.where(good, bulk(table.at[slot], 10 * j + 5 * h + i), jnp.float32(WEIGHTS[q])) for h in range(2)]
                )
            line = [jnp.where(odd, found[1][h], found[0][h]) for h in range(2)]
        outside = jnp.where(yh == 1, planes[0][1], planes[0][0]) if c[0] else None

        if c[2]:
            up = c[2] > 0
            edge = z == (0 if up else 15)
            if not c[0] or c[2]:
                values = [
                    jnp.where(edge, pick(planes[2][t // 4], bases[t % 4] + yh * 8 + (lane >> 4)), lanes(v, c[2]))
                    for t, v in enumerate(values)
                ]
            if c[0]:
                spread = jnp.where(yh == 1, line[1], line[0])
                outside = jnp.where(edge, lanes(spread, -15 if up else 15), lanes(outside, c[2]))
        if c[1]:
            up = c[1] > 0
            edge = lane < 16 if up else lane >= 112
            inner = yh == (1 if up else 0)

            def moved(v, border):
                rolled = lanes(v, 16 * c[1])
                return jnp.where(edge, jnp.where(inner, subs(rolled, 2 * c[1]), border), rolled)

            for t in range(TILES):
                base, source = bases[t % 4], planes[1][t // 4]
                if c[2]:
                    if c[2] > 0:
                        border = jnp.where(z == 0, pick(line[t // 4], base + 15), pick(source, base + jnp.maximum(z - 1, 0)))
                    else:
                        border = jnp.where(z == 15, pick(line[t // 4], base), pick(source, base + jnp.minimum(z + 1, 15)))
                else:
                    border = pick(source, base + z)
                values[t] = moved(values[t], border)
            if c[0]:
                outside = moved(outside, lanes(line[1 if up else 0], 16 * c[1]))
        if c[0]:
            rolled = [subs(v, 4) for v in values]
            if c[0] > 0:
                values = [jnp.where(sub < 4, rolled[t - 1] if t else outside, rolled[t]) for t in range(TILES)]
            else:
                values = [
                    jnp.where(sub >= 4, rolled[t + 1] if t < TILES - 1 else outside, rolled[t]) for t in range(TILES)
                ]
        for t in range(TILES):
            dst[q, 8 * t : 8 * t + 8, :] = values[t]


def first_kernel(sizes, level_ref, pops, mask, star, out):
    level = level_ref[lax.axis_index("section")]

    @pl.when(level >= 1)
    def _():
        collide(pops, star, mask, relax_rate(level))

    @pl.when(level < 1)
    def _():
        star[...] = pops[...]

    export(star, out)


def fetch(sizes, parts, table, sems):
    sections, _, blocks = sizes
    each = sections * blocks
    copies = [
        pltpu.make_async_copy(part, table.at[pl.ds(each * i, each)], sems.at[i]) for i, part in enumerate(parts)
    ]
    for copy in copies:
        copy.start()
    for copy in copies:
        copy.wait()


def next_kernel(sizes, last, level_ref, near_ref, link_ref, star, mask, own, chip, far, dst, *rest):
    out = None if last else rest[0]
    table, halo, sems = rest[-3:]
    me = (lax.axis_index("section"), lax.axis_index("member"))
    level = level_ref[me[0]]
    fetch(sizes, (own, chip, far), table, sems)
    moves = level == 2 if last else level >= 1

    @pl.when(moves)
    def _():
        arrived(level_ref, near_ref, link_ref, table, halo, me, sizes)
        stream(star, dst, near_ref, table, halo, me, sizes)

    @pl.when(jnp.logical_not(moves))
    def _():
        dst[...] = star[...]

    if not last:

        @pl.when(level == 2)
        def _():
            collide(dst, dst, mask, relax_rate(level))

        export(dst, out)


def swap(x, sections, members, target):
    pairs = []
    for s in range(sections):
        for m in range(members):
            t = target(s, m)
            if 0 <= t[1] < members:
                pairs.append((s * members + m, t[0] * members + t[1]))
    return lax.ppermute(x, ("section", "member"), pairs)


def exchange(exports, sections, members):
    power = sections & (sections - 1) == 0

    def across(d):
        return lambda s, m: (s ^ d if power else (s + d) % sections, m)

    parts = [exports] + [swap(exports, sections, members, across(d)) for d in range(1, sections)]
    own = jnp.concatenate(parts, axis=0)
    chip = swap(own, sections, members, lambda s, m: (s, m ^ 1))
    far = swap(own, sections, members, lambda s, m: (s, ((m + 1) ^ 1) - 1))
    return own, chip, far


def packed(x):
    n, cells = x.shape[0], x.shape[-1]
    x = x.reshape(n, -1, cells // 128, 128)
    return x.transpose(1, 2, 0, 3).reshape(-1, n * cells // 128, 128)


VMEM = pl.BlockSpec(memory_space=pltpu.VMEM)
SMEM = pl.BlockSpec(memory_space=pltpu.SMEM)
ANY = pl.BlockSpec(memory_space=pl.ANY)


def body(populations, fluid_mask, section_level, neighbours, interface):
    sections, members = lax.axis_size("section"), lax.axis_size("member")
    blocks, _, cells = populations.shape
    sizes = (sections, members, blocks)
    params = pltpu.CompilerParams(vmem_limit_bytes=16 << 20)
    pops = packed(populations)
    mask = packed(fluid_mask)[0]
    links = interface.transpose(0, 2, 1)
    field = jax.ShapeDtypeStruct(pops.shape, jnp.float32)
    planes = jax.ShapeDtypeStruct((blocks, ROWS, 128), jnp.float32)
    star, exports = pl.pallas_call(
        functools.partial(first_kernel, sizes),
        out_shape=(field, planes),
        in_specs=[SMEM, VMEM, VMEM],
        out_specs=(VMEM, VMEM),
        compiler_params=params,
        name="first",
    )(section_level, pops, mask)
    scratch = [
        pltpu.VMEM((3 * sections * blocks, ROWS, 128), jnp.float32),
        pltpu.VMEM((blocks, ROWS, 128), jnp.float32),
        pltpu.SemaphoreType.DMA((3,)),
    ]
    for last in (False, True):
        own, chip, far = exchange(exports, sections, members)
        result = pl.pallas_call(
            functools.partial(next_kernel, sizes, last),
            out_shape=(field,) if last else (field, planes),
            in_specs=[SMEM, SMEM, SMEM, VMEM, VMEM, ANY, ANY, ANY],
            out_specs=(VMEM,) if last else (VMEM, VMEM),
            scratch_shapes=scratch,
            compiler_params=params,
            name="last" if last else "middle",
        )(section_level, neighbours, links, star, mask, own, chip, far)
        if last:
            (star,) = result
        else:
            star, exports = result
    out = star.reshape(19, cells // 128, blocks, 128).transpose(2, 0, 1, 3)
    return out.reshape(blocks, 19, cells)


def solution(mesh):
    return jax.shard_map(
        body,
        mesh=mesh,
        in_specs=(
            P(("section", "member"), None, None),
            P(("section", "member"), None),
            P(),
            P(("section", "member"), None),
            P(("section", "member"), None, None),
        ),
        out_specs=P(("section", "member"), None, None),
        check_vma=False,
    )
```

```python
import functools

import jax
import jax.numpy as jnp
from jax import lax
from jax.experimental import pallas as pl
from jax.experimental.pallas import tpu as pltpu
from jax.sharding import PartitionSpec as P

VELOCITIES = (
    (0, 0, 0), (1, 0, 0), (-1, 0, 0), (0, 1, 0), (0, -1, 0), (0, 0, 1), (0, 0, -1),
    (1, 1, 0), (-1, -1, 0), (1, -1, 0), (-1, 1, 0), (1, 0, 1), (-1, 0, -1), (1, 0, -1),
    (-1, 0, 1), (0, 1, 1), (0, -1, -1), (0, 1, -1), (0, -1, 1),
)
WEIGHTS = (1.0 / 3.0,) + (1.0 / 18.0,) * 6 + (1.0 / 36.0,) * 12
OPPOSITE = (0, 2, 1, 4, 3, 6, 5, 8, 7, 10, 9, 12, 11, 14, 13, 16, 15, 18, 17)
LISTS = [
    [q for q in range(19) if sum(a * b for a, b in zip(VELOCITIES[q], VELOCITIES[1 + j])) == 1]
    for j in range(6)
]
ROWS = 64
TILES = 8


def iotas():
    sub = lax.broadcasted_iota(jnp.int32, (8, 128), 0)
    lane = lax.broadcasted_iota(jnp.int32, (8, 128), 1)
    return sub, lane


def pick(x, index):
    return jnp.take_along_axis(x, index, axis=1, mode="promise_in_bounds")


def lanes(x, shift):
    return pltpu.roll(x, shift % 128, 1)


def subs(x, shift):
    return pltpu.roll(x, shift % 8, 0)


def tile(ref, q, t):
    return ref[q, 8 * t : 8 * t + 8, :]


def bulk(ref, row):
    return jnp.broadcast_to(ref[row : row + 1, :], (8, 128))


def relax_rate(level):
    return jnp.where(
        level == 0, jnp.float32(1.0 / 0.55), jnp.where(level == 1, jnp.float32(1.0 / 0.6), jnp.float32(1.0 / 0.7))
    )


def collide(src, dst, mask, rate, ready):
    for t in range(TILES):
        ready(t)
        f = [tile(src, q, t) for q in range(19)]
        density = f[0]
        for q in range(1, 19):
            density = density + f[q]
        velocity = []
        for a in range(3):
            plus = [q for q in range(19) if VELOCITIES[q][a] > 0]
            total = f[plus[0]] - f[OPPOSITE[plus[0]]]
            for q in plus[1:]:
                total = total + (f[q] - f[OPPOSITE[q]])
            velocity.append(total / density)
        speed = velocity[0] * velocity[0] + velocity[1] * velocity[1] + velocity[2] * velocity[2]
        base = 1.0 - 1.5 * speed
        fluid = mask[8 * t : 8 * t + 8, :] == 1
        keep = 1.0 - rate
        scaled = [rate * jnp.float32(w) * density for w in (WEIGHTS[0], WEIGHTS[1], WEIGHTS[7])]
        out = keep * f[0] + scaled[0] * base
        dst[0, 8 * t : 8 * t + 8, :] = jnp.where(fluid, out, f[0])
        for q in range(1, 19, 2):
            o = OPPOSITE[q]
            along = None
            for a in range(3):
                c = VELOCITIES[q][a]
                if c:
                    term = velocity[a] if c > 0 else -velocity[a]
                    along = term if along is None else along + term
            weight = scaled[1] if q < 7 else scaled[2]
            even = base + 4.5 * along * along
            odd = 3.0 * along
            dst[q, 8 * t : 8 * t + 8, :] = jnp.where(fluid, keep * f[q] + weight * (even + odd), f[o])
            dst[o, 8 * t : 8 * t + 8, :] = jnp.where(fluid, keep * f[o] + weight * (even - odd), f[q])


def export(src, out):
    sub, lane = iotas()
    xl, yh = sub // 4, (sub // 2) % 2
    for j in range(6):
        axis, high = j // 2, j % 2 == 0
        for i, q in enumerate(LISTS[j]):
            if axis == 0:
                v = tile(src, q, TILES - 1 if high else 0)
                first = 4 if high else 0
                for h in range(2):
                    for b in range(2):
                        s = first + 2 * h + b
                        r = 10 * j + 5 * h + i
                        out[b, r : r + 1, :] = v[s : s + 1, :]
                continue
            for h in range(2):
                total = jnp.zeros((8, 128), jnp.float32)
                for k in range(4):
                    if axis == 1:
                        index = (lane & 15) + (112 if high else 0)
                        here = (lane >> 4 == 2 * k + xl) & (yh == (1 if high else 0))
                    else:
                        index = (lane & 7) * 16 + (15 if high else 0)
                        here = lane >> 3 == (2 * k + xl) * 2 + yh
                    total = jnp.where(here, pick(tile(src, q, 4 * h + k), index), total)
                total = total + subs(total, 4)
                total = total + subs(total, 2)
                for b in range(2):
                    r = 10 * j + 5 * h + i
                    out[b, r : r + 1, :] = total[b : b + 1, :]


def divide(x, n):
    return x >> (n.bit_length() - 1) if n & (n - 1) == 0 else lax.div(x, jnp.int32(n))


def plan_rows(level_ref, near_ref, link_ref, plan, me, sizes):
    sections, members, blocks = sizes
    level = level_ref[me[0]]
    chip = jnp.where(me[1] % 2 == 0, 1, -1)

    def placed(ids):
        safe = jnp.maximum(ids, 0)
        local = divide(safe, blocks)
        within = safe - local * blocks
        section = divide(local, members)
        offset = local - section * members - me[1]
        which = jnp.where(offset == 0, 0, jnp.where(offset == chip, 1, 2))
        if sections & (sections - 1) == 0:
            apart = section ^ me[0]
        else:
            apart = me[0] - section
            apart = jnp.where(apart < 0, apart + sections, apart)
        one = (which * sections + apart) * blocks + within
        two = jnp.maximum((which * (sections - 1) + section - 1) * blocks + within, 0)
        source = jnp.zeros_like(ids)
        for s in range(sections):
            source = jnp.where(section == s, level_ref[s], source)
        return (one, two), source

    plan[0:1, 64:65] = jnp.full((1, 1), level, jnp.int32)
    for block in range(blocks):
        near = near_ref[block : block + 1, :]
        near_slots, _ = placed(near)
        links = link_ref[block]
        link_slots, source = placed(links)
        coarse = (links >= 0) & (source < level)
        fine = (links >= 0) & (source >= level)
        place = lax.broadcasted_iota(jnp.int32, links.shape, 0)
        quadrant = jnp.max(jnp.where(coarse, place, -1), axis=0, keepdims=True)
        any_fine = jnp.max(jnp.where(fine, 1, 0), axis=0, keepdims=True)
        kind = jnp.where(quadrant >= 0, 1, jnp.where(any_fine > 0, 2, 3))
        kind = jnp.where(near[:, :6] >= 0, 0, kind)
        for r in range(2):
            first = 32 * r
            plan[block : block + 1, first : first + 18] = jnp.where(near >= 0, near_slots[r], -1)
            plan[2 + 4 * block : 6 + 4 * block, first : first + 6] = jnp.where(fine, link_slots[r], -1)
            chosen = jnp.max(jnp.where(coarse, link_slots[r], -1), axis=0, keepdims=True)
            plan[10 + block : 11 + block, first : first + 6] = chosen
            plan[12 + block : 13 + block, first : first + 6] = kind
            plan[14 + block : 15 + block, first : first + 6] = quadrant


def arrived(plan, base, table, halo, blocks):
    sub, lane = iotas()
    sub, lane = sub[:5], lane[:5]
    for block in range(blocks):
        for j in range(6):
            first = 10 * (j ^ 1)
            kind = plan[12 + block, base + j]

            def rows(slot, part):
                return table[slot, first + 5 * part : first + 5 * part + 5, :]

            @pl.when(kind == 0)
            def _():
                halo[block, 10 * j : 10 * j + 10, :] = table[plan[block, base + j], first : first + 10, :]

            @pl.when(kind == 1)
            def _():
                slot = plan[10 + block, base + j]
                quadrant = plan[14 + block, base + j]
                low = jnp.full((5, 128), quadrant, jnp.int32) < 2
                source = jnp.where(low, rows(slot, 0), rows(slot, 1))
                shift = 8 * (quadrant & 1)
                for h in range(2):
                    index = (4 * h + (lane >> 5)) * 16 + shift + ((lane & 15) >> 1)
                    halo[block, 10 * j + 5 * h : 10 * j + 5 * h + 5, :] = pick(source, index)

            @pl.when(kind == 2)
            def _():
                index = ((lane >> 4) & 3) * 32 + 2 * (lane & 7)
                quads = []
                for k in range(4):
                    slot = plan[2 + 4 * block + k, base + j]
                    scale = jnp.where(slot >= 0, jnp.float32(0.25), jnp.float32(0.0))
                    slot = jnp.maximum(slot, 0)
                    parts = []
                    for h in range(2):
                        v = rows(slot, h)
                        v = v + lanes(v, -1)
                        v = v + lanes(v, -16)
                        parts.append(pick(v, index))
                    quads.append(jnp.where(lane >= 64, parts[1], parts[0]) * scale)
                for a in range(2):
                    halo[block, 10 * j + 5 * a : 10 * j + 5 * a + 5, :] = jnp.where(
                        lane & 8 == 0, quads[2 * a], quads[2 * a + 1]
                    )

            @pl.when(kind == 3)
            def _():
                rest = [WEIGHTS[q] for q in LISTS[j ^ 1]]
                straight = rest.index(WEIGHTS[1])
                value = jnp.where(sub == straight, jnp.float32(WEIGHTS[1]), jnp.float32(WEIGHTS[7]))
                halo[block, 10 * j : 10 * j + 5, :] = value
                halo[block, 10 * j + 5 : 10 * j + 10, :] = value


def stream(src, dst, plan, base, table, halo, blocks, done):
    sub, lane = iotas()
    odd = (sub & 1) == 1
    xl, yh = sub // 4, (sub // 2) % 2
    z = lane & 15
    starts = [(2 * k + xl) * 16 for k in range(4)]

    def plane(j, i, h):
        return jnp.where(odd, bulk(halo.at[1], 10 * j + 5 * h + i), bulk(halo.at[0], 10 * j + 5 * h + i))

    for q in range(19):
        c = VELOCITIES[q]
        moving = [a for a in range(3) if c[a]]
        values = [tile(src, q, t) for t in range(TILES)]
        planes = {}
        for a in moving:
            j = 2 * a + (0 if c[a] < 0 else 1)
            i = LISTS[j ^ 1].index(q)
            planes[a] = [plane(j, i, h) for h in range(2)]
        line = None
        if len(moving) == 2:
            e = VELOCITIES.index(tuple(-v for v in c)) - 1
            j = 2 * moving[0] + (0 if c[moving[0]] > 0 else 1)
            i = LISTS[j].index(q)
            found = []
            for block in range(blocks):
                slot = plan[block, base + e]
                good = jnp.full((8, 128), slot, jnp.int32) >= 0
                slot = jnp.maximum(slot, 0)
                found.append(
                    [jnp.where(good, bulk(table.at[slot], 10 * j + 5 * h + i), jnp.float32(WEIGHTS[q])) for h in range(2)]
                )
            line = [jnp.where(odd, found[1][h], found[0][h]) for h in range(2)]
        outside = jnp.where(yh == 1, planes[0][1], planes[0][0]) if c[0] else None

        if c[2]:
            up = c[2] > 0
            edge = z == (0 if up else 15)
            values = [
                jnp.where(edge, pick(planes[2][t // 4], starts[t % 4] + yh * 8 + (lane >> 4)), lanes(v, c[2]))
                for t, v in enumerate(values)
            ]
            if c[0]:
                spread = jnp.where(yh == 1, line[1], line[0])
                outside = jnp.where(edge, lanes(spread, -15 if up else 15), lanes(outside, c[2]))
        if c[1]:
            up = c[1] > 0
            edge = lane < 16 if up else lane >= 112
            inner = yh == (1 if up else 0)

            def moved(v, border):
                rolled = lanes(v, 16 * c[1])
                return jnp.where(edge, jnp.where(inner, subs(rolled, 2 * c[1]), border), rolled)

            for t in range(TILES):
                start, source = starts[t % 4], planes[1][t // 4]
                if c[2]:
                    if c[2] > 0:
                        border = jnp.where(z == 0, pick(line[t // 4], start + 15), pick(source, start + jnp.maximum(z - 1, 0)))
                    else:
                        border = jnp.where(z == 15, pick(line[t // 4], start), pick(source, start + jnp.minimum(z + 1, 15)))
                else:
                    border = pick(source, start + z)
                values[t] = moved(values[t], border)
            if c[0]:
                outside = moved(outside, lanes(line[1 if up else 0], 16 * c[1]))
        if c[0]:
            rolled = [subs(v, 4) for v in values]
            if c[0] > 0:
                values = [jnp.where(sub < 4, rolled[t - 1] if t else outside, rolled[t]) for t in range(TILES)]
            else:
                values = [
                    jnp.where(sub >= 4, rolled[t + 1] if t < TILES - 1 else outside, rolled[t]) for t in range(TILES)
                ]
        for t in range(TILES):
            dst[q, 8 * t : 8 * t + 8, :] = values[t]
        done(q)


def nothing(_):
    pass


def first_kernel(sizes, level_hbm, near_hbm, link_hbm, pops_hbm, mask_hbm, star, out, plan, mask, level_ref, near, links, pops, sems):
    me = (lax.axis_index("section"), lax.axis_index("member"))
    small = [
        pltpu.make_async_copy(level_hbm, level_ref, sems.at[TILES]),
        pltpu.make_async_copy(near_hbm, near, sems.at[TILES + 1]),
        pltpu.make_async_copy(link_hbm, links, sems.at[TILES + 2]),
        pltpu.make_async_copy(mask_hbm, mask, sems.at[TILES + 3]),
    ]
    parts = [
        pltpu.make_async_copy(pops_hbm.at[:, 8 * t : 8 * t + 8, :], pops.at[:, 8 * t : 8 * t + 8, :], sems.at[t])
        for t in range(TILES)
    ]
    for copy in small + parts:
        copy.start()
    for copy in small:
        copy.wait()
    level = level_ref[me[0]]
    plan_rows(level_ref, near, links, plan, me, sizes)

    @pl.when(level >= 1)
    def _():
        collide(pops, star, mask, relax_rate(level), lambda t: parts[t].wait())

    @pl.when(level < 1)
    def _():
        for t in range(TILES):
            parts[t].wait()
        star[...] = pops[...]

    export(star, out)


def gathered(plan_ref, plan, sem, parts, table):
    copy = pltpu.make_async_copy(plan_ref, plan, sem)
    copy.start()
    for i, part in enumerate(parts):
        for k in range(part.shape[0]):
            table[part.shape[0] * i + k] = part[k]
    copy.wait()


def middle_kernel(sizes, plan_ref, star, mask, own, chip, far, dst, out, plan, table, halo, sems):
    gathered(plan_ref, plan, sems.at[0], (own, chip, far), table)
    level = plan[0, 64]

    @pl.when(level >= 1)
    def _():
        arrived(plan, 0, table, halo, sizes[2])
        stream(star, dst, plan, 0, table, halo, sizes[2], nothing)

    @pl.when(level < 1)
    def _():
        dst[...] = star[...]

    @pl.when(level == 2)
    def _():
        collide(dst, dst, mask, relax_rate(level), nothing)

    export(dst, out)


def last_kernel(sizes, plan_ref, star, own, chip, far, result, plan, table, halo, moved, sems):
    gathered(plan_ref, plan, sems.at[19], (own, chip, far), table)
    level = plan[0, 64]

    @pl.when(level == 2)
    def _():
        copies = [pltpu.make_async_copy(moved.at[q], result.at[q], sems.at[q]) for q in range(19)]
        arrived(plan, 32, table, halo, sizes[2])
        stream(star, moved, plan, 32, table, halo, sizes[2], lambda q: copies[q].start())
        for copy in copies:
            copy.wait()

    @pl.when(level < 2)
    def _():
        copy = pltpu.make_async_copy(star, result, sems.at[0])
        copy.start()
        copy.wait()


def swap(x, sections, members, target):
    pairs = []
    for s in range(sections):
        for m in range(members):
            t = target(s, m)
            if 0 <= t[1] < members:
                pairs.append((s * members + m, t[0] * members + t[1]))
    return lax.ppermute(x, ("section", "member"), pairs)


def exchange(exports, sections, members, last):
    power = sections & (sections - 1) == 0
    me = lax.axis_index("section")

    def across(d):
        return lambda s, m: (s ^ d if power else (s + d) % sections, m)

    def beside(s, m):
        t = ((m + 1) ^ 1) - 1
        return (s, t) if 0 <= t < members or sections % 2 else (s ^ 1, m)

    parts = [swap(exports, sections, members, across(d)) for d in range(1, sections)]
    if last:
        blocks = exports.shape[0]
        own = jnp.zeros(((sections - 1) * blocks,) + exports.shape[1:], exports.dtype)
        for d, part in enumerate(parts, 1):
            source = me ^ d if power else (me + sections - d) % sections
            own = lax.dynamic_update_slice(own, part, (jnp.where(source == 0, me - 1, source - 1) * blocks, 0, 0))
        own = lax.dynamic_update_slice(own, exports, ((me - 1) * blocks, 0, 0))
    else:
        own = jnp.concatenate([exports] + parts, axis=0)
    chip = swap(own, sections, members, lambda s, m: (s, m ^ 1))
    far = swap(own, sections, members, beside)
    return own, chip, far


def packed(x):
    n, cells = x.shape[0], x.shape[-1]
    x = x.reshape(n, -1, cells // 128, 128)
    return x.transpose(1, 2, 0, 3).reshape(-1, n * cells // 128, 128)


VMEM = pl.BlockSpec(memory_space=pltpu.VMEM)
ANY = pl.BlockSpec(memory_space=pl.ANY)
HBM = pl.BlockSpec(memory_space=pltpu.HBM)


def body(populations, fluid_mask, section_level, neighbours, interface):
    sections, members = lax.axis_size("section"), lax.axis_size("member")
    blocks, _, cells = populations.shape
    sizes = (sections, members, blocks)
    params = pltpu.CompilerParams(vmem_limit_bytes=16 << 20)
    pops = packed(populations)
    mask = packed(fluid_mask)[0]
    links = interface.transpose(0, 2, 1)
    field = jax.ShapeDtypeStruct(pops.shape, jnp.float32)
    planes = jax.ShapeDtypeStruct((blocks, ROWS, 128), jnp.float32)
    plan = jax.ShapeDtypeStruct((16, 128), jnp.int32)
    plan_scratch = pltpu.SMEM((16, 128), jnp.int32)
    halo = pltpu.VMEM((blocks, ROWS, 128), jnp.float32)
    star, exports, plan, mask = pl.pallas_call(
        functools.partial(first_kernel, sizes),
        out_shape=(field, planes, plan, jax.ShapeDtypeStruct(mask.shape, jnp.int32)),
        in_specs=[HBM] * 5,
        out_specs=(VMEM,) * 4,
        scratch_shapes=[
            pltpu.SMEM(section_level.shape, jnp.int32),
            pltpu.VMEM(neighbours.shape, jnp.int32),
            pltpu.VMEM(links.shape, jnp.int32),
            pltpu.VMEM(pops.shape, jnp.float32),
            pltpu.SemaphoreType.DMA((TILES + 4,)),
        ],
        compiler_params=params,
        name="first",
    )(*(pltpu.with_memory_space_constraint(x, pltpu.HBM) for x in (section_level, neighbours, links, pops, mask)))
    own, chip, far = exchange(exports, sections, members, False)
    star, exports = pl.pallas_call(
        functools.partial(middle_kernel, sizes),
        out_shape=(field, planes),
        in_specs=[ANY] + [VMEM] * 5,
        out_specs=(VMEM, VMEM),
        scratch_shapes=[
            plan_scratch,
            pltpu.VMEM((3 * sections * blocks, ROWS, 128), jnp.float32),
            halo,
            pltpu.SemaphoreType.DMA((1,)),
        ],
        compiler_params=params,
        name="middle",
    )(plan, star, mask, own, chip, far)
    own, chip, far = exchange(exports, sections, members, True)
    result = pl.pallas_call(
        functools.partial(last_kernel, sizes),
        out_shape=field,
        in_specs=[ANY] + [VMEM] * 4,
        out_specs=HBM,
        scratch_shapes=[
            plan_scratch,
            pltpu.VMEM((3 * (sections - 1) * blocks, ROWS, 128), jnp.float32),
            halo,
            pltpu.VMEM(pops.shape, jnp.float32),
            pltpu.SemaphoreType.DMA((20,)),
        ],
        compiler_params=params,
        name="last",
    )(plan, star, own, chip, far)
    out = result.reshape(19, cells // 128, blocks, 128).transpose(2, 0, 1, 3)
    return out.reshape(blocks, 19, cells)


def solution(mesh):
    return jax.shard_map(
        body,
        mesh=mesh,
        in_specs=(
            P(("section", "member"), None, None),
            P(("section", "member"), None),
            P(),
            P(("section", "member"), None),
            P(("section", "member"), None, None),
        ),
        out_specs=P(("section", "member"), None, None),
        check_vma=False,
    )
```

```python
import functools

import jax
import jax.numpy as jnp
from jax import lax
from jax.experimental import pallas as pl
from jax.experimental.pallas import tpu as pltpu
from jax.sharding import PartitionSpec as P


VELOCITIES = (
    (0, 0, 0), (1, 0, 0), (-1, 0, 0), (0, 1, 0), (0, -1, 0), (0, 0, 1), (0, 0, -1),
    (1, 1, 0), (-1, -1, 0), (1, -1, 0), (-1, 1, 0), (1, 0, 1), (-1, 0, -1), (1, 0, -1),
    (-1, 0, 1), (0, 1, 1), (0, -1, -1), (0, 1, -1), (0, -1, 1),
)
WEIGHTS = (1.0 / 3.0,) + (1.0 / 18.0,) * 6 + (1.0 / 36.0,) * 12
OPPOSITE = (0, 2, 1, 4, 3, 6, 5, 8, 7, 10, 9, 12, 11, 14, 13, 16, 15, 18, 17)
LISTS = [
    [q for q in range(19) if sum(a * b for a, b in zip(VELOCITIES[q], VELOCITIES[1 + j])) == 1]
    for j in range(6)
]
ROWS = 64
TILES = 8


def iotas():
    sub = lax.broadcasted_iota(jnp.int32, (8, 128), 0)
    lane = lax.broadcasted_iota(jnp.int32, (8, 128), 1)
    return sub, lane


def pick(x, index):
    return jnp.take_along_axis(x, index, axis=1, mode="promise_in_bounds")


def lanes(x, shift):
    return pltpu.roll(x, shift % 128, 1)


def subs(x, shift):
    return pltpu.roll(x, shift % 8, 0)


def tile(ref, q, t):
    return ref[q, 8 * t : 8 * t + 8, :]


def bulk(ref, row):
    return jnp.broadcast_to(ref[row : row + 1, :], (8, 128))


def relax_rate(level):
    return jnp.where(
        level == 0, jnp.float32(1.0 / 0.55), jnp.where(level == 1, jnp.float32(1.0 / 0.6), jnp.float32(1.0 / 0.7))
    )


def collide(src, dst, mask, rate, ready):
    for t in range(TILES):
        ready(t)
        f = [tile(src, q, t) for q in range(19)]
        density = f[0]
        for q in range(1, 19):
            density = density + f[q]
        velocity = []
        for a in range(3):
            plus = [q for q in range(19) if VELOCITIES[q][a] > 0]
            total = f[plus[0]] - f[OPPOSITE[plus[0]]]
            for q in plus[1:]:
                total = total + (f[q] - f[OPPOSITE[q]])
            velocity.append(total / density)
        speed = velocity[0] * velocity[0] + velocity[1] * velocity[1] + velocity[2] * velocity[2]
        base = 1.0 - 1.5 * speed
        fluid = mask[8 * t : 8 * t + 8, :] == 1
        keep = 1.0 - rate
        scaled = [rate * jnp.float32(w) * density for w in (WEIGHTS[0], WEIGHTS[1], WEIGHTS[7])]
        out = keep * f[0] + scaled[0] * base
        dst[0, 8 * t : 8 * t + 8, :] = jnp.where(fluid, out, f[0])
        for q in range(1, 19, 2):
            o = OPPOSITE[q]
            along = None
            for a in range(3):
                c = VELOCITIES[q][a]
                if c:
                    term = velocity[a] if c > 0 else -velocity[a]
                    along = term if along is None else along + term
            weight = scaled[1] if q < 7 else scaled[2]
            even = base + 4.5 * along * along
            odd = 3.0 * along
            dst[q, 8 * t : 8 * t + 8, :] = jnp.where(fluid, keep * f[q] + weight * (even + odd), f[o])
            dst[o, 8 * t : 8 * t + 8, :] = jnp.where(fluid, keep * f[o] + weight * (even - odd), f[q])


def export(src, out):
    sub, lane = iotas()
    xl, yh = sub // 4, (sub // 2) % 2
    for j in range(6):
        axis, high = j // 2, j % 2 == 0
        for i, q in enumerate(LISTS[j]):
            if axis == 0:
                v = tile(src, q, TILES - 1 if high else 0)
                first = 4 if high else 0
                for h in range(2):
                    for b in range(2):
                        s = first + 2 * h + b
                        r = 10 * j + 5 * h + i
                        out[b, r : r + 1, :] = v[s : s + 1, :]
                continue
            for h in range(2):
                total = jnp.zeros((8, 128), jnp.float32)
                for k in range(4):
                    if axis == 1:
                        index = (lane & 15) + (112 if high else 0)
                        here = (lane >> 4 == 2 * k + xl) & (yh == (1 if high else 0))
                    else:
                        index = (lane & 7) * 16 + (15 if high else 0)
                        here = lane >> 3 == (2 * k + xl) * 2 + yh
                    total = jnp.where(here, pick(tile(src, q, 4 * h + k), index), total)
                total = total + subs(total, 4)
                total = total + subs(total, 2)
                for b in range(2):
                    r = 10 * j + 5 * h + i
                    out[b, r : r + 1, :] = total[b : b + 1, :]


def divide(x, n):
    return x >> (n.bit_length() - 1) if n & (n - 1) == 0 else lax.div(x, jnp.int32(n))


def plan_rows(level_ref, near_ref, link_ref, plan, me, sizes):
    sections, members, blocks = sizes
    level = level_ref[me[0]]
    chip = jnp.where(me[1] % 2 == 0, 1, -1)

    def placed(ids):
        safe = jnp.maximum(ids, 0)
        local = divide(safe, blocks)
        within = safe - local * blocks
        section = divide(local, members)
        offset = local - section * members - me[1]
        which = jnp.where(offset == 0, 0, jnp.where(offset == chip, 1, 2))
        apart = section ^ me[0]
        one = (which * sections + apart) * blocks + within
        later = jnp.clip(section + 1, 2, max(sections - 2, 2))
        two = (which * (sections - 1) + jnp.where(apart < 2, apart, later)) * blocks + within
        source = jnp.zeros_like(ids)
        for s in range(sections):
            source = jnp.where(section == s, level_ref[s], source)
        return (one, two), source

    plan[0:1, 64:65] = jnp.full((1, 1), level, jnp.int32)
    for block in range(blocks):
        near = near_ref[block : block + 1, :]
        near_slots, _ = placed(near)
        links = link_ref[block]
        link_slots, source = placed(links)
        coarse = (links >= 0) & (source < level)
        fine = (links >= 0) & (source >= level)
        place = lax.broadcasted_iota(jnp.int32, links.shape, 0)
        quadrant = jnp.max(jnp.where(coarse, place, -1), axis=0, keepdims=True)
        any_fine = jnp.max(jnp.where(fine, 1, 0), axis=0, keepdims=True)
        kind = jnp.where(quadrant >= 0, 1, jnp.where(any_fine > 0, 2, 3))
        kind = jnp.where(near[:, :6] >= 0, 0, kind)
        for r in range(2):
            first = 32 * r
            plan[block : block + 1, first : first + 18] = jnp.where(near >= 0, near_slots[r], -1)
            plan[2 + 4 * block : 6 + 4 * block, first : first + 6] = jnp.where(fine, link_slots[r], -1)
            chosen = jnp.max(jnp.where(coarse, link_slots[r], -1), axis=0, keepdims=True)
            plan[10 + block : 11 + block, first : first + 6] = chosen
            plan[12 + block : 13 + block, first : first + 6] = kind
            plan[14 + block : 15 + block, first : first + 6] = quadrant


def arrived(plan, base, table, halo, blocks):
    sub, lane = iotas()
    sub, lane = sub[:5], lane[:5]
    for block in range(blocks):
        for j in range(6):
            first = 10 * (j ^ 1)
            kind = plan[12 + block, base + j]

            def rows(slot, part):
                return table[slot, first + 5 * part : first + 5 * part + 5, :]

            @pl.when(kind == 0)
            def _():
                halo[block, 10 * j : 10 * j + 10, :] = table[plan[block, base + j], first : first + 10, :]

            @pl.when(kind == 1)
            def _():
                slot = plan[10 + block, base + j]
                quadrant = plan[14 + block, base + j]
                low = jnp.full((5, 128), quadrant, jnp.int32) < 2
                source = jnp.where(low, rows(slot, 0), rows(slot, 1))
                shift = 8 * (quadrant & 1)
                for h in range(2):
                    index = (4 * h + (lane >> 5)) * 16 + shift + ((lane & 15) >> 1)
                    halo[block, 10 * j + 5 * h : 10 * j + 5 * h + 5, :] = pick(source, index)

            @pl.when(kind == 2)
            def _():
                index = ((lane >> 4) & 3) * 32 + 2 * (lane & 7)
                quads = []
                for k in range(4):
                    slot = plan[2 + 4 * block + k, base + j]
                    scale = jnp.where(slot >= 0, jnp.float32(0.25), jnp.float32(0.0))
                    slot = jnp.maximum(slot, 0)
                    parts = []
                    for h in range(2):
                        v = rows(slot, h)
                        v = v + lanes(v, -1)
                        v = v + lanes(v, -16)
                        parts.append(pick(v, index))
                    quads.append(jnp.where(lane >= 64, parts[1], parts[0]) * scale)
                for a in range(2):
                    halo[block, 10 * j + 5 * a : 10 * j + 5 * a + 5, :] = jnp.where(
                        lane & 8 == 0, quads[2 * a], quads[2 * a + 1]
                    )

            @pl.when(kind == 3)
            def _():
                rest = [WEIGHTS[q] for q in LISTS[j ^ 1]]
                straight = rest.index(WEIGHTS[1])
                value = jnp.where(sub == straight, jnp.float32(WEIGHTS[1]), jnp.float32(WEIGHTS[7]))
                halo[block, 10 * j : 10 * j + 5, :] = value
                halo[block, 10 * j + 5 : 10 * j + 10, :] = value


def stream(src, dst, plan, base, table, halo, blocks, done):
    sub, lane = iotas()
    odd = (sub & 1) == 1
    xl, yh = sub // 4, (sub // 2) % 2
    z = lane & 15
    starts = [(2 * k + xl) * 16 for k in range(4)]

    def plane(j, i, h):
        return jnp.where(odd, bulk(halo.at[1], 10 * j + 5 * h + i), bulk(halo.at[0], 10 * j + 5 * h + i))

    for q in range(19):
        c = VELOCITIES[q]
        moving = [a for a in range(3) if c[a]]
        values = [tile(src, q, t) for t in range(TILES)]
        planes = {}
        for a in moving:
            j = 2 * a + (0 if c[a] < 0 else 1)
            i = LISTS[j ^ 1].index(q)
            planes[a] = [plane(j, i, h) for h in range(2)]
        line = None
        if len(moving) == 2:
            e = VELOCITIES.index(tuple(-v for v in c)) - 1
            j = 2 * moving[0] + (0 if c[moving[0]] > 0 else 1)
            i = LISTS[j].index(q)
            found = []
            for block in range(blocks):
                slot = plan[block, base + e]
                good = jnp.full((8, 128), slot, jnp.int32) >= 0
                slot = jnp.maximum(slot, 0)
                found.append(
                    [jnp.where(good, bulk(table.at[slot], 10 * j + 5 * h + i), jnp.float32(WEIGHTS[q])) for h in range(2)]
                )
            line = [jnp.where(odd, found[1][h], found[0][h]) for h in range(2)]
        outside = jnp.where(yh == 1, planes[0][1], planes[0][0]) if c[0] else None

        if c[2]:
            up = c[2] > 0
            edge = z == (0 if up else 15)
            values = [
                jnp.where(edge, pick(planes[2][t // 4], starts[t % 4] + yh * 8 + (lane >> 4)), lanes(v, c[2]))
                for t, v in enumerate(values)
            ]
            if c[0]:
                spread = jnp.where(yh == 1, line[1], line[0])
                outside = jnp.where(edge, lanes(spread, -15 if up else 15), lanes(outside, c[2]))
        if c[1]:
            up = c[1] > 0
            edge = lane < 16 if up else lane >= 112
            inner = yh == (1 if up else 0)

            def moved(v, border):
                rolled = lanes(v, 16 * c[1])
                return jnp.where(edge, jnp.where(inner, subs(rolled, 2 * c[1]), border), rolled)

            for t in range(TILES):
                start, source = starts[t % 4], planes[1][t // 4]
                if c[2]:
                    if c[2] > 0:
                        border = jnp.where(z == 0, pick(line[t // 4], start + 15), pick(source, start + jnp.maximum(z - 1, 0)))
                    else:
                        border = jnp.where(z == 15, pick(line[t // 4], start), pick(source, start + jnp.minimum(z + 1, 15)))
                else:
                    border = pick(source, start + z)
                values[t] = moved(values[t], border)
            if c[0]:
                outside = moved(outside, lanes(line[1 if up else 0], 16 * c[1]))
        if c[0]:
            rolled = [subs(v, 4) for v in values]
            if c[0] > 0:
                values = [jnp.where(sub < 4, rolled[t - 1] if t else outside, rolled[t]) for t in range(TILES)]
            else:
                values = [
                    jnp.where(sub >= 4, rolled[t + 1] if t < TILES - 1 else outside, rolled[t]) for t in range(TILES)
                ]
        for t in range(TILES):
            dst[q, 8 * t : 8 * t + 8, :] = values[t]
        done(q)


def nothing(_):
    pass


def first_kernel(sizes, level_hbm, near_hbm, link_hbm, pops_hbm, mask_hbm, star, out, plan, mask, level_ref, near, links, pops, sems):
    me = (lax.axis_index("section"), lax.axis_index("member"))
    small = [
        pltpu.make_async_copy(level_hbm, level_ref, sems.at[TILES]),
        pltpu.make_async_copy(near_hbm, near, sems.at[TILES + 1]),
        pltpu.make_async_copy(link_hbm, links, sems.at[TILES + 2]),
        pltpu.make_async_copy(mask_hbm, mask, sems.at[TILES + 3]),
    ]
    parts = [
        pltpu.make_async_copy(pops_hbm.at[:, 8 * t : 8 * t + 8, :], pops.at[:, 8 * t : 8 * t + 8, :], sems.at[t])
        for t in range(TILES)
    ]
    for copy in small + parts:
        copy.start()
    for copy in small:
        copy.wait()
    level = level_ref[me[0]]
    plan_rows(level_ref, near, links, plan, me, sizes)

    @pl.when(level >= 1)
    def _():
        collide(pops, star, mask, relax_rate(level), lambda t: parts[t].wait())

    @pl.when(level < 1)
    def _():
        for t in range(TILES):
            parts[t].wait()
        star[...] = pops[...]

    export(star, out)


def gathered(plan_ref, plan, sem, parts, table):
    copy = pltpu.make_async_copy(plan_ref, plan, sem)
    copy.start()
    row = 0
    for part in parts:
        for k in range(part.shape[0]):
            table[row] = part[k]
            row += 1
    copy.wait()


def middle_kernel(sizes, plan_ref, star, mask, own, chip, near, far, dst, out, plan, table, halo, sems):
    gathered(plan_ref, plan, sems.at[0], (own, chip, near, far), table)
    level = plan[0, 64]

    @pl.when(level >= 1)
    def _():
        arrived(plan, 0, table, halo, sizes[2])
        stream(star, dst, plan, 0, table, halo, sizes[2], nothing)

    @pl.when(level < 1)
    def _():
        dst[...] = star[...]

    @pl.when(level == 2)
    def _():
        collide(dst, dst, mask, relax_rate(level), nothing)

    export(dst, out)


def last_kernel(sizes, plan_ref, star, own, chip, near, far, result, plan, table, halo, moved, sems):
    gathered(plan_ref, plan, sems.at[19], (own, chip, near, far), table)
    level = plan[0, 64]

    @pl.when(level == 2)
    def _():
        copies = [pltpu.make_async_copy(moved.at[q], result.at[q], sems.at[q]) for q in range(19)]
        arrived(plan, 32, table, halo, sizes[2])
        stream(star, moved, plan, 32, table, halo, sizes[2], lambda q: copies[q].start())
        for copy in copies:
            copy.wait()

    @pl.when(level < 2)
    def _():
        copy = pltpu.make_async_copy(star, result, sems.at[0])
        copy.start()
        copy.wait()


def swap(x, sections, members, target):
    pairs = []
    for s in range(sections):
        for m in range(members):
            t = target(s, m)
            if 0 <= t[1] < members:
                pairs.append((s * members + m, t[0] * members + t[1]))
    return lax.ppermute(x, ("section", "member"), pairs)


def exchange(exports, sections, members, last):
    me = lax.axis_index("section")

    def named(x, target):
        return swap(x, sections, members, target)

    def beside(s, m):
        t = ((m + 1) ^ 1) - 1
        return (s, t) if 0 <= t < members else (s ^ 1, m)

    parts = [exports] + [named(exports, lambda s, m, d=d: (s ^ d, m)) for d in range(1, sections)]
    first = jnp.concatenate(parts[:2], axis=0)
    if last:
        second = []
        for t in range(1, sections - 2):
            value = parts[sections - 1]
            for d in range(2, sections - 1):
                value = jnp.where(me ^ d == t, parts[d], value)
            second.append(value)
        second = jnp.concatenate(second, axis=0)
    else:
        second = jnp.concatenate(parts[2:], axis=0)
    own = jnp.concatenate([first, second], axis=0)
    near = named(first, beside)
    far = named(second, beside)
    chip = named(own, lambda s, m: (s, m ^ 1))
    return own, chip, near, far


def packed(x):
    n, cells = x.shape[0], x.shape[-1]
    x = x.reshape(n, -1, cells // 128, 128)
    return x.transpose(1, 2, 0, 3).reshape(-1, n * cells // 128, 128)


VMEM = pl.BlockSpec(memory_space=pltpu.VMEM)
ANY = pl.BlockSpec(memory_space=pl.ANY)
HBM = pl.BlockSpec(memory_space=pltpu.HBM)


def body(populations, fluid_mask, section_level, neighbours, interface):
    sections, members = lax.axis_size("section"), lax.axis_size("member")
    blocks, _, cells = populations.shape
    sizes = (sections, members, blocks)
    params = pltpu.CompilerParams(vmem_limit_bytes=16 << 20)
    pops = packed(populations)
    mask = packed(fluid_mask)[0]
    links = interface.transpose(0, 2, 1)
    field = jax.ShapeDtypeStruct(pops.shape, jnp.float32)
    planes = jax.ShapeDtypeStruct((blocks, ROWS, 128), jnp.float32)
    plan = jax.ShapeDtypeStruct((16, 128), jnp.int32)
    plan_scratch = pltpu.SMEM((16, 128), jnp.int32)
    halo = pltpu.VMEM((blocks, ROWS, 128), jnp.float32)
    star, exports, plan, mask = pl.pallas_call(
        functools.partial(first_kernel, sizes),
        out_shape=(field, planes, plan, jax.ShapeDtypeStruct(mask.shape, jnp.int32)),
        in_specs=[HBM] * 5,
        out_specs=(VMEM,) * 4,
        scratch_shapes=[
            pltpu.SMEM(section_level.shape, jnp.int32),
            pltpu.VMEM(neighbours.shape, jnp.int32),
            pltpu.VMEM(links.shape, jnp.int32),
            pltpu.VMEM(pops.shape, jnp.float32),
            pltpu.SemaphoreType.DMA((TILES + 4,)),
        ],
        compiler_params=params,
        name="first",
    )(*(pltpu.with_memory_space_constraint(x, pltpu.HBM) for x in (section_level, neighbours, links, pops, mask)))
    parts = exchange(exports, sections, members, False)
    star, exports = pl.pallas_call(
        functools.partial(middle_kernel, sizes),
        out_shape=(field, planes),
        in_specs=[ANY] + [VMEM] * 6,
        out_specs=(VMEM, VMEM),
        scratch_shapes=[
            plan_scratch,
            pltpu.VMEM((3 * sections * blocks, ROWS, 128), jnp.float32),
            halo,
            pltpu.SemaphoreType.DMA((1,)),
        ],
        compiler_params=params,
        name="middle",
    )(plan, star, mask, *parts)
    parts = exchange(exports, sections, members, True)
    result = pl.pallas_call(
        functools.partial(last_kernel, sizes),
        out_shape=field,
        in_specs=[ANY] + [VMEM] * 5,
        out_specs=HBM,
        scratch_shapes=[
            plan_scratch,
            pltpu.VMEM((3 * (sections - 1) * blocks, ROWS, 128), jnp.float32),
            halo,
            pltpu.VMEM(pops.shape, jnp.float32),
            pltpu.SemaphoreType.DMA((20,)),
        ],
        compiler_params=params,
        name="last",
    )(plan, star, *parts)
    out = result.reshape(19, cells // 128, blocks, 128).transpose(2, 0, 1, 3)
    return out.reshape(blocks, 19, cells)


def solution(mesh):
    return jax.shard_map(
        body,
        mesh=mesh,
        in_specs=(
            P(("section", "member"), None, None),
            P(("section", "member"), None),
            P(),
            P(("section", "member"), None),
            P(("section", "member"), None, None),
        ),
        out_specs=P(("section", "member"), None, None),
        check_vma=False,
    )
```

```python
import functools

import jax
import jax.numpy as jnp
from jax import lax
from jax.experimental import pallas as pl
from jax.experimental.pallas import tpu as pltpu
from jax.sharding import PartitionSpec as P


VELOCITIES = (
    (0, 0, 0), (1, 0, 0), (-1, 0, 0), (0, 1, 0), (0, -1, 0), (0, 0, 1), (0, 0, -1),
    (1, 1, 0), (-1, -1, 0), (1, -1, 0), (-1, 1, 0), (1, 0, 1), (-1, 0, -1), (1, 0, -1),
    (-1, 0, 1), (0, 1, 1), (0, -1, -1), (0, 1, -1), (0, -1, 1),
)
WEIGHTS = (1.0 / 3.0,) + (1.0 / 18.0,) * 6 + (1.0 / 36.0,) * 12
OPPOSITE = (0, 2, 1, 4, 3, 6, 5, 8, 7, 10, 9, 12, 11, 14, 13, 16, 15, 18, 17)
LISTS = [
    [q for q in range(19) if sum(a * b for a, b in zip(VELOCITIES[q], VELOCITIES[1 + j])) == 1]
    for j in range(6)
]
ROWS = 64
TILES = 8


def iotas():
    sub = lax.broadcasted_iota(jnp.int32, (8, 128), 0)
    lane = lax.broadcasted_iota(jnp.int32, (8, 128), 1)
    return sub, lane


def pick(x, index):
    return jnp.take_along_axis(x, index, axis=1, mode="promise_in_bounds")


def lanes(x, shift):
    return pltpu.roll(x, shift % 128, 1)


def subs(x, shift):
    return pltpu.roll(x, shift % 8, 0)


def tile(ref, q, t, base=0):
    return ref[q, base + 8 * t : base + 8 * t + 8, :]


def bulk(ref, row):
    return jnp.broadcast_to(ref[row : row + 1, :], (8, 128))


def relax_rate(level):
    return jnp.where(
        level == 0, jnp.float32(1.0 / 0.55), jnp.where(level == 1, jnp.float32(1.0 / 0.6), jnp.float32(1.0 / 0.7))
    )


def collide(src, base, dst, mask, rate, ready):
    for t in range(TILES):
        ready(t)
        f = [tile(src, q, t, base) for q in range(19)]
        density = f[0]
        for q in range(1, 19):
            density = density + f[q]
        velocity = []
        for a in range(3):
            plus = [q for q in range(19) if VELOCITIES[q][a] > 0]
            total = f[plus[0]] - f[OPPOSITE[plus[0]]]
            for q in plus[1:]:
                total = total + (f[q] - f[OPPOSITE[q]])
            velocity.append(total / density)
        speed = velocity[0] * velocity[0] + velocity[1] * velocity[1] + velocity[2] * velocity[2]
        still = 1.0 - 1.5 * speed
        fluid = mask[8 * t : 8 * t + 8, :] == 1
        keep = 1.0 - rate
        scaled = [rate * jnp.float32(w) * density for w in (WEIGHTS[0], WEIGHTS[1], WEIGHTS[7])]
        out = keep * f[0] + scaled[0] * still
        dst[0, 8 * t : 8 * t + 8, :] = jnp.where(fluid, out, f[0])
        for q in range(1, 19, 2):
            o = OPPOSITE[q]
            along = None
            for a in range(3):
                c = VELOCITIES[q][a]
                if c:
                    term = velocity[a] if c > 0 else -velocity[a]
                    along = term if along is None else along + term
            weight = scaled[1] if q < 7 else scaled[2]
            even = still + 4.5 * along * along
            odd = 3.0 * along
            dst[q, 8 * t : 8 * t + 8, :] = jnp.where(fluid, keep * f[q] + weight * (even + odd), f[o])
            dst[o, 8 * t : 8 * t + 8, :] = jnp.where(fluid, keep * f[o] + weight * (even - odd), f[q])


def export(src, out):
    sub, lane = iotas()
    xl, yh = sub // 4, (sub // 2) % 2
    z = lane & 15
    own_x = ((lane >> 4) & 1) == xl
    own_y = ((lane >> 3) & 1) == yh
    for j in range(6):
        axis, high = j // 2, j % 2 == 0
        index = (lane & 7) * 16 + (15 - (lane >> 5) if high else lane >> 5)
        for i, q in enumerate(LISTS[j]):
            for h in range(2):
                r = 10 * j + 5 * h + i
                if axis == 0:
                    v = tile(src, q, TILES - 1 if high else 0)
                    first = (4 if high else 0) + 2 * h
                elif axis == 1:
                    v = None
                    for k in range(4):
                        part = lanes(tile(src, q, 4 * h + k), 32 * k + (16 if high else 0))
                        v = part if v is None else jnp.where(lane >> 5 == k, part, v)
                    v = jnp.where(xl == 1, lanes(v, 16), v)
                    v = jnp.where(own_x, v, subs(v, 4))
                    first = 2 if high else 0
                else:
                    v = tile(src, q, 4 * h)
                    for k in range(1, 4):
                        part = lanes(tile(src, q, 4 * h + k), -k if high else k)
                        v = jnp.where(z == (15 - k if high else k), part, v)
                    v = pick(v, index)
                    v = jnp.where(own_x, v, subs(v, 4))
                    v = jnp.where(own_y, v, subs(v, 2))
                    first = 0
                for b in range(2):
                    out[b, r : r + 1, :] = v[first + b : first + b + 1, :]


def divide(x, n):
    return x >> (n.bit_length() - 1) if n & (n - 1) == 0 else lax.div(x, jnp.int32(n))


def plan_rows(level_ref, near_ref, link_ref, plan, me, sizes):
    sections, members, blocks = sizes
    level = level_ref[me[0]]
    chip = jnp.where(me[1] % 2 == 0, 1, -1)

    def placed(ids):
        safe = jnp.maximum(ids, 0)
        local = divide(safe, blocks)
        within = safe - local * blocks
        section = divide(local, members)
        offset = local - section * members - me[1]
        which = jnp.where(offset == 0, 0, jnp.where(offset == chip, 1, 2))
        apart = section ^ me[0]
        one = (which * sections + apart) * blocks + within
        later = jnp.clip(section + 1, 2, max(sections - 2, 2))
        two = (which * (sections - 1) + jnp.where(apart < 2, apart, later)) * blocks + within
        source = jnp.zeros_like(ids)
        for s in range(sections):
            source = jnp.where(section == s, level_ref[s], source)
        return (one, two), source

    plan[0:1, 64:65] = jnp.full((1, 1), level, jnp.int32)
    split = jnp.zeros((1, 1), jnp.int32)
    for block in range(blocks):
        near = near_ref[block : block + 1, :]
        near_slots, _ = placed(near)
        links = link_ref[block]
        link_slots, source = placed(links)
        coarse = (links >= 0) & (source < level)
        fine = (links >= 0) & (source >= level)
        place = lax.broadcasted_iota(jnp.int32, links.shape, 0)
        quadrant = jnp.max(jnp.where(coarse, place, -1), axis=0, keepdims=True)
        any_fine = jnp.max(jnp.where(fine, 1, 0), axis=0, keepdims=True)
        kind = jnp.where(quadrant >= 0, 1, jnp.where(any_fine > 0, 2, 3))
        kind = jnp.where(near[:, :6] >= 0, 0, kind)
        split = jnp.maximum(split, jnp.max(jnp.where(kind == 2, 1, 0), axis=1, keepdims=True))
        for r in range(2):
            first = 32 * r
            plan[block : block + 1, first : first + 18] = jnp.where(near >= 0, near_slots[r], -1)
            plan[2 + 4 * block : 6 + 4 * block, first : first + 6] = jnp.where(fine, link_slots[r], -1)
            chosen = jnp.max(jnp.where(coarse, link_slots[r], -1), axis=0, keepdims=True)
            plan[10 + block : 11 + block, first : first + 6] = chosen
            plan[12 + block : 13 + block, first : first + 6] = kind
            plan[14 + block : 15 + block, first : first + 6] = quadrant
    plan[0:1, 65:66] = split


def arrived(plan, base, table, halo, blocks):
    sub, lane = iotas()
    sub, lane = sub[:5], lane[:5]

    def rows(slot, j, part):
        first = 10 * (j ^ 1) + 5 * part
        return table[slot, first : first + 5, :]

    def whole(scalar):
        return jnp.full((5, 128), scalar, jnp.int32)

    spread = (lane >> 5) * 16 + ((lane & 15) >> 1)
    for block in range(blocks):
        for j in range(6):
            kind = whole(plan[12 + block, base + j])
            near = jnp.maximum(plan[block, base + j], 0)
            slot = jnp.maximum(plan[10 + block, base + j], 0)
            quadrant = whole(plan[14 + block, base + j])
            source = jnp.where(quadrant < 2, rows(slot, j, 0), rows(slot, j, 1))
            source = jnp.where((quadrant & 1) == 1, lanes(source, -8), source)
            rest = [WEIGHTS[q] for q in LISTS[j ^ 1]]
            straight = rest.index(WEIGHTS[1])
            rest = jnp.where(sub == straight, jnp.float32(WEIGHTS[1]), jnp.float32(WEIGHTS[7]))
            for h in range(2):
                coarse = pick(lanes(source, 64) if h else source, spread)
                value = jnp.where(kind == 0, rows(near, j, h), jnp.where(kind == 1, coarse, rest))
                halo[block, 10 * j + 5 * h : 10 * j + 5 * h + 5, :] = value


def arrived_fine(plan, base, table, halo, blocks):
    _, lane = iotas()
    lane = lane[:5]
    odd_v, odd_u = (lane & 1) == 1, ((lane >> 4) & 1) == 1
    gather = (2 * ((lane >> 4) & 3) + (lane >> 6)) * 16 + 2 * (lane & 7) + ((lane >> 3) & 1)
    for block in range(blocks):
        for j in range(6):
            kind = jnp.full((5, 128), plan[12 + block, base + j], jnp.int32)
            first = 10 * (j ^ 1)
            for a in range(2):
                pairs = []
                for h in range(2):
                    sums = []
                    for b in range(2):
                        slot = plan[2 + 4 * block + 2 * a + b, base + j]
                        scale = jnp.where(slot >= 0, jnp.float32(0.25), jnp.float32(0.0))
                        v = table[jnp.maximum(slot, 0), first + 5 * h : first + 5 * h + 5, :] * scale
                        sums.append(v + lanes(v, 1 if b else -1))
                    v = jnp.where(odd_v, sums[1], sums[0])
                    pairs.append(v + lanes(v, 16 if h else -16))
                value = pick(jnp.where(odd_u, pairs[1], pairs[0]), gather)
                r = 10 * j + 5 * a
                halo[block, r : r + 5, :] = jnp.where(kind == 2, value, halo[block, r : r + 5, :])


def stream(src, dst, plan, base, table, halo, blocks, done):
    sub, lane = iotas()
    odd = (sub & 1) == 1
    xl, yh = sub // 4, (sub // 2) % 2
    z = lane & 15

    def both(one, two):
        return jnp.where(odd, two, one)

    def plane(j, i, h):
        r = 10 * j + 5 * h + i
        return both(bulk(halo.at[0], r), bulk(halo.at[1], r))

    def edge_row(q, e, h):
        a = [n for n in range(3) if VELOCITIES[q][n]][0]
        j = 2 * a + (0 if VELOCITIES[q][a] > 0 else 1)
        r = 10 * j + 5 * h + LISTS[j].index(q)
        found = []
        for block in range(blocks):
            slot = plan[block, base + e]
            good = jnp.full((8, 128), slot, jnp.int32) >= 0
            found.append(jnp.where(good, bulk(table.at[jnp.maximum(slot, 0)], r), jnp.float32(WEIGHTS[q])))
        return both(*found)

    for q in range(19):
        c = VELOCITIES[q]
        moving = [a for a in range(3) if c[a]]
        e = VELOCITIES.index(tuple(-v for v in c)) - 1
        planes = {}
        for a in moving:
            j = 2 * a + (0 if c[a] < 0 else 1)
            i = LISTS[j ^ 1].index(q)
            planes[a] = [plane(j, i, h) for h in range(2)]
        if c[1]:
            up = c[1] > 0
            y_edge = lane >= 112 if up else lane < 16
            inner = yh == (1 if up else 0)
            beside = [jnp.where(xl == 0, v, lanes(v, -16)) for v in planes[1]]

            def joined(v, border):
                return jnp.where(y_edge, jnp.where(inner, subs(v, 2 * c[1]), border), v)

        if c[2]:
            z_edge = z == (0 if c[2] > 0 else 15)
            tile_of = z & 3 if c[2] > 0 else (15 - z) & 3
            index = (2 * tile_of + xl) * 16 + ((yh * 8 + (lane >> 4) - c[1]) & 15)
            columns = []
            for h in range(2):
                v = planes[2][h]
                if c[1]:
                    line = edge_row(q, e, h)
                    place, natural = (15 if c[1] > 0 else 0), (15 if c[2] > 0 else 0)
                    if place != natural:
                        line = lanes(line, place - natural)
                    v = jnp.where(z == place, line, v)
                columns.append(pick(v, index))
        shift = 16 * c[1] + c[2]
        first = 8 + 4 * c[0]
        for t in range(TILES):
            h, k = t // 4, t % 4
            v = tile(src, q, t)
            if c[1]:
                turn = (112 if c[1] > 0 else 0) - 32 * k
                v = joined(v, lanes(beside[h], turn) if turn % 128 else beside[h])
            if shift:
                v = lanes(v, shift)
            if c[2]:
                v = jnp.where(z_edge, lanes(columns[h], -k * c[2]) if k else columns[h], v)
            dst[q, first + 8 * t : first + 8 * t + 8, :] = v
        if c[0]:
            v = jnp.where(yh == 1, planes[0][1], planes[0][0])
            if c[1]:
                v = lanes(joined(v, edge_row(q, e, 1 if c[1] > 0 else 0)), shift)
            if c[2]:
                line = jnp.where(yh == 1, edge_row(q, e, 1), edge_row(q, e, 0))
                v = jnp.where(z_edge, lanes(line, -15 * c[2]), lanes(v, shift))
            r = 8 if c[0] > 0 else 68
            dst[q, r : r + 4, :] = v[:4]
        done(q)


def nothing(_):
    pass


def first_kernel(sizes, level_hbm, near_hbm, link_hbm, pops_hbm, mask_hbm, star, out, plan, mask, level_ref, near, links, pops, sems):
    me = (lax.axis_index("section"), lax.axis_index("member"))
    small = [
        pltpu.make_async_copy(level_hbm, level_ref, sems.at[TILES]),
        pltpu.make_async_copy(near_hbm, near, sems.at[TILES + 1]),
        pltpu.make_async_copy(link_hbm, links, sems.at[TILES + 2]),
        pltpu.make_async_copy(mask_hbm, mask, sems.at[TILES + 3]),
    ]
    parts = [
        pltpu.make_async_copy(pops_hbm.at[:, 8 * t : 8 * t + 8, :], pops.at[:, 8 * t : 8 * t + 8, :], sems.at[t])
        for t in range(TILES)
    ]
    for copy in small + parts:
        copy.start()
    for copy in small:
        copy.wait()
    level = level_ref[me[0]]
    plan_rows(level_ref, near, links, plan, me, sizes)

    @pl.when(level >= 1)
    def _():
        collide(pops, 0, star, mask, relax_rate(level), lambda t: parts[t].wait())

    @pl.when(level < 1)
    def _():
        for t in range(TILES):
            parts[t].wait()
        star[...] = pops[...]

    export(star, out)


def gathered(plan_ref, plan, sem, parts, table):
    copy = pltpu.make_async_copy(plan_ref, plan, sem)
    copy.start()
    row = 0
    for part in parts:
        for k in range(part.shape[0]):
            table[row] = part[k]
            row += 1
    copy.wait()


def middle_kernel(sizes, plan_ref, star, mask, own, chip, near, far, dst, out, plan, table, halo, moved, sems):
    gathered(plan_ref, plan, sems.at[0], (own, chip, near, far), table)
    level = plan[0, 64]

    @pl.when(level >= 1)
    def _():
        arrived(plan, 0, table, halo, sizes[2])

        @pl.when(plan[0, 65] > 0)
        def _():
            arrived_fine(plan, 0, table, halo, sizes[2])

        stream(star, moved, plan, 0, table, halo, sizes[2], nothing)

    @pl.when(level < 1)
    def _():
        dst[...] = star[...]

    @pl.when(level == 1)
    def _():
        dst[...] = moved[:, 8 : 8 + ROWS, :]

    @pl.when(level == 2)
    def _():
        collide(moved, 8, dst, mask, relax_rate(level), nothing)

    export(dst, out)


def last_kernel(sizes, plan_ref, star, own, chip, near, far, result, plan, table, halo, moved, sems):
    gathered(plan_ref, plan, sems.at[19], (own, chip, near, far), table)
    level = plan[0, 64]

    @pl.when(level == 2)
    def _():
        copies = [
            pltpu.make_async_copy(moved.at[q, 8 : 8 + ROWS], result.at[q], sems.at[q]) for q in range(19)
        ]
        arrived(plan, 32, table, halo, sizes[2])
        stream(star, moved, plan, 32, table, halo, sizes[2], lambda q: copies[q].start())
        for copy in copies:
            copy.wait()

    @pl.when(level < 2)
    def _():
        copy = pltpu.make_async_copy(star, result, sems.at[0])
        copy.start()
        copy.wait()


def swap(x, sections, members, target):
    pairs = []
    for s in range(sections):
        for m in range(members):
            t = target(s, m)
            if 0 <= t[1] < members:
                pairs.append((s * members + m, t[0] * members + t[1]))
    return lax.ppermute(x, ("section", "member"), pairs)


def exchange(exports, sections, members, last):
    me = lax.axis_index("section")

    def named(x, target):
        return swap(x, sections, members, target)

    def beside(s, m):
        t = ((m + 1) ^ 1) - 1
        return (s, t) if 0 <= t < members else (s ^ 1, m)

    parts = [exports] + [named(exports, lambda s, m, d=d: (s ^ d, m)) for d in range(1, sections)]
    first = jnp.concatenate(parts[:2], axis=0)
    if last:
        second = []
        for t in range(1, sections - 2):
            value = parts[sections - 1]
            for d in range(2, sections - 1):
                value = jnp.where(me ^ d == t, parts[d], value)
            second.append(value)
        second = jnp.concatenate(second, axis=0)
    else:
        second = jnp.concatenate(parts[2:], axis=0)
    own = jnp.concatenate([first, second], axis=0)
    near = named(first, beside)
    far = named(second, beside)
    chip = named(own, lambda s, m: (s, m ^ 1))
    return own, chip, near, far


def packed(x):
    n, cells = x.shape[0], x.shape[-1]
    x = x.reshape(n, -1, cells // 128, 128)
    return x.transpose(1, 2, 0, 3).reshape(-1, n * cells // 128, 128)


VMEM = pl.BlockSpec(memory_space=pltpu.VMEM)
ANY = pl.BlockSpec(memory_space=pl.ANY)
HBM = pl.BlockSpec(memory_space=pltpu.HBM)


def body(populations, fluid_mask, section_level, neighbours, interface):
    sections, members = lax.axis_size("section"), lax.axis_size("member")
    blocks, _, cells = populations.shape
    sizes = (sections, members, blocks)
    params = pltpu.CompilerParams(vmem_limit_bytes=16 << 20)
    pops = packed(populations)
    mask = packed(fluid_mask)[0]
    links = interface.transpose(0, 2, 1)
    field = jax.ShapeDtypeStruct(pops.shape, jnp.float32)
    planes = jax.ShapeDtypeStruct((blocks, ROWS, 128), jnp.float32)
    plan = jax.ShapeDtypeStruct((16, 128), jnp.int32)
    plan_scratch = pltpu.SMEM((16, 128), jnp.int32)
    halo = pltpu.VMEM((blocks, ROWS, 128), jnp.float32)
    star, exports, plan, mask = pl.pallas_call(
        functools.partial(first_kernel, sizes),
        out_shape=(field, planes, plan, jax.ShapeDtypeStruct(mask.shape, jnp.int32)),
        in_specs=[HBM] * 5,
        out_specs=(VMEM,) * 4,
        scratch_shapes=[
            pltpu.SMEM(section_level.shape, jnp.int32),
            pltpu.VMEM(neighbours.shape, jnp.int32),
            pltpu.VMEM(links.shape, jnp.int32),
            pltpu.VMEM(pops.shape, jnp.float32),
            pltpu.SemaphoreType.DMA((TILES + 4,)),
        ],
        compiler_params=params,
        name="first",
    )(*(pltpu.with_memory_space_constraint(x, pltpu.HBM) for x in (section_level, neighbours, links, pops, mask)))
    parts = exchange(exports, sections, members, False)
    star, exports = pl.pallas_call(
        functools.partial(middle_kernel, sizes),
        out_shape=(field, planes),
        in_specs=[ANY] + [VMEM] * 6,
        out_specs=(VMEM, VMEM),
        scratch_shapes=[
            plan_scratch,
            pltpu.VMEM((3 * sections * blocks, ROWS, 128), jnp.float32),
            halo,
            pltpu.VMEM((19, ROWS + 16, 128), jnp.float32),
            pltpu.SemaphoreType.DMA((1,)),
        ],
        compiler_params=params,
        name="middle",
    )(plan, star, mask, *parts)
    parts = exchange(exports, sections, members, True)
    result = pl.pallas_call(
        functools.partial(last_kernel, sizes),
        out_shape=field,
        in_specs=[ANY] + [VMEM] * 5,
        out_specs=HBM,
        scratch_shapes=[
            plan_scratch,
            pltpu.VMEM((3 * (sections - 1) * blocks, ROWS, 128), jnp.float32),
            halo,
            pltpu.VMEM((19, ROWS + 16, 128), jnp.float32),
            pltpu.SemaphoreType.DMA((20,)),
        ],
        compiler_params=params,
        name="last",
    )(plan, star, *parts)
    out = result.reshape(19, cells // 128, blocks, 128).transpose(2, 0, 1, 3)
    return out.reshape(blocks, 19, cells)


def solution(mesh):
    return jax.shard_map(
        body,
        mesh=mesh,
        in_specs=(
            P(("section", "member"), None, None),
            P(("section", "member"), None),
            P(),
            P(("section", "member"), None),
            P(("section", "member"), None, None),
        ),
        out_specs=P(("section", "member"), None, None),
        check_vma=False,
    )
```

```python
import functools

import jax
import jax.numpy as jnp
from jax import lax
from jax.experimental import pallas as pl
from jax.experimental.pallas import tpu as pltpu
from jax.sharding import PartitionSpec as P


VELOCITIES = (
    (0, 0, 0), (1, 0, 0), (-1, 0, 0), (0, 1, 0), (0, -1, 0), (0, 0, 1), (0, 0, -1),
    (1, 1, 0), (-1, -1, 0), (1, -1, 0), (-1, 1, 0), (1, 0, 1), (-1, 0, -1), (1, 0, -1),
    (-1, 0, 1), (0, 1, 1), (0, -1, -1), (0, 1, -1), (0, -1, 1),
)
WEIGHTS = (1.0 / 3.0,) + (1.0 / 18.0,) * 6 + (1.0 / 36.0,) * 12
OPPOSITE = (0, 2, 1, 4, 3, 6, 5, 8, 7, 10, 9, 12, 11, 14, 13, 16, 15, 18, 17)
LISTS = [
    [q for q in range(19) if sum(a * b for a, b in zip(VELOCITIES[q], VELOCITIES[1 + j])) == 1]
    for j in range(6)
]
ROWS = 64
TILES = 8


def iotas():
    sub = lax.broadcasted_iota(jnp.int32, (8, 128), 0)
    lane = lax.broadcasted_iota(jnp.int32, (8, 128), 1)
    return sub, lane


def pick(x, index):
    return jnp.take_along_axis(x, index, axis=1, mode="promise_in_bounds")


def lanes(x, shift):
    return pltpu.roll(x, shift % 128, 1)


def subs(x, shift):
    return pltpu.roll(x, shift % 8, 0)


def tile(ref, q, t, base=0):
    return ref[q, base + 8 * t : base + 8 * t + 8, :]


def bulk(ref, row):
    return jnp.broadcast_to(ref[row : row + 1, :], (8, 128))


def relax_rate(level):
    return jnp.where(
        level == 0, jnp.float32(1.0 / 0.55), jnp.where(level == 1, jnp.float32(1.0 / 0.6), jnp.float32(1.0 / 0.7))
    )


def collide(src, base, dst, mask, rate, ready):
    for t in range(TILES):
        ready(t)
        f = [tile(src, q, t, base) for q in range(19)]
        density = f[0]
        for q in range(1, 19):
            density = density + f[q]
        velocity = []
        for a in range(3):
            plus = [q for q in range(19) if VELOCITIES[q][a] > 0]
            total = f[plus[0]] - f[OPPOSITE[plus[0]]]
            for q in plus[1:]:
                total = total + (f[q] - f[OPPOSITE[q]])
            velocity.append(total / density)
        speed = velocity[0] * velocity[0] + velocity[1] * velocity[1] + velocity[2] * velocity[2]
        still = 1.0 - 1.5 * speed
        fluid = mask[8 * t : 8 * t + 8, :] == 1
        keep = 1.0 - rate
        scaled = [rate * jnp.float32(w) * density for w in (WEIGHTS[0], WEIGHTS[1], WEIGHTS[7])]
        out = keep * f[0] + scaled[0] * still
        dst[0, 8 * t : 8 * t + 8, :] = jnp.where(fluid, out, f[0])
        for q in range(1, 19, 2):
            o = OPPOSITE[q]
            along = None
            for a in range(3):
                c = VELOCITIES[q][a]
                if c:
                    term = velocity[a] if c > 0 else -velocity[a]
                    along = term if along is None else along + term
            weight = scaled[1] if q < 7 else scaled[2]
            even = still + 4.5 * along * along
            odd = 3.0 * along
            dst[q, 8 * t : 8 * t + 8, :] = jnp.where(fluid, keep * f[q] + weight * (even + odd), f[o])
            dst[o, 8 * t : 8 * t + 8, :] = jnp.where(fluid, keep * f[o] + weight * (even - odd), f[q])


def export(src, out):
    sub, lane = iotas()
    xl, yh = sub // 4, (sub // 2) % 2
    own_x = ((lane >> 4) & 1) == xl
    own_y = ((lane >> 3) & 1) == yh
    for j in range(6):
        axis, high = j // 2, j % 2 == 0
        index = (lane & 7) * 16 + (15 if high else 0)
        for i, q in enumerate(LISTS[j]):
            for h in range(2):
                r = 10 * j + 5 * h + i
                if axis == 0:
                    v = tile(src, q, TILES - 1 if high else 0)
                    first = (4 if high else 0) + 2 * h
                elif axis == 1:
                    edge = (lane & 15) + (112 if high else 0)
                    v = pick(tile(src, q, 4 * h), edge)
                    for k in range(1, 4):
                        v = jnp.where(lane >> 5 == k, pick(tile(src, q, 4 * h + k), edge), v)
                    v = jnp.where(own_x, v, subs(v, 4))
                    first = 2 if high else 0
                else:
                    v = pick(tile(src, q, 4 * h), index)
                    for k in range(1, 4):
                        v = jnp.where(lane >> 5 == k, pick(tile(src, q, 4 * h + k), index), v)
                    v = jnp.where(own_x, v, subs(v, 4))
                    v = jnp.where(own_y, v, subs(v, 2))
                    first = 0
                for b in range(2):
                    out[b, r : r + 1, :] = v[first + b : first + b + 1, :]


def divide(x, n):
    return x >> (n.bit_length() - 1) if n & (n - 1) == 0 else lax.div(x, jnp.int32(n))


def plan_rows(level_ref, near_ref, link_ref, plan, me, sizes):
    sections, members, blocks = sizes
    level = level_ref[me[0]]
    chip = jnp.where(me[1] % 2 == 0, 1, -1)

    def placed(ids):
        safe = jnp.maximum(ids, 0)
        local = divide(safe, blocks)
        within = safe - local * blocks
        section = divide(local, members)
        offset = local - section * members - me[1]
        which = jnp.where(offset == 0, 0, jnp.where(offset == chip, 1, 2))
        apart = section ^ me[0]
        one = (which * sections + apart) * blocks + within
        later = jnp.clip(section + 1, 2, max(sections - 2, 2))
        two = (which * (sections - 1) + jnp.where(apart < 2, apart, later)) * blocks + within
        source = jnp.zeros_like(ids)
        for s in range(sections):
            source = jnp.where(section == s, level_ref[s], source)
        return (one, two), source

    plan[0:1, 64:65] = jnp.full((1, 1), level, jnp.int32)
    split = jnp.zeros((1, 1), jnp.int32)
    for block in range(blocks):
        near = near_ref[block : block + 1, :]
        near_slots, _ = placed(near)
        links = link_ref[block]
        link_slots, source = placed(links)
        coarse = (links >= 0) & (source < level)
        fine = (links >= 0) & (source >= level)
        place = lax.broadcasted_iota(jnp.int32, links.shape, 0)
        quadrant = jnp.max(jnp.where(coarse, place, -1), axis=0, keepdims=True)
        any_fine = jnp.max(jnp.where(fine, 1, 0), axis=0, keepdims=True)
        kind = jnp.where(quadrant >= 0, 1, jnp.where(any_fine > 0, 2, 3))
        kind = jnp.where(near[:, :6] >= 0, 0, kind)
        split = jnp.maximum(split, jnp.max(jnp.where(kind == 2, 1, 0), axis=1, keepdims=True))
        for r in range(2):
            first = 32 * r
            plan[block : block + 1, first : first + 18] = jnp.where(near >= 0, near_slots[r], -1)
            plan[2 + 4 * block : 6 + 4 * block, first : first + 6] = jnp.where(fine, link_slots[r], -1)
            chosen = jnp.max(jnp.where(coarse, link_slots[r], -1), axis=0, keepdims=True)
            plan[10 + block : 11 + block, first : first + 6] = chosen
            plan[12 + block : 13 + block, first : first + 6] = kind
            plan[14 + block : 15 + block, first : first + 6] = quadrant
    plan[0:1, 65:66] = split


def arrived(plan, base, table, halo, blocks, fine):
    sub, lane = iotas()
    sub, lane = sub[:5], lane[:5]

    def rows(slot, j, part):
        first = 10 * (j ^ 1) + 5 * part
        return table[slot, first : first + 5, :]

    def whole(scalar):
        return jnp.full((5, 128), scalar, jnp.int32)

    spread = (lane >> 5) * 16 + ((lane & 15) >> 1)
    for block in range(blocks):
        for j in range(6):
            kind = whole(plan[12 + block, base + j])
            near = jnp.maximum(plan[block, base + j], 0)
            slot = jnp.maximum(plan[10 + block, base + j], 0)
            quadrant = whole(plan[14 + block, base + j])
            source = jnp.where(quadrant < 2, rows(slot, j, 0), rows(slot, j, 1))
            source = jnp.where((quadrant & 1) == 1, lanes(source, -8), source)
            rest = [WEIGHTS[q] for q in LISTS[j ^ 1]]
            straight = rest.index(WEIGHTS[1])
            rest = jnp.where(sub == straight, jnp.float32(WEIGHTS[1]), jnp.float32(WEIGHTS[7]))
            for h in range(2):
                coarse = pick(lanes(source, 64) if h else source, spread)
                value = jnp.where(kind == 0, rows(near, j, h), jnp.where(kind == 1, coarse, rest))
                r = 10 * j + 5 * h
                if fine:
                    value = jnp.where(kind == 2, halo[block, r : r + 5, :], value)
                halo[block, r : r + 5, :] = value


def arrived_fine(plan, base, table, halo, blocks):
    _, lane = iotas()
    lane = lane[:5]
    odd_v, odd_u = (lane & 1) == 1, ((lane >> 4) & 1) == 1
    gather = (2 * ((lane >> 4) & 3) + (lane >> 6)) * 16 + 2 * (lane & 7) + ((lane >> 3) & 1)
    for block in range(blocks):
        for j in range(6):
            first = 10 * (j ^ 1)
            for a in range(2):
                pairs = []
                for h in range(2):
                    sums = []
                    for b in range(2):
                        slot = plan[2 + 4 * block + 2 * a + b, base + j]
                        scale = jnp.where(slot >= 0, jnp.float32(0.25), jnp.float32(0.0))
                        v = table[jnp.maximum(slot, 0), first + 5 * h : first + 5 * h + 5, :] * scale
                        sums.append(v + lanes(v, 1 if b else -1))
                    v = jnp.where(odd_v, sums[1], sums[0])
                    pairs.append(v + lanes(v, 16 if h else -16))
                r = 10 * j + 5 * a
                halo[block, r : r + 5, :] = pick(jnp.where(odd_u, pairs[1], pairs[0]), gather)


def stream(src, dst, plan, base, table, halo, blocks, done):
    sub, lane = iotas()
    odd = (sub & 1) == 1
    xl, yh = sub // 4, (sub // 2) % 2
    z = lane & 15

    def both(one, two):
        return jnp.where(odd, two, one)

    def plane(j, i, h):
        r = 10 * j + 5 * h + i
        return both(bulk(halo.at[0], r), bulk(halo.at[1], r))

    def edge_row(q, e, h):
        a = [n for n in range(3) if VELOCITIES[q][n]][0]
        j = 2 * a + (0 if VELOCITIES[q][a] > 0 else 1)
        r = 10 * j + 5 * h + LISTS[j].index(q)
        found = []
        for block in range(blocks):
            slot = plan[block, base + e]
            good = jnp.full((8, 128), slot, jnp.int32) >= 0
            found.append(jnp.where(good, bulk(table.at[jnp.maximum(slot, 0)], r), jnp.float32(WEIGHTS[q])))
        return both(*found)

    for q in range(19):
        c = VELOCITIES[q]
        moving = [a for a in range(3) if c[a]]
        e = VELOCITIES.index(tuple(-v for v in c)) - 1
        planes = {}
        for a in moving:
            j = 2 * a + (0 if c[a] < 0 else 1)
            i = LISTS[j ^ 1].index(q)
            planes[a] = [plane(j, i, h) for h in range(2)]
        if c[1]:
            up = c[1] > 0
            y_edge = lane >= 112 if up else lane < 16
            inner = yh == (1 if up else 0)
            beside = [jnp.where(xl == 0, v, lanes(v, -16)) for v in planes[1]]

            def joined(v, border):
                return jnp.where(y_edge, jnp.where(inner, subs(v, 2 * c[1]), border), v)

        if c[2]:
            z_edge = z == (0 if c[2] > 0 else 15)
            tile_of = z & 3 if c[2] > 0 else (15 - z) & 3
            index = (2 * tile_of + xl) * 16 + ((yh * 8 + (lane >> 4) - c[1]) & 15)
            columns = []
            for h in range(2):
                v = planes[2][h]
                if c[1]:
                    line = edge_row(q, e, h)
                    place, natural = (15 if c[1] > 0 else 0), (15 if c[2] > 0 else 0)
                    if place != natural:
                        line = lanes(line, place - natural)
                    v = jnp.where(z == place, line, v)
                columns.append(pick(v, index))
        shift = 16 * c[1] + c[2]
        first = 8 + 4 * c[0]
        for t in range(TILES):
            h, k = t // 4, t % 4
            v = tile(src, q, t)
            if c[1]:
                turn = (112 if c[1] > 0 else 0) - 32 * k
                v = joined(v, lanes(beside[h], turn) if turn % 128 else beside[h])
            if shift:
                v = lanes(v, shift)
            if c[2]:
                v = jnp.where(z_edge, lanes(columns[h], -k * c[2]) if k else columns[h], v)
            dst[q, first + 8 * t : first + 8 * t + 8, :] = v
        if c[0]:
            v = jnp.where(yh == 1, planes[0][1], planes[0][0])
            if c[1]:
                v = lanes(joined(v, edge_row(q, e, 1 if c[1] > 0 else 0)), shift)
            if c[2]:
                line = jnp.where(yh == 1, edge_row(q, e, 1), edge_row(q, e, 0))
                v = jnp.where(z_edge, lanes(line, -15 * c[2]), lanes(v, shift))
            r = 8 if c[0] > 0 else 68
            dst[q, r : r + 4, :] = v[:4]
        done(q)


def nothing(_):
    pass


def first_kernel(level_hbm, pops_hbm, mask_hbm, star, out, mask, level_ref, pops, sems):
    def part(t):
        here = pl.ds(8 * t, 8)
        return pltpu.make_async_copy(pops_hbm.at[:, here, :], pops.at[:, here, :], sems.at[t])

    small = [
        pltpu.make_async_copy(level_hbm, level_ref, sems.at[TILES]),
        pltpu.make_async_copy(mask_hbm, mask, sems.at[TILES + 1]),
    ]
    parts = [part(t) for t in range(TILES)]
    for copy in small + parts:
        copy.start()
    for copy in small:
        copy.wait()
    level = level_ref[lax.axis_index("section")]

    @pl.when(level >= 1)
    def _():
        collide(pops, 0, star, mask, relax_rate(level), lambda t: parts[t].wait())

    @pl.when(level < 1)
    def _():
        for copy in parts:
            copy.wait()
        star[...] = pops[...]

    export(star, out)


def plan_kernel(sizes, level_hbm, near_hbm, link_hbm, plan, level_ref, near, links, sems):
    copies = [
        pltpu.make_async_copy(level_hbm, level_ref, sems.at[0]),
        pltpu.make_async_copy(near_hbm, near, sems.at[1]),
        pltpu.make_async_copy(link_hbm, links, sems.at[2]),
    ]
    for copy in copies:
        copy.start()
    for copy in copies:
        copy.wait()
    me = (lax.axis_index("section"), lax.axis_index("member"))
    plan_rows(level_ref, near, links, plan, me, sizes)


def gathered(parts, table):
    row = 0
    for part in parts:
        for k in range(part.shape[0]):
            table[row] = part[k]
            row += 1


def settle_kernel(plan, star, result, sems):
    @pl.when(plan[0, 64] < 2)
    def _():
        copy = pltpu.make_async_copy(star, result, sems.at[0])
        copy.start()
        copy.wait()


def middle_kernel(blocks, plan, star, mask, own, chip, near, far, dst, out, table, halo, moved):
    level = plan[0, 64]

    @pl.when(level >= 1)
    def _():
        gathered((own, chip, near, far), table)

        @pl.when(plan[0, 65] > 0)
        def _():
            arrived_fine(plan, 0, table, halo, blocks)

        arrived(plan, 0, table, halo, blocks, True)
        stream(star, moved, plan, 0, table, halo, blocks, nothing)

    @pl.when(level < 1)
    def _():
        dst[...] = star[...]

    @pl.when(level == 1)
    def _():
        dst[...] = moved[:, 8 : 8 + ROWS, :]

    @pl.when(level == 2)
    def _():
        collide(moved, 8, dst, mask, relax_rate(level), nothing)

    export(dst, out)


def last_kernel(blocks, plan, star, own, chip, near, far, settled, result, table, halo, moved, sems):
    @pl.when(plan[0, 64] == 2)
    def _():
        copies = [
            pltpu.make_async_copy(moved.at[q, 8 : 8 + ROWS], result.at[q], sems.at[q]) for q in range(19)
        ]
        gathered((own, chip, near, far), table)
        arrived(plan, 32, table, halo, blocks, False)
        stream(star, moved, plan, 32, table, halo, blocks, lambda q: copies[q].start())
        for copy in copies:
            copy.wait()


def swap(x, sections, members, target):
    pairs = []
    for s in range(sections):
        for m in range(members):
            t = target(s, m)
            if 0 <= t[1] < members:
                pairs.append((s * members + m, t[0] * members + t[1]))
    return lax.ppermute(x, ("section", "member"), pairs)


def exchange(exports, sections, members, last):
    me = lax.axis_index("section")

    def named(x, target):
        return swap(x, sections, members, target)

    def beside(s, m):
        t = ((m + 1) ^ 1) - 1
        return (s, t) if 0 <= t < members else (s ^ 1, m)

    parts = [exports] + [named(exports, lambda s, m, d=d: (s ^ d, m)) for d in range(1, sections)]
    first = jnp.concatenate(parts[:2], axis=0)
    if last:
        second = []
        for t in range(1, sections - 2):
            value = parts[sections - 1]
            for d in range(2, sections - 1):
                value = jnp.where(me ^ d == t, parts[d], value)
            second.append(value)
        second = jnp.concatenate(second, axis=0)
    else:
        second = jnp.concatenate(parts[2:], axis=0)
    own = jnp.concatenate([first, second], axis=0)
    near = named(first, beside)
    far = named(second, beside)
    chip = named(own, lambda s, m: (s, m ^ 1))
    return own, chip, near, far


def packed(x):
    n, cells = x.shape[0], x.shape[-1]
    x = x.reshape(n, -1, cells // 128, 128)
    return x.transpose(1, 2, 0, 3).reshape(-1, n * cells // 128, 128)


VMEM = pl.BlockSpec(memory_space=pltpu.VMEM)
HBM = pl.BlockSpec(memory_space=pltpu.HBM)


def body(populations, fluid_mask, section_level, neighbours, interface):
    sections, members = lax.axis_size("section"), lax.axis_size("member")
    blocks, _, cells = populations.shape
    sizes = (sections, members, blocks)
    params = pltpu.CompilerParams(vmem_limit_bytes=16 << 20)
    pops = packed(populations)
    mask = packed(fluid_mask)[0]
    links = interface.transpose(0, 2, 1)
    field = jax.ShapeDtypeStruct(pops.shape, jnp.float32)
    planes = jax.ShapeDtypeStruct((blocks, ROWS, 128), jnp.float32)
    halo = pltpu.VMEM((blocks, ROWS, 128), jnp.float32)
    moved = pltpu.VMEM((19, ROWS + 16, 128), jnp.float32)

    def fixed(*values):
        return tuple(pltpu.with_memory_space_constraint(x, pltpu.HBM) for x in values)

    star, exports, mask = pl.pallas_call(
        first_kernel,
        out_shape=(field, planes, jax.ShapeDtypeStruct(mask.shape, jnp.int32)),
        in_specs=[HBM] * 3,
        out_specs=(VMEM,) * 3,
        scratch_shapes=[
            pltpu.SMEM(section_level.shape, jnp.int32),
            pltpu.VMEM(pops.shape, jnp.float32),
            pltpu.SemaphoreType.DMA((TILES + 2,)),
        ],
        compiler_params=params,
        name="first",
    )(*fixed(section_level, pops, mask))
    plan = pl.pallas_call(
        functools.partial(plan_kernel, sizes),
        out_shape=jax.ShapeDtypeStruct((16, 128), jnp.int32),
        in_specs=[HBM] * 3,
        out_specs=VMEM,
        scratch_shapes=[
            pltpu.SMEM(section_level.shape, jnp.int32),
            pltpu.VMEM(neighbours.shape, jnp.int32),
            pltpu.VMEM(links.shape, jnp.int32),
            pltpu.SemaphoreType.DMA((3,)),
        ],
        compiler_params=params,
        name="plan",
    )(*fixed(section_level, neighbours, links))
    parts = exchange(exports, sections, members, False)
    star, exports = pl.pallas_call(
        functools.partial(middle_kernel, blocks),
        out_shape=(field, planes),
        in_specs=[VMEM] * 7,
        out_specs=(VMEM, VMEM),
        scratch_shapes=[pltpu.VMEM((3 * sections * blocks, ROWS, 128), jnp.float32), halo, moved],
        compiler_params=params,
        name="middle",
    )(plan, star, mask, *parts)
    settled = pl.pallas_call(
        settle_kernel,
        out_shape=field,
        in_specs=[VMEM] * 2,
        out_specs=HBM,
        scratch_shapes=[pltpu.SemaphoreType.DMA((1,))],
        compiler_params=params,
        name="settled",
    )(plan, star)
    parts = exchange(exports, sections, members, True)
    result = pl.pallas_call(
        functools.partial(last_kernel, blocks),
        out_shape=field,
        in_specs=[VMEM] * 6 + [HBM],
        out_specs=HBM,
        input_output_aliases={6: 0},
        scratch_shapes=[
            pltpu.VMEM((3 * (sections - 1) * blocks, ROWS, 128), jnp.float32),
            halo,
            moved,
            pltpu.SemaphoreType.DMA((19,)),
        ],
        compiler_params=params,
        name="last",
    )(plan, star, *parts, settled)
    out = result.reshape(19, cells // 128, blocks, 128).transpose(2, 0, 1, 3)
    return out.reshape(blocks, 19, cells)


def solution(mesh):
    return jax.shard_map(
        body,
        mesh=mesh,
        in_specs=(
            P(("section", "member"), None, None),
            P(("section", "member"), None),
            P(),
            P(("section", "member"), None),
            P(("section", "member"), None, None),
        ),
        out_specs=P(("section", "member"), None, None),
        check_vma=False,
    )
```

```python
import functools

import jax
import jax.numpy as jnp
from jax import lax
from jax.experimental import pallas as pl
from jax.experimental.pallas import tpu as pltpu
from jax.sharding import PartitionSpec as P


VELOCITIES = (
    (0, 0, 0), (1, 0, 0), (-1, 0, 0), (0, 1, 0), (0, -1, 0), (0, 0, 1), (0, 0, -1),
    (1, 1, 0), (-1, -1, 0), (1, -1, 0), (-1, 1, 0), (1, 0, 1), (-1, 0, -1), (1, 0, -1),
    (-1, 0, 1), (0, 1, 1), (0, -1, -1), (0, 1, -1), (0, -1, 1),
)
WEIGHTS = (1.0 / 3.0,) + (1.0 / 18.0,) * 6 + (1.0 / 36.0,) * 12
OPPOSITE = (0, 2, 1, 4, 3, 6, 5, 8, 7, 10, 9, 12, 11, 14, 13, 16, 15, 18, 17)
LISTS = [
    [q for q in range(19) if sum(a * b for a, b in zip(VELOCITIES[q], VELOCITIES[1 + j])) == 1]
    for j in range(6)
]
ROWS = 64
PLANES = 60
TILES = 8


def iotas():
    sub = lax.broadcasted_iota(jnp.int32, (8, 128), 0)
    lane = lax.broadcasted_iota(jnp.int32, (8, 128), 1)
    return sub, lane


def pick(x, index):
    return jnp.take_along_axis(x, index, axis=1, mode="promise_in_bounds")


def lanes(x, shift):
    return pltpu.roll(x, shift % 128, 1)


def subs(x, shift):
    return pltpu.roll(x, shift % 8, 0)


def tile(ref, q, t, base=0):
    return ref[q, base + 8 * t : base + 8 * t + 8, :]


def bulk(ref, row):
    return jnp.broadcast_to(ref[row : row + 1, :], (8, 128))


def entry(row, lane):
    column = lane if lane < 32 else lane - 14 if lane < 64 else lane - 28
    return 16 * column + row


def number(plan, row, lane):
    return plan[entry(row, lane), 0]


def spread_rows(plan, row, lane, height):
    r = entry(row, lane)
    return jnp.broadcast_to(plan[r : r + 1, :], (height, 128))


def relax_rate(level):
    return jnp.where(
        level == 0, jnp.float32(1.0 / 0.55), jnp.where(level == 1, jnp.float32(1.0 / 0.6), jnp.float32(1.0 / 0.7))
    )


def collide(src, base, dst, mask, rate, ready):
    for t in range(TILES):
        ready(t)
        f = [tile(src, q, t, base) for q in range(19)]
        density = f[0]
        for q in range(1, 19):
            density = density + f[q]
        velocity = []
        for a in range(3):
            plus = [q for q in range(19) if VELOCITIES[q][a] > 0]
            total = f[plus[0]] - f[OPPOSITE[plus[0]]]
            for q in plus[1:]:
                total = total + (f[q] - f[OPPOSITE[q]])
            velocity.append(total / density)
        speed = velocity[0] * velocity[0] + velocity[1] * velocity[1] + velocity[2] * velocity[2]
        still = 1.0 - 1.5 * speed
        fluid = mask[8 * t : 8 * t + 8, :] == 1
        keep = 1.0 - rate
        scaled = [rate * jnp.float32(w) * density for w in (WEIGHTS[0], WEIGHTS[1], WEIGHTS[7])]
        out = keep * f[0] + scaled[0] * still
        dst[0, 8 * t : 8 * t + 8, :] = jnp.where(fluid, out, f[0])
        for q in range(1, 19, 2):
            o = OPPOSITE[q]
            along = None
            for a in range(3):
                c = VELOCITIES[q][a]
                if c:
                    term = velocity[a] if c > 0 else -velocity[a]
                    along = term if along is None else along + term
            weight = scaled[1] if q < 7 else scaled[2]
            even = still + 4.5 * along * along
            odd = 3.0 * along
            dst[q, 8 * t : 8 * t + 8, :] = jnp.where(fluid, keep * f[q] + weight * (even + odd), f[o])
            dst[o, 8 * t : 8 * t + 8, :] = jnp.where(fluid, keep * f[o] + weight * (even - odd), f[q])


def export(src, out):
    sub, lane = iotas()
    xl, yh = sub // 4, (sub // 2) % 2
    own_x = ((lane >> 4) & 1) == xl
    own_y = ((lane >> 3) & 1) == yh
    for j in range(6):
        axis, high = j // 2, j % 2 == 0
        index = (lane & 7) * 16 + (15 if high else 0)
        for i, q in enumerate(LISTS[j]):
            for h in range(2):
                r = 10 * j + 5 * h + i
                if axis == 0:
                    v = tile(src, q, TILES - 1 if high else 0)
                    first = (4 if high else 0) + 2 * h
                elif axis == 1:
                    edge = (lane & 15) + (112 if high else 0)
                    v = pick(tile(src, q, 4 * h), edge)
                    for k in range(1, 4):
                        v = jnp.where(lane >> 5 == k, pick(tile(src, q, 4 * h + k), edge), v)
                    v = jnp.where(own_x, v, subs(v, 4))
                    first = 2 if high else 0
                else:
                    v = pick(tile(src, q, 4 * h), index)
                    for k in range(1, 4):
                        v = jnp.where(lane >> 5 == k, pick(tile(src, q, 4 * h + k), index), v)
                    v = jnp.where(own_x, v, subs(v, 4))
                    v = jnp.where(own_y, v, subs(v, 2))
                    first = 0
                for b in range(2):
                    out[PLANES * b + r : PLANES * b + r + 1, :] = v[first + b : first + b + 1, :]


def divide(x, n):
    return x >> (n.bit_length() - 1) if n & (n - 1) == 0 else lax.div(x, jnp.int32(n))


def plan_rows(level_ref, near_ref, link_ref, plan, me, sizes):
    sections, members, blocks = sizes
    level = level_ref[me[0]]
    chip = jnp.where(me[1] % 2 == 0, 1, -1)

    def placed(ids):
        safe = jnp.maximum(ids, 0)
        local = divide(safe, blocks)
        within = safe - local * blocks
        section = divide(local, members)
        offset = local - section * members - me[1]
        which = jnp.where(offset == 0, 0, jnp.where(offset == chip, 1, 2))
        apart = section ^ me[0]
        one = (which * sections + apart) * blocks + within
        later = jnp.clip(section + 1, 2, max(sections - 2, 2))
        two = (which * (sections - 1) + jnp.where(apart < 2, apart, later)) * blocks + within
        source = jnp.zeros_like(ids)
        for s in range(sections):
            source = jnp.where(section == s, level_ref[s], source)
        return (one, two), source

    plan[0:1, 64:65] = jnp.full((1, 1), level, jnp.int32)
    split = jnp.zeros((1, 1), jnp.int32)
    for block in range(blocks):
        near = near_ref[block : block + 1, :]
        near_slots, _ = placed(near)
        links = link_ref[block]
        link_slots, source = placed(links)
        coarse = (links >= 0) & (source < level)
        fine = (links >= 0) & (source >= level)
        place = lax.broadcasted_iota(jnp.int32, links.shape, 0)
        quadrant = jnp.max(jnp.where(coarse, place, -1), axis=0, keepdims=True)
        any_fine = jnp.max(jnp.where(fine, 1, 0), axis=0, keepdims=True)
        kind = jnp.where(quadrant >= 0, 1, jnp.where(any_fine > 0, 2, 3))
        kind = jnp.where(near[:, :6] >= 0, 0, kind)
        split = jnp.maximum(split, jnp.max(jnp.where(kind == 2, 1, 0), axis=1, keepdims=True))
        for r in range(2):
            first = 32 * r
            plan[block : block + 1, first : first + 18] = jnp.where(near >= 0, near_slots[r], -1)
            plan[2 + 4 * block : 6 + 4 * block, first : first + 6] = jnp.where(fine, link_slots[r], -1)
            chosen = jnp.max(jnp.where(coarse, link_slots[r], -1), axis=0, keepdims=True)
            plan[10 + block : 11 + block, first : first + 6] = chosen
            plan[12 + block : 13 + block, first : first + 6] = kind
            plan[14 + block : 15 + block, first : first + 6] = quadrant
    plan[0:1, 65:66] = split


def arrived(plan, base, table, halo, blocks, fine):
    sub, lane = iotas()
    sub, lane = sub[:5], lane[:5]

    def rows(slot, j, part):
        first = 10 * (j ^ 1) + 5 * part
        return table[slot, first : first + 5, :]

    spread = (lane >> 5) * 16 + ((lane & 15) >> 1)
    for block in range(blocks):
        for j in range(6):
            kind = spread_rows(plan, 12 + block, base + j, 5)
            near = jnp.maximum(number(plan, block, base + j), 0)
            slot = jnp.maximum(number(plan, 10 + block, base + j), 0)
            quadrant = spread_rows(plan, 14 + block, base + j, 5)
            source = jnp.where(quadrant < 2, rows(slot, j, 0), rows(slot, j, 1))
            source = jnp.where((quadrant & 1) == 1, lanes(source, -8), source)
            rest = [WEIGHTS[q] for q in LISTS[j ^ 1]]
            straight = rest.index(WEIGHTS[1])
            rest = jnp.where(sub == straight, jnp.float32(WEIGHTS[1]), jnp.float32(WEIGHTS[7]))
            for h in range(2):
                coarse = pick(lanes(source, 64) if h else source, spread)
                value = jnp.where(kind == 0, rows(near, j, h), jnp.where(kind == 1, coarse, rest))
                r = 10 * j + 5 * h
                if fine:
                    value = jnp.where(kind == 2, halo[block, r : r + 5, :], value)
                halo[block, r : r + 5, :] = value


def arrived_fine(plan, base, table, halo, blocks):
    _, lane = iotas()
    lane = lane[:5]
    odd_v, odd_u = (lane & 1) == 1, ((lane >> 4) & 1) == 1
    gather = (2 * ((lane >> 4) & 3) + (lane >> 6)) * 16 + 2 * (lane & 7) + ((lane >> 3) & 1)
    for block in range(blocks):
        for j in range(6):
            first = 10 * (j ^ 1)
            for a in range(2):
                pairs = []
                for h in range(2):
                    sums = []
                    for b in range(2):
                        place = 2 + 4 * block + 2 * a + b
                        slot = jnp.maximum(number(plan, place, base + j), 0)
                        named = spread_rows(plan, place, base + j, 5) >= 0
                        scale = jnp.where(named, jnp.float32(0.25), jnp.float32(0.0))
                        v = table[slot, first + 5 * h : first + 5 * h + 5, :] * scale
                        sums.append(v + lanes(v, 1 if b else -1))
                    v = jnp.where(odd_v, sums[1], sums[0])
                    pairs.append(v + lanes(v, 16 if h else -16))
                r = 10 * j + 5 * a
                halo[block, r : r + 5, :] = pick(jnp.where(odd_u, pairs[1], pairs[0]), gather)


def stream(src, dst, plan, base, table, halo, blocks, done):
    sub, lane = iotas()
    odd = (sub & 1) == 1
    xl, yh = sub // 4, (sub // 2) % 2
    z = lane & 15

    def both(one, two):
        return jnp.where(odd, two, one)

    def plane(j, i, h):
        r = 10 * j + 5 * h + i
        return both(bulk(halo.at[0], r), bulk(halo.at[1], r))

    def edge_row(q, e, h):
        a = [n for n in range(3) if VELOCITIES[q][n]][0]
        j = 2 * a + (0 if VELOCITIES[q][a] > 0 else 1)
        r = 10 * j + 5 * h + LISTS[j].index(q)
        found = []
        for block in range(blocks):
            slot = jnp.maximum(number(plan, block, base + e), 0)
            good = spread_rows(plan, block, base + e, 8) >= 0
            found.append(jnp.where(good, bulk(table.at[slot], r), jnp.float32(WEIGHTS[q])))
        return both(*found)

    for q in range(19):
        c = VELOCITIES[q]
        moving = [a for a in range(3) if c[a]]
        e = VELOCITIES.index(tuple(-v for v in c)) - 1
        planes = {}
        for a in moving:
            j = 2 * a + (0 if c[a] < 0 else 1)
            i = LISTS[j ^ 1].index(q)
            planes[a] = [plane(j, i, h) for h in range(2)]
        if c[1]:
            up = c[1] > 0
            y_edge = lane >= 112 if up else lane < 16
            inner = yh == (1 if up else 0)
            beside = [jnp.where(xl == 0, v, lanes(v, -16)) for v in planes[1]]

            def joined(v, border):
                return jnp.where(y_edge, jnp.where(inner, subs(v, 2 * c[1]), border), v)

        if c[2]:
            z_edge = z == (0 if c[2] > 0 else 15)
            tile_of = z & 3 if c[2] > 0 else (15 - z) & 3
            index = (2 * tile_of + xl) * 16 + ((yh * 8 + (lane >> 4) - c[1]) & 15)
            columns = []
            for h in range(2):
                v = planes[2][h]
                if c[1]:
                    line = edge_row(q, e, h)
                    place, natural = (15 if c[1] > 0 else 0), (15 if c[2] > 0 else 0)
                    if place != natural:
                        line = lanes(line, place - natural)
                    v = jnp.where(z == place, line, v)
                columns.append(pick(v, index))
        shift = 16 * c[1] + c[2]
        first = 8 + 4 * c[0]
        for t in range(TILES):
            h, k = t // 4, t % 4
            v = tile(src, q, t)
            if c[1]:
                turn = (112 if c[1] > 0 else 0) - 32 * k
                v = joined(v, lanes(beside[h], turn) if turn % 128 else beside[h])
            if shift:
                v = lanes(v, shift)
            if c[2]:
                v = jnp.where(z_edge, lanes(columns[h], -k * c[2]) if k else columns[h], v)
            dst[q, first + 8 * t : first + 8 * t + 8, :] = v
        if c[0]:
            v = jnp.where(yh == 1, planes[0][1], planes[0][0])
            if c[1]:
                v = lanes(joined(v, edge_row(q, e, 1 if c[1] > 0 else 0)), shift)
            if c[2]:
                line = jnp.where(yh == 1, edge_row(q, e, 1), edge_row(q, e, 0))
                v = jnp.where(z_edge, lanes(line, -15 * c[2]), lanes(v, shift))
            r = 8 if c[0] > 0 else 68
            dst[q, r : r + 4, :] = v[:4]
        done(q)


def nothing(_):
    pass


def first_kernel(level_hbm, pops_hbm, mask_hbm, star, out, mask, level_ref, pops, sems):
    def part(t):
        here = pl.ds(8 * t, 8)
        return pltpu.make_async_copy(pops_hbm.at[:, here, :], pops.at[:, here, :], sems.at[t])

    small = [
        pltpu.make_async_copy(level_hbm, level_ref, sems.at[TILES]),
        pltpu.make_async_copy(mask_hbm, mask, sems.at[TILES + 1]),
    ]
    parts = [part(t) for t in range(TILES)]
    for copy in small + parts:
        copy.start()
    for copy in small:
        copy.wait()
    level = level_ref[lax.axis_index("section")]

    @pl.when(level >= 1)
    def _():
        collide(pops, 0, star, mask, relax_rate(level), lambda t: parts[t].wait())

    @pl.when(level < 1)
    def _():
        for copy in parts:
            copy.wait()
        star[...] = pops[...]

    export(star, out)


def plan_kernel(sizes, level_hbm, near_hbm, link_hbm, plan, level_ref, near, links, packed_plan, sems):
    copies = [
        pltpu.make_async_copy(level_hbm, level_ref, sems.at[0]),
        pltpu.make_async_copy(near_hbm, near, sems.at[1]),
        pltpu.make_async_copy(link_hbm, links, sems.at[2]),
    ]
    for copy in copies:
        copy.start()
    for copy in copies:
        copy.wait()
    me = (lax.axis_index("section"), lax.axis_index("member"))
    plan_rows(level_ref, near, links, packed_plan, me, sizes)
    for lane in [*range(18), *range(32, 50), 64, 65]:
        r = entry(0, lane)
        plan[r : r + 16, :] = jnp.broadcast_to(packed_plan[:, lane : lane + 1], (16, 128))


def gathered(parts, table):
    slot = 0
    for part in parts:
        for r in range(0, part.shape[0], PLANES):
            table[slot, :PLANES] = part[r : r + PLANES, :]
            slot += 1


def settle_kernel(plan, star, result, sems):
    @pl.when(number(plan, 0, 64) < 2)
    def _():
        copy = pltpu.make_async_copy(star, result, sems.at[0])
        copy.start()
        copy.wait()


def middle_kernel(blocks, plan, star, mask, own, chip, near, far, dst, out, table, halo, moved):
    level = number(plan, 0, 64)

    @pl.when(level >= 1)
    def _():
        gathered((own, chip, near, far), table)

        @pl.when(number(plan, 0, 65) > 0)
        def _():
            arrived_fine(plan, 0, table, halo, blocks)

        arrived(plan, 0, table, halo, blocks, True)
        stream(star, moved, plan, 0, table, halo, blocks, nothing)

    @pl.when(level < 1)
    def _():
        dst[...] = star[...]

    @pl.when(level == 1)
    def _():
        dst[...] = moved[:, 8 : 8 + ROWS, :]

    @pl.when(level == 2)
    def _():
        collide(moved, 8, dst, mask, relax_rate(level), nothing)

    export(dst, out)


def last_kernel(blocks, plan, star, own, chip, near, far, settled, result, table, halo, moved, sems):
    @pl.when(number(plan, 0, 64) == 2)
    def _():
        copies = [
            pltpu.make_async_copy(moved.at[q, 8 : 8 + ROWS], result.at[q], sems.at[q]) for q in range(19)
        ]
        gathered((own, chip, near, far), table)
        arrived(plan, 32, table, halo, blocks, False)
        stream(star, moved, plan, 32, table, halo, blocks, lambda q: copies[q].start())
        for copy in copies:
            copy.wait()


def swap(x, sections, members, target):
    pairs = []
    for s in range(sections):
        for m in range(members):
            t = target(s, m)
            if 0 <= t[1] < members:
                pairs.append((s * members + m, t[0] * members + t[1]))
    return lax.ppermute(x, ("section", "member"), pairs)


def exchange(exports, sections, members, last):
    me = lax.axis_index("section")

    def named(x, target):
        return swap(x, sections, members, target)

    def beside(s, m):
        t = ((m + 1) ^ 1) - 1
        return (s, t) if 0 <= t < members else (s ^ 1, m)

    parts = [exports] + [named(exports, lambda s, m, d=d: (s ^ d, m)) for d in range(1, sections)]
    first = jnp.concatenate(parts[:2], axis=0)
    if last:
        second = []
        for t in range(1, sections - 2):
            value = parts[sections - 1]
            for d in range(2, sections - 1):
                value = jnp.where(me ^ d == t, parts[d], value)
            second.append(value)
        second = jnp.concatenate(second, axis=0)
    else:
        second = jnp.concatenate(parts[2:], axis=0)
    own = jnp.concatenate([first, second], axis=0)
    near = named(first, beside)
    far = named(second, beside)
    chip = named(own, lambda s, m: (s, m ^ 1))
    return own, chip, near, far


def packed(x):
    n, cells = x.shape[0], x.shape[-1]
    x = x.reshape(n, -1, cells // 128, 128)
    return x.transpose(1, 2, 0, 3).reshape(-1, n * cells // 128, 128)


VMEM = pl.BlockSpec(memory_space=pltpu.VMEM)
HBM = pl.BlockSpec(memory_space=pltpu.HBM)


def body(populations, fluid_mask, section_level, neighbours, interface):
    sections, members = lax.axis_size("section"), lax.axis_size("member")
    blocks, _, cells = populations.shape
    sizes = (sections, members, blocks)
    params = pltpu.CompilerParams(vmem_limit_bytes=16 << 20)
    pops = packed(populations)
    mask = packed(fluid_mask)[0]
    links = interface.transpose(0, 2, 1)
    field = jax.ShapeDtypeStruct(pops.shape, jnp.float32)
    planes = jax.ShapeDtypeStruct((blocks * PLANES, 128), jnp.float32)
    halo = pltpu.VMEM((blocks, ROWS, 128), jnp.float32)
    moved = pltpu.VMEM((19, ROWS + 16, 128), jnp.float32)

    def fixed(*values):
        return tuple(pltpu.with_memory_space_constraint(x, pltpu.HBM) for x in values)

    star, exports, mask = pl.pallas_call(
        first_kernel,
        out_shape=(field, planes, jax.ShapeDtypeStruct(mask.shape, jnp.int32)),
        in_specs=[HBM] * 3,
        out_specs=(VMEM,) * 3,
        scratch_shapes=[
            pltpu.SMEM(section_level.shape, jnp.int32),
            pltpu.VMEM(pops.shape, jnp.float32),
            pltpu.SemaphoreType.DMA((TILES + 2,)),
        ],
        compiler_params=params,
        name="first",
    )(*fixed(section_level, pops, mask))
    plan = pl.pallas_call(
        functools.partial(plan_kernel, sizes),
        out_shape=jax.ShapeDtypeStruct((16 * 38, 128), jnp.int32),
        in_specs=[HBM] * 3,
        out_specs=VMEM,
        scratch_shapes=[
            pltpu.SMEM(section_level.shape, jnp.int32),
            pltpu.VMEM(neighbours.shape, jnp.int32),
            pltpu.VMEM(links.shape, jnp.int32),
            pltpu.VMEM((16, 128), jnp.int32),
            pltpu.SemaphoreType.DMA((3,)),
        ],
        compiler_params=params,
        name="plan",
    )(*fixed(section_level, neighbours, links))
    parts = exchange(exports, sections, members, False)
    star, exports = pl.pallas_call(
        functools.partial(middle_kernel, blocks),
        out_shape=(field, planes),
        in_specs=[VMEM] * 7,
        out_specs=(VMEM, VMEM),
        scratch_shapes=[pltpu.VMEM((3 * sections * blocks, ROWS, 128), jnp.float32), halo, moved],
        compiler_params=params,
        name="middle",
    )(plan, star, mask, *parts)
    settled = pl.pallas_call(
        settle_kernel,
        out_shape=field,
        in_specs=[VMEM] * 2,
        out_specs=HBM,
        scratch_shapes=[pltpu.SemaphoreType.DMA((1,))],
        compiler_params=params,
        name="settled",
    )(plan, star)
    parts = exchange(exports, sections, members, True)
    result = pl.pallas_call(
        functools.partial(last_kernel, blocks),
        out_shape=field,
        in_specs=[VMEM] * 6 + [HBM],
        out_specs=HBM,
        input_output_aliases={6: 0},
        scratch_shapes=[
            pltpu.VMEM((3 * (sections - 1) * blocks, ROWS, 128), jnp.float32),
            halo,
            moved,
            pltpu.SemaphoreType.DMA((19,)),
        ],
        compiler_params=params,
        name="last",
    )(plan, star, *parts, settled)
    out = result.reshape(19, cells // 128, blocks, 128).transpose(2, 0, 1, 3)
    return out.reshape(blocks, 19, cells)


def solution(mesh):
    return jax.shard_map(
        body,
        mesh=mesh,
        in_specs=(
            P(("section", "member"), None, None),
            P(("section", "member"), None),
            P(),
            P(("section", "member"), None),
            P(("section", "member"), None, None),
        ),
        out_specs=P(("section", "member"), None, None),
        check_vma=False,
    )
```

```python
import functools

import jax
import jax.numpy as jnp
from jax import lax
from jax.experimental import pallas as pl
from jax.experimental.pallas import tpu as pltpu
from jax.sharding import PartitionSpec as P


VELOCITIES = (
    (0, 0, 0), (1, 0, 0), (-1, 0, 0), (0, 1, 0), (0, -1, 0), (0, 0, 1), (0, 0, -1),
    (1, 1, 0), (-1, -1, 0), (1, -1, 0), (-1, 1, 0), (1, 0, 1), (-1, 0, -1), (1, 0, -1),
    (-1, 0, 1), (0, 1, 1), (0, -1, -1), (0, 1, -1), (0, -1, 1),
)
WEIGHTS = (1.0 / 3.0,) + (1.0 / 18.0,) * 6 + (1.0 / 36.0,) * 12
OPPOSITE = (0, 2, 1, 4, 3, 6, 5, 8, 7, 10, 9, 12, 11, 14, 13, 16, 15, 18, 17)
LISTS = [
    [q for q in range(19) if sum(a * b for a, b in zip(VELOCITIES[q], VELOCITIES[1 + j])) == 1]
    for j in range(6)
]
ROWS = 64
PLANES = 60
TILES = 8


def iotas():
    sub = lax.broadcasted_iota(jnp.int32, (8, 128), 0)
    lane = lax.broadcasted_iota(jnp.int32, (8, 128), 1)
    return sub, lane


def pick(x, index):
    return jnp.take_along_axis(x, index, axis=1, mode="promise_in_bounds")


def lanes(x, shift):
    return pltpu.roll(x, shift % 128, 1)


def subs(x, shift):
    return pltpu.roll(x, shift % 8, 0)


def tile(ref, q, t, base=0):
    return ref[q, base + 8 * t : base + 8 * t + 8, :]


def bulk(ref, row):
    return jnp.broadcast_to(ref[row : row + 1, :], (8, 128))


def entry(row, lane):
    column = lane if lane < 32 else lane - 14 if lane < 64 else lane - 28
    return 16 * column + row


def number(plan, row, lane):
    return plan[entry(row, lane), 0]


def spread_rows(plan, row, lane, height):
    r = entry(row, lane)
    return jnp.broadcast_to(plan[r : r + 1, :], (height, 128))


def relax_rate(level):
    return jnp.where(
        level == 0, jnp.float32(1.0 / 0.55), jnp.where(level == 1, jnp.float32(1.0 / 0.6), jnp.float32(1.0 / 0.7))
    )


def collide(src, base, dst, mask, rate, ready):
    for t in range(TILES):
        ready(t)
        f = [tile(src, q, t, base) for q in range(19)]
        density = f[0]
        for q in range(1, 19):
            density = density + f[q]
        velocity = []
        for a in range(3):
            plus = [q for q in range(19) if VELOCITIES[q][a] > 0]
            total = f[plus[0]] - f[OPPOSITE[plus[0]]]
            for q in plus[1:]:
                total = total + (f[q] - f[OPPOSITE[q]])
            velocity.append(total / density)
        speed = velocity[0] * velocity[0] + velocity[1] * velocity[1] + velocity[2] * velocity[2]
        still = 1.0 - 1.5 * speed
        fluid = mask[8 * t : 8 * t + 8, :] == 1
        keep = 1.0 - rate
        scaled = [rate * jnp.float32(w) * density for w in (WEIGHTS[0], WEIGHTS[1], WEIGHTS[7])]
        out = keep * f[0] + scaled[0] * still
        dst[0, 8 * t : 8 * t + 8, :] = jnp.where(fluid, out, f[0])
        for q in range(1, 19, 2):
            o = OPPOSITE[q]
            along = None
            for a in range(3):
                c = VELOCITIES[q][a]
                if c:
                    term = velocity[a] if c > 0 else -velocity[a]
                    along = term if along is None else along + term
            weight = scaled[1] if q < 7 else scaled[2]
            even = still + 4.5 * along * along
            odd = 3.0 * along
            dst[q, 8 * t : 8 * t + 8, :] = jnp.where(fluid, keep * f[q] + weight * (even + odd), f[o])
            dst[o, 8 * t : 8 * t + 8, :] = jnp.where(fluid, keep * f[o] + weight * (even - odd), f[q])


def export(src, out):
    sub, lane = iotas()
    xl, yh = sub // 4, (sub // 2) % 2
    own_x = ((lane >> 4) & 1) == xl
    own_y = ((lane >> 3) & 1) == yh
    for j in range(6):
        axis, high = j // 2, j % 2 == 0
        index = (lane & 7) * 16 + (15 if high else 0)
        for i, q in enumerate(LISTS[j]):
            for h in range(2):
                r = 10 * j + 5 * h + i
                if axis == 0:
                    v = tile(src, q, TILES - 1 if high else 0)
                    first = (4 if high else 0) + 2 * h
                elif axis == 1:
                    edge = (lane & 15) + (112 if high else 0)
                    v = pick(tile(src, q, 4 * h), edge)
                    for k in range(1, 4):
                        v = jnp.where(lane >> 5 == k, pick(tile(src, q, 4 * h + k), edge), v)
                    v = jnp.where(own_x, v, subs(v, 4))
                    first = 2 if high else 0
                else:
                    v = pick(tile(src, q, 4 * h), index)
                    for k in range(1, 4):
                        v = jnp.where(lane >> 5 == k, pick(tile(src, q, 4 * h + k), index), v)
                    v = jnp.where(own_x, v, subs(v, 4))
                    v = jnp.where(own_y, v, subs(v, 2))
                    first = 0
                for b in range(2):
                    out[PLANES * b + r : PLANES * b + r + 1, :] = v[first + b : first + b + 1, :]


def divide(x, n):
    return x >> (n.bit_length() - 1) if n & (n - 1) == 0 else lax.div(x, jnp.int32(n))


def plan_rows(level_ref, near_ref, link_ref, plan, me, sizes):
    sections, members, blocks = sizes
    level = level_ref[me[0]]
    chip = jnp.where(me[1] % 2 == 0, 1, -1)

    def placed(ids):
        safe = jnp.maximum(ids, 0)
        local = divide(safe, blocks)
        within = safe - local * blocks
        section = divide(local, members)
        offset = local - section * members - me[1]
        which = jnp.where(offset == 0, 0, jnp.where(offset == chip, 1, 2))
        apart = section ^ me[0]
        one = (which * sections + apart) * blocks + within
        later = jnp.clip(section + 1, 2, max(sections - 2, 2))
        two = (which * (sections - 1) + jnp.where(apart < 2, apart, later)) * blocks + within
        source = jnp.zeros_like(ids)
        for s in range(sections):
            source = jnp.where(section == s, level_ref[s], source)
        return (one, two), source

    plan[0:1, 64:65] = jnp.full((1, 1), level, jnp.int32)
    split = jnp.zeros((1, 1), jnp.int32)
    for block in range(blocks):
        near = near_ref[block : block + 1, :]
        near_slots, _ = placed(near)
        links = link_ref[block]
        link_slots, source = placed(links)
        coarse = (links >= 0) & (source < level)
        fine = (links >= 0) & (source >= level)
        place = lax.broadcasted_iota(jnp.int32, links.shape, 0)
        quadrant = jnp.max(jnp.where(coarse, place, -1), axis=0, keepdims=True)
        any_fine = jnp.max(jnp.where(fine, 1, 0), axis=0, keepdims=True)
        kind = jnp.where(quadrant >= 0, 1, jnp.where(any_fine > 0, 2, 3))
        kind = jnp.where(near[:, :6] >= 0, 0, kind)
        split = jnp.maximum(split, jnp.max(jnp.where(kind == 2, 1, 0), axis=1, keepdims=True))
        for r in range(2):
            first = 32 * r
            plan[block : block + 1, first : first + 18] = jnp.where(near >= 0, near_slots[r], -1)
            plan[2 + 4 * block : 6 + 4 * block, first : first + 6] = jnp.where(fine, link_slots[r], -1)
            chosen = jnp.max(jnp.where(coarse, link_slots[r], -1), axis=0, keepdims=True)
            plan[10 + block : 11 + block, first : first + 6] = chosen
            plan[12 + block : 13 + block, first : first + 6] = kind
            plan[14 + block : 15 + block, first : first + 6] = quadrant
    plan[0:1, 65:66] = split


def arrived(plan, base, table, halo, blocks, fine):
    sub, lane = iotas()
    sub, lane = sub[:5], lane[:5]

    def rows(slot, j, part):
        first = 10 * (j ^ 1) + 5 * part
        return table[slot, first : first + 5, :]

    spread = (lane >> 5) * 16 + ((lane & 15) >> 1)
    for block in range(blocks):
        for j in range(6):
            kind = spread_rows(plan, 12 + block, base + j, 5)
            near = jnp.maximum(number(plan, block, base + j), 0)
            slot = jnp.maximum(number(plan, 10 + block, base + j), 0)
            quadrant = spread_rows(plan, 14 + block, base + j, 5)
            source = jnp.where(quadrant < 2, rows(slot, j, 0), rows(slot, j, 1))
            source = jnp.where((quadrant & 1) == 1, lanes(source, -8), source)
            rest = [WEIGHTS[q] for q in LISTS[j ^ 1]]
            straight = rest.index(WEIGHTS[1])
            rest = jnp.where(sub == straight, jnp.float32(WEIGHTS[1]), jnp.float32(WEIGHTS[7]))
            for h in range(2):
                coarse = pick(lanes(source, 64) if h else source, spread)
                value = jnp.where(kind == 0, rows(near, j, h), jnp.where(kind == 1, coarse, rest))
                r = 10 * j + 5 * h
                if fine:
                    value = jnp.where(kind == 2, halo[block, r : r + 5, :], value)
                halo[block, r : r + 5, :] = value


def arrived_fine(plan, base, table, halo, blocks):
    _, lane = iotas()
    lane = lane[:5]
    odd_v, odd_u = (lane & 1) == 1, ((lane >> 4) & 1) == 1
    gather = (2 * ((lane >> 4) & 3) + (lane >> 6)) * 16 + 2 * (lane & 7) + ((lane >> 3) & 1)
    for block in range(blocks):
        for j in range(6):
            first = 10 * (j ^ 1)
            for a in range(2):
                pairs = []
                for h in range(2):
                    sums = []
                    for b in range(2):
                        place = 2 + 4 * block + 2 * a + b
                        slot = jnp.maximum(number(plan, place, base + j), 0)
                        named = spread_rows(plan, place, base + j, 5) >= 0
                        scale = jnp.where(named, jnp.float32(0.25), jnp.float32(0.0))
                        v = table[slot, first + 5 * h : first + 5 * h + 5, :] * scale
                        sums.append(v + lanes(v, 1 if b else -1))
                    v = jnp.where(odd_v, sums[1], sums[0])
                    pairs.append(v + lanes(v, 16 if h else -16))
                r = 10 * j + 5 * a
                halo[block, r : r + 5, :] = pick(jnp.where(odd_u, pairs[1], pairs[0]), gather)


def stream(src, dst, plan, base, table, halo, blocks, done):
    sub, lane = iotas()
    odd = (sub & 1) == 1
    xl, yh = sub // 4, (sub // 2) % 2
    z = lane & 15

    def both(one, two):
        return jnp.where(odd, two, one)

    def plane(j, i, h):
        r = 10 * j + 5 * h + i
        return both(bulk(halo.at[0], r), bulk(halo.at[1], r))

    def edge_row(q, e, h):
        a = [n for n in range(3) if VELOCITIES[q][n]][0]
        j = 2 * a + (0 if VELOCITIES[q][a] > 0 else 1)
        r = 10 * j + 5 * h + LISTS[j].index(q)
        found = []
        for block in range(blocks):
            slot = jnp.maximum(number(plan, block, base + e), 0)
            good = spread_rows(plan, block, base + e, 8) >= 0
            found.append(jnp.where(good, bulk(table.at[slot], r), jnp.float32(WEIGHTS[q])))
        return both(*found)

    for q in range(19):
        c = VELOCITIES[q]
        moving = [a for a in range(3) if c[a]]
        e = VELOCITIES.index(tuple(-v for v in c)) - 1
        planes = {}
        for a in moving:
            j = 2 * a + (0 if c[a] < 0 else 1)
            i = LISTS[j ^ 1].index(q)
            planes[a] = [plane(j, i, h) for h in range(2)]
        if c[1]:
            up = c[1] > 0
            y_edge = lane >= 112 if up else lane < 16
            inner = yh == (1 if up else 0)
            beside = [jnp.where(xl == 0, v, lanes(v, -16)) for v in planes[1]]

            def joined(v, border):
                return jnp.where(y_edge, jnp.where(inner, subs(v, 2 * c[1]), border), v)

        if c[2]:
            z_edge = z == (0 if c[2] > 0 else 15)
            tile_of = z & 3 if c[2] > 0 else (15 - z) & 3
            index = (2 * tile_of + xl) * 16 + ((yh * 8 + (lane >> 4) - c[1]) & 15)
            columns = []
            for h in range(2):
                v = planes[2][h]
                if c[1]:
                    line = edge_row(q, e, h)
                    place, natural = (15 if c[1] > 0 else 0), (15 if c[2] > 0 else 0)
                    if place != natural:
                        line = lanes(line, place - natural)
                    v = jnp.where(z == place, line, v)
                columns.append(pick(v, index))
        shift = 16 * c[1] + c[2]
        first = 8 + 4 * c[0]
        for t in range(TILES):
            h, k = t // 4, t % 4
            v = tile(src, q, t)
            if c[1]:
                turn = (112 if c[1] > 0 else 0) - 32 * k
                v = joined(v, lanes(beside[h], turn) if turn % 128 else beside[h])
            if shift:
                v = lanes(v, shift)
            if c[2]:
                v = jnp.where(z_edge, lanes(columns[h], -k * c[2]) if k else columns[h], v)
            dst[q, first + 8 * t : first + 8 * t + 8, :] = v
        if c[0]:
            v = jnp.where(yh == 1, planes[0][1], planes[0][0])
            if c[1]:
                v = lanes(joined(v, edge_row(q, e, 1 if c[1] > 0 else 0)), shift)
            if c[2]:
                line = jnp.where(yh == 1, edge_row(q, e, 1), edge_row(q, e, 0))
                v = jnp.where(z_edge, lanes(line, -15 * c[2]), lanes(v, shift))
            r = 8 if c[0] > 0 else 68
            dst[q, r : r + 4, :] = v[:4]
        done(q)


def nothing(_):
    pass


def first_kernel(level_hbm, pops_hbm, mask_hbm, star, out, mask, level_ref, pops, sems):
    def part(t):
        here = pl.ds(8 * t, 8)
        return pltpu.make_async_copy(pops_hbm.at[:, here, :], pops.at[:, here, :], sems.at[t])

    small = [
        pltpu.make_async_copy(level_hbm, level_ref, sems.at[TILES]),
        pltpu.make_async_copy(mask_hbm, mask, sems.at[TILES + 1]),
    ]
    parts = [part(t) for t in range(TILES)]
    for copy in small + parts:
        copy.start()
    for copy in small:
        copy.wait()
    level = level_ref[lax.axis_index("section")]

    @pl.when(level >= 1)
    def _():
        collide(pops, 0, star, mask, relax_rate(level), lambda t: parts[t].wait())

    @pl.when(level < 1)
    def _():
        for copy in parts:
            copy.wait()
        star[...] = pops[...]

    export(star, out)


def plan_kernel(sizes, level_hbm, near_hbm, link_hbm, plan, level_ref, near, links, packed_plan, sems):
    copies = [
        pltpu.make_async_copy(level_hbm, level_ref, sems.at[0]),
        pltpu.make_async_copy(near_hbm, near, sems.at[1]),
        pltpu.make_async_copy(link_hbm, links, sems.at[2]),
    ]
    for copy in copies:
        copy.start()
    for copy in copies:
        copy.wait()
    me = (lax.axis_index("section"), lax.axis_index("member"))
    plan_rows(level_ref, near, links, packed_plan, me, sizes)
    for lane in [*range(18), *range(32, 50), 64, 65]:
        r = entry(0, lane)
        plan[r : r + 16, :] = jnp.broadcast_to(packed_plan[:, lane : lane + 1], (16, 128))


def gathered(parts, table):
    slot = 0
    for part in parts:
        for r in range(0, part.shape[0], PLANES):
            table[slot, :PLANES] = part[r : r + PLANES, :]
            slot += 1


def settle_kernel(plan, star, result, sems):
    @pl.when(number(plan, 0, 64) < 2)
    def _():
        copy = pltpu.make_async_copy(star, result, sems.at[0])
        copy.start()
        copy.wait()


def middle_kernel(blocks, plan, star, mask, own, own2, chip, chip2, near, far, dst, out, table, halo, moved):
    level = number(plan, 0, 64)

    @pl.when(level >= 1)
    def _():
        gathered((own, own2, chip, chip2, near, far), table)

        @pl.when(number(plan, 0, 65) > 0)
        def _():
            arrived_fine(plan, 0, table, halo, blocks)

        arrived(plan, 0, table, halo, blocks, True)
        stream(star, moved, plan, 0, table, halo, blocks, nothing)

    @pl.when(level < 1)
    def _():
        dst[...] = star[...]

    @pl.when(level == 1)
    def _():
        dst[...] = moved[:, 8 : 8 + ROWS, :]

    @pl.when(level == 2)
    def _():
        collide(moved, 8, dst, mask, relax_rate(level), nothing)

    export(dst, out)


def last_kernel(blocks, plan, star, own, own2, chip, chip2, near, far, settled, result, table, halo, moved, sems):
    @pl.when(number(plan, 0, 64) == 2)
    def _():
        copies = [
            pltpu.make_async_copy(moved.at[q, 8 : 8 + ROWS], result.at[q], sems.at[q]) for q in range(19)
        ]
        gathered((own, own2, chip, chip2, near, far), table)
        arrived(plan, 32, table, halo, blocks, False)
        stream(star, moved, plan, 32, table, halo, blocks, lambda q: copies[q].start())
        for copy in copies:
            copy.wait()


def swap(x, sections, members, target):
    pairs = []
    for s in range(sections):
        for m in range(members):
            t = target(s, m)
            if 0 <= t[1] < members:
                pairs.append((s * members + m, t[0] * members + t[1]))
    return lax.ppermute(x, ("section", "member"), pairs)


def exchange(exports, sections, members, last):
    me = lax.axis_index("section")

    def named(x, target):
        return swap(x, sections, members, target)

    def across(d):
        def target(s, m):
            low, high = min(s, s ^ d), max(s, s ^ d)
            needed = low >= 1 if last else (low, high) != (0, sections - 1)
            return (s ^ d, m) if needed else (s, m ^ 1)

        return target

    def beside(s, m):
        if last and s < 2:
            return (s, m ^ 1)
        t = ((m + 1) ^ 1) - 1
        return (s, t) if 0 <= t < members else (s ^ 1, m)

    parts = [exports] + [named(exports, across(d)) for d in range(1, sections)]
    first = jnp.concatenate(parts[:2], axis=0)
    if last:
        second = []
        for t in range(1, sections - 2):
            value = parts[sections - 1]
            for d in range(2, sections - 1):
                value = jnp.where(me ^ d == t, parts[d], value)
            second.append(value)
        second = jnp.concatenate(second, axis=0)
    else:
        second = jnp.concatenate(parts[2:], axis=0)
    near = named(first, beside)
    far = named(second, beside)
    chip = named(first, lambda s, m: (s, m ^ 1))
    rest = named(second, lambda s, m: (s, m ^ 1))
    return first, second, chip, rest, near, far


def packed(x):
    n, cells = x.shape[0], x.shape[-1]
    x = x.reshape(n, -1, cells // 128, 128)
    return x.transpose(1, 2, 0, 3).reshape(-1, n * cells // 128, 128)


VMEM = pl.BlockSpec(memory_space=pltpu.VMEM)
HBM = pl.BlockSpec(memory_space=pltpu.HBM)


def body(populations, fluid_mask, section_level, neighbours, interface):
    sections, members = lax.axis_size("section"), lax.axis_size("member")
    blocks, _, cells = populations.shape
    sizes = (sections, members, blocks)
    params = pltpu.CompilerParams(vmem_limit_bytes=16 << 20)
    pops = packed(populations)
    mask = packed(fluid_mask)[0]
    links = interface.transpose(0, 2, 1)
    field = jax.ShapeDtypeStruct(pops.shape, jnp.float32)
    planes = jax.ShapeDtypeStruct((blocks * PLANES, 128), jnp.float32)
    halo = pltpu.VMEM((blocks, ROWS, 128), jnp.float32)
    moved = pltpu.VMEM((19, ROWS + 16, 128), jnp.float32)

    def fixed(*values):
        return tuple(pltpu.with_memory_space_constraint(x, pltpu.HBM) for x in values)

    star, exports, mask = pl.pallas_call(
        first_kernel,
        out_shape=(field, planes, jax.ShapeDtypeStruct(mask.shape, jnp.int32)),
        in_specs=[HBM] * 3,
        out_specs=(VMEM,) * 3,
        scratch_shapes=[
            pltpu.SMEM(section_level.shape, jnp.int32),
            pltpu.VMEM(pops.shape, jnp.float32),
            pltpu.SemaphoreType.DMA((TILES + 2,)),
        ],
        compiler_params=params,
        name="first",
    )(*fixed(section_level, pops, mask))
    plan = pl.pallas_call(
        functools.partial(plan_kernel, sizes),
        out_shape=jax.ShapeDtypeStruct((16 * 38, 128), jnp.int32),
        in_specs=[HBM] * 3,
        out_specs=VMEM,
        scratch_shapes=[
            pltpu.SMEM(section_level.shape, jnp.int32),
            pltpu.VMEM(neighbours.shape, jnp.int32),
            pltpu.VMEM(links.shape, jnp.int32),
            pltpu.VMEM((16, 128), jnp.int32),
            pltpu.SemaphoreType.DMA((3,)),
        ],
        compiler_params=params,
        name="plan",
    )(*fixed(section_level, neighbours, links))
    parts = exchange(exports, sections, members, False)
    star, exports = pl.pallas_call(
        functools.partial(middle_kernel, blocks),
        out_shape=(field, planes),
        in_specs=[VMEM] * 9,
        out_specs=(VMEM, VMEM),
        scratch_shapes=[pltpu.VMEM((3 * sections * blocks, ROWS, 128), jnp.float32), halo, moved],
        compiler_params=params,
        name="middle",
    )(plan, star, mask, *parts)
    settled = pl.pallas_call(
        settle_kernel,
        out_shape=field,
        in_specs=[VMEM] * 2,
        out_specs=HBM,
        scratch_shapes=[pltpu.SemaphoreType.DMA((1,))],
        compiler_params=params,
        name="settled",
    )(plan, star)
    parts = exchange(exports, sections, members, True)
    result = pl.pallas_call(
        functools.partial(last_kernel, blocks),
        out_shape=field,
        in_specs=[VMEM] * 8 + [HBM],
        out_specs=HBM,
        input_output_aliases={8: 0},
        scratch_shapes=[
            pltpu.VMEM((3 * (sections - 1) * blocks, ROWS, 128), jnp.float32),
            halo,
            moved,
            pltpu.SemaphoreType.DMA((19,)),
        ],
        compiler_params=params,
        name="last",
    )(plan, star, *parts, settled)
    out = result.reshape(19, cells // 128, blocks, 128).transpose(2, 0, 1, 3)
    return out.reshape(blocks, 19, cells)


def solution(mesh):
    return jax.shard_map(
        body,
        mesh=mesh,
        in_specs=(
            P(("section", "member"), None, None),
            P(("section", "member"), None),
            P(),
            P(("section", "member"), None),
            P(("section", "member"), None, None),
        ),
        out_specs=P(("section", "member"), None, None),
        check_vma=False,
    )
```

```python
import functools

import jax
import jax.numpy as jnp
from jax import lax
from jax.experimental import pallas as pl
from jax.experimental.pallas import tpu as pltpu
from jax.sharding import PartitionSpec as P


VELOCITIES = (
    (0, 0, 0), (1, 0, 0), (-1, 0, 0), (0, 1, 0), (0, -1, 0), (0, 0, 1), (0, 0, -1),
    (1, 1, 0), (-1, -1, 0), (1, -1, 0), (-1, 1, 0), (1, 0, 1), (-1, 0, -1), (1, 0, -1),
    (-1, 0, 1), (0, 1, 1), (0, -1, -1), (0, 1, -1), (0, -1, 1),
)
WEIGHTS = (1.0 / 3.0,) + (1.0 / 18.0,) * 6 + (1.0 / 36.0,) * 12
OPPOSITE = (0, 2, 1, 4, 3, 6, 5, 8, 7, 10, 9, 12, 11, 14, 13, 16, 15, 18, 17)
LISTS = [
    [q for q in range(19) if sum(a * b for a, b in zip(VELOCITIES[q], VELOCITIES[1 + j])) == 1]
    for j in range(6)
]
ROWS = 64
PLANES = 60
TILES = 8


def iotas():
    sub = lax.broadcasted_iota(jnp.int32, (8, 128), 0)
    lane = lax.broadcasted_iota(jnp.int32, (8, 128), 1)
    return sub, lane


def pick(x, index):
    return jnp.take_along_axis(x, index, axis=1, mode="promise_in_bounds")


def lanes(x, shift):
    return pltpu.roll(x, shift % 128, 1)


def subs(x, shift):
    return pltpu.roll(x, shift % 8, 0)


def tile(ref, q, t, base=0):
    return ref[q, base + 8 * t : base + 8 * t + 8, :]


def bulk(ref, row):
    return jnp.broadcast_to(ref[row : row + 1, :], (8, 128))


def entry(row, lane):
    column = lane if lane < 32 else lane - 14 if lane < 64 else lane - 28
    return 16 * column + row


def number(plan, row, lane):
    return plan[entry(row, lane), 0]


def spread_rows(plan, row, lane, height):
    r = entry(row, lane)
    return jnp.broadcast_to(plan[r : r + 1, :], (height, 128))


def relax_rate(level):
    return jnp.where(
        level == 0, jnp.float32(1.0 / 0.55), jnp.where(level == 1, jnp.float32(1.0 / 0.6), jnp.float32(1.0 / 0.7))
    )


def collide(src, base, dst, mask, rate, ready):
    for t in range(TILES):
        ready(t)
        f = [tile(src, q, t, base) for q in range(19)]
        density = f[0]
        for q in range(1, 19):
            density = density + f[q]
        velocity = []
        for a in range(3):
            plus = [q for q in range(19) if VELOCITIES[q][a] > 0]
            total = f[plus[0]] - f[OPPOSITE[plus[0]]]
            for q in plus[1:]:
                total = total + (f[q] - f[OPPOSITE[q]])
            velocity.append(total / density)
        speed = velocity[0] * velocity[0] + velocity[1] * velocity[1] + velocity[2] * velocity[2]
        still = 1.0 - 1.5 * speed
        fluid = mask[8 * t : 8 * t + 8, :] == 1
        keep = 1.0 - rate
        scaled = [rate * jnp.float32(w) * density for w in (WEIGHTS[0], WEIGHTS[1], WEIGHTS[7])]
        out = keep * f[0] + scaled[0] * still
        dst[0, 8 * t : 8 * t + 8, :] = jnp.where(fluid, out, f[0])
        for q in range(1, 19, 2):
            o = OPPOSITE[q]
            along = None
            for a in range(3):
                c = VELOCITIES[q][a]
                if c:
                    term = velocity[a] if c > 0 else -velocity[a]
                    along = term if along is None else along + term
            weight = scaled[1] if q < 7 else scaled[2]
            even = still + 4.5 * along * along
            odd = 3.0 * along
            dst[q, 8 * t : 8 * t + 8, :] = jnp.where(fluid, keep * f[q] + weight * (even + odd), f[o])
            dst[o, 8 * t : 8 * t + 8, :] = jnp.where(fluid, keep * f[o] + weight * (even - odd), f[q])


def export(src, out):
    sub, lane = iotas()
    xl, yh = sub // 4, (sub // 2) % 2
    own_x = ((lane >> 4) & 1) == xl
    own_y = ((lane >> 3) & 1) == yh
    for j in range(6):
        axis, high = j // 2, j % 2 == 0
        index = (lane & 7) * 16 + (15 if high else 0)
        for i, q in enumerate(LISTS[j]):
            for h in range(2):
                r = 10 * j + 5 * h + i
                if axis == 0:
                    v = tile(src, q, TILES - 1 if high else 0)
                    first = (4 if high else 0) + 2 * h
                elif axis == 1:
                    edge = (lane & 15) + (112 if high else 0)
                    v = pick(tile(src, q, 4 * h), edge)
                    for k in range(1, 4):
                        v = jnp.where(lane >> 5 == k, pick(tile(src, q, 4 * h + k), edge), v)
                    v = jnp.where(own_x, v, subs(v, 4))
                    first = 2 if high else 0
                else:
                    v = pick(tile(src, q, 4 * h), index)
                    for k in range(1, 4):
                        v = jnp.where(lane >> 5 == k, pick(tile(src, q, 4 * h + k), index), v)
                    v = jnp.where(own_x, v, subs(v, 4))
                    v = jnp.where(own_y, v, subs(v, 2))
                    first = 0
                for b in range(2):
                    out[PLANES * b + r : PLANES * b + r + 1, :] = v[first + b : first + b + 1, :]


def divide(x, n):
    return x >> (n.bit_length() - 1) if n & (n - 1) == 0 else lax.div(x, jnp.int32(n))


def plan_rows(level_ref, near_ref, link_ref, plan, me, sizes):
    sections, members, blocks = sizes
    level = level_ref[me[0]]
    chip = jnp.where(me[1] % 2 == 0, 1, -1)

    def placed(ids):
        safe = jnp.maximum(ids, 0)
        local = divide(safe, blocks)
        within = safe - local * blocks
        section = divide(local, members)
        offset = local - section * members - me[1]
        which = jnp.where(offset == 0, 0, jnp.where(offset == chip, 1, 2))
        apart = section ^ me[0]
        one = (which * sections + apart) * blocks + within
        later = jnp.clip(section + 1, 2, max(sections - 2, 2))
        two = (which * (sections - 1) + jnp.where(apart < 2, apart, later)) * blocks + within
        source = jnp.zeros_like(ids)
        for s in range(sections):
            source = jnp.where(section == s, level_ref[s], source)
        return (one, two), source

    plan[0:1, 64:65] = jnp.full((1, 1), level, jnp.int32)
    split = jnp.zeros((1, 1), jnp.int32)
    for block in range(blocks):
        near = near_ref[block : block + 1, :]
        near_slots, _ = placed(near)
        links = link_ref[block]
        link_slots, source = placed(links)
        coarse = (links >= 0) & (source < level)
        fine = (links >= 0) & (source >= level)
        place = lax.broadcasted_iota(jnp.int32, links.shape, 0)
        quadrant = jnp.max(jnp.where(coarse, place, -1), axis=0, keepdims=True)
        any_fine = jnp.max(jnp.where(fine, 1, 0), axis=0, keepdims=True)
        kind = jnp.where(quadrant >= 0, 1, jnp.where(any_fine > 0, 2, 3))
        kind = jnp.where(near[:, :6] >= 0, 0, kind)
        split = jnp.maximum(split, jnp.max(jnp.where(kind == 2, 1, 0), axis=1, keepdims=True))
        for r in range(2):
            first = 32 * r
            plan[block : block + 1, first : first + 18] = jnp.where(near >= 0, near_slots[r], -1)
            plan[2 + 4 * block : 6 + 4 * block, first : first + 6] = jnp.where(fine, link_slots[r], -1)
            chosen = jnp.max(jnp.where(coarse, link_slots[r], -1), axis=0, keepdims=True)
            plan[10 + block : 11 + block, first : first + 6] = chosen
            plan[12 + block : 13 + block, first : first + 6] = kind
            plan[14 + block : 15 + block, first : first + 6] = quadrant
    plan[0:1, 65:66] = split


def arrived(plan, base, table, halo, blocks, fine):
    sub, lane = iotas()
    sub, lane = sub[:5], lane[:5]

    def rows(slot, j, part):
        first = 10 * (j ^ 1) + 5 * part
        return table[slot, first : first + 5, :]

    spread = (lane >> 5) * 16 + ((lane & 15) >> 1)
    for block in range(blocks):
        for j in range(6):
            kind = spread_rows(plan, 12 + block, base + j, 5)
            near = jnp.maximum(number(plan, block, base + j), 0)
            slot = jnp.maximum(number(plan, 10 + block, base + j), 0)
            quadrant = spread_rows(plan, 14 + block, base + j, 5)
            source = jnp.where(quadrant < 2, rows(slot, j, 0), rows(slot, j, 1))
            source = jnp.where((quadrant & 1) == 1, lanes(source, -8), source)
            rest = [WEIGHTS[q] for q in LISTS[j ^ 1]]
            straight = rest.index(WEIGHTS[1])
            rest = jnp.where(sub == straight, jnp.float32(WEIGHTS[1]), jnp.float32(WEIGHTS[7]))
            for h in range(2):
                coarse = pick(lanes(source, 64) if h else source, spread)
                value = jnp.where(kind == 0, rows(near, j, h), jnp.where(kind == 1, coarse, rest))
                r = 10 * j + 5 * h
                if fine:
                    value = jnp.where(kind == 2, halo[block, r : r + 5, :], value)
                halo[block, r : r + 5, :] = value


def arrived_fine(plan, base, table, halo, blocks):
    _, lane = iotas()
    lane = lane[:5]
    odd_v, odd_u = (lane & 1) == 1, ((lane >> 4) & 1) == 1
    gather = (2 * ((lane >> 4) & 3) + (lane >> 6)) * 16 + 2 * (lane & 7) + ((lane >> 3) & 1)
    for block in range(blocks):
        for j in range(6):
            first = 10 * (j ^ 1)
            for a in range(2):
                pairs = []
                for h in range(2):
                    sums = []
                    for b in range(2):
                        place = 2 + 4 * block + 2 * a + b
                        slot = jnp.maximum(number(plan, place, base + j), 0)
                        named = spread_rows(plan, place, base + j, 5) >= 0
                        scale = jnp.where(named, jnp.float32(0.25), jnp.float32(0.0))
                        v = table[slot, first + 5 * h : first + 5 * h + 5, :] * scale
                        sums.append(v + lanes(v, 1 if b else -1))
                    v = jnp.where(odd_v, sums[1], sums[0])
                    pairs.append(v + lanes(v, 16 if h else -16))
                r = 10 * j + 5 * a
                halo[block, r : r + 5, :] = pick(jnp.where(odd_u, pairs[1], pairs[0]), gather)


def stream(src, dst, plan, base, table, halo, blocks, done):
    sub, lane = iotas()
    odd = (sub & 1) == 1
    xl, yh = sub // 4, (sub // 2) % 2
    z = lane & 15

    def both(one, two):
        return jnp.where(odd, two, one)

    def plane(j, i, h):
        r = 10 * j + 5 * h + i
        return both(bulk(halo.at[0], r), bulk(halo.at[1], r))

    def edge_row(q, e, h):
        a = [n for n in range(3) if VELOCITIES[q][n]][0]
        j = 2 * a + (0 if VELOCITIES[q][a] > 0 else 1)
        r = 10 * j + 5 * h + LISTS[j].index(q)
        found = []
        for block in range(blocks):
            slot = jnp.maximum(number(plan, block, base + e), 0)
            good = spread_rows(plan, block, base + e, 8) >= 0
            found.append(jnp.where(good, bulk(table.at[slot], r), jnp.float32(WEIGHTS[q])))
        return both(*found)

    for q in range(19):
        c = VELOCITIES[q]
        moving = [a for a in range(3) if c[a]]
        e = VELOCITIES.index(tuple(-v for v in c)) - 1
        planes = {}
        for a in moving:
            j = 2 * a + (0 if c[a] < 0 else 1)
            i = LISTS[j ^ 1].index(q)
            planes[a] = [plane(j, i, h) for h in range(2)]
        if c[1]:
            up = c[1] > 0
            y_edge = lane >= 112 if up else lane < 16
            inner = yh == (1 if up else 0)
            beside = [jnp.where(xl == 0, v, lanes(v, -16)) for v in planes[1]]

            def joined(v, border):
                return jnp.where(y_edge, jnp.where(inner, subs(v, 2 * c[1]), border), v)

        if c[2]:
            z_edge = z == (0 if c[2] > 0 else 15)
            tile_of = z & 3 if c[2] > 0 else (15 - z) & 3
            index = (2 * tile_of + xl) * 16 + ((yh * 8 + (lane >> 4) - c[1]) & 15)
            columns = []
            for h in range(2):
                v = planes[2][h]
                if c[1]:
                    line = edge_row(q, e, h)
                    place, natural = (15 if c[1] > 0 else 0), (15 if c[2] > 0 else 0)
                    if place != natural:
                        line = lanes(line, place - natural)
                    v = jnp.where(z == place, line, v)
                columns.append(pick(v, index))
        shift = 16 * c[1] + c[2]
        first = 8 + 4 * c[0]
        for t in range(TILES):
            h, k = t // 4, t % 4
            v = tile(src, q, t)
            if c[1]:
                turn = (112 if c[1] > 0 else 0) - 32 * k
                v = joined(v, lanes(beside[h], turn) if turn % 128 else beside[h])
            if shift:
                v = lanes(v, shift)
            if c[2]:
                v = jnp.where(z_edge, lanes(columns[h], -k * c[2]) if k else columns[h], v)
            dst[q, first + 8 * t : first + 8 * t + 8, :] = v
        if c[0]:
            v = jnp.where(yh == 1, planes[0][1], planes[0][0])
            if c[1]:
                v = lanes(joined(v, edge_row(q, e, 1 if c[1] > 0 else 0)), shift)
            if c[2]:
                line = jnp.where(yh == 1, edge_row(q, e, 1), edge_row(q, e, 0))
                v = jnp.where(z_edge, lanes(line, -15 * c[2]), lanes(v, shift))
            r = 8 if c[0] > 0 else 68
            dst[q, r : r + 4, :] = v[:4]
        done(q)


def nothing(_):
    pass


def first_kernel(level_hbm, pops_hbm, mask_hbm, star, out, mask, level_ref, pops, sems):
    def part(t):
        here = pl.ds(64 * t, 64)
        return pltpu.make_async_copy(pops_hbm.at[:, here, :], pops.at[:, here, :], sems.at[t])

    small = [
        pltpu.make_async_copy(level_hbm, level_ref, sems.at[TILES]),
        pltpu.make_async_copy(mask_hbm, mask, sems.at[TILES + 1]),
    ]
    parts = [part(t) for t in range(1)]
    for copy in small + parts:
        copy.start()
    for copy in small:
        copy.wait()
    level = level_ref[lax.axis_index("section")]

    @pl.when(level >= 1)
    def _():
        collide(pops, 0, star, mask, relax_rate(level), lambda t: parts[t // 8].wait() if t % 8 == 0 else None)

    @pl.when(level < 1)
    def _():
        for copy in parts:
            copy.wait()
        star[...] = pops[...]

    export(star, out)


def plan_kernel(sizes, level_hbm, near_hbm, link_hbm, plan, level_ref, near, links, packed_plan, sems):
    copies = [
        pltpu.make_async_copy(level_hbm, level_ref, sems.at[0]),
        pltpu.make_async_copy(near_hbm, near, sems.at[1]),
        pltpu.make_async_copy(link_hbm, links, sems.at[2]),
    ]
    for copy in copies:
        copy.start()
    for copy in copies:
        copy.wait()
    me = (lax.axis_index("section"), lax.axis_index("member"))
    plan_rows(level_ref, near, links, packed_plan, me, sizes)
    for lane in [*range(18), *range(32, 50), 64, 65]:
        r = entry(0, lane)
        plan[r : r + 16, :] = jnp.broadcast_to(packed_plan[:, lane : lane + 1], (16, 128))


def gathered(parts, table):
    slot = 0
    for part in parts:
        for r in range(0, part.shape[0], PLANES):
            table[slot, :PLANES] = part[r : r + PLANES, :]
            slot += 1


def settle_kernel(plan, star, result, sems):
    @pl.when(number(plan, 0, 64) < 2)
    def _():
        copy = pltpu.make_async_copy(star, result, sems.at[0])
        copy.start()
        copy.wait()


def middle_kernel(blocks, plan, star, mask, own, own2, chip, chip2, near, far, dst, out, table, halo, moved):
    level = number(plan, 0, 64)

    @pl.when(level >= 1)
    def _():
        gathered((own, own2, chip, chip2, near, far), table)

        @pl.when(number(plan, 0, 65) > 0)
        def _():
            arrived_fine(plan, 0, table, halo, blocks)

        arrived(plan, 0, table, halo, blocks, True)
        stream(star, moved, plan, 0, table, halo, blocks, nothing)

    @pl.when(level < 1)
    def _():
        dst[...] = star[...]

    @pl.when(level == 1)
    def _():
        dst[...] = moved[:, 8 : 8 + ROWS, :]

    @pl.when(level == 2)
    def _():
        collide(moved, 8, dst, mask, relax_rate(level), nothing)

    export(dst, out)


def last_kernel(blocks, plan, star, own, own2, chip, chip2, near, far, settled, result, table, halo, moved, sems):
    @pl.when(number(plan, 0, 64) == 2)
    def _():
        copies = [
            pltpu.make_async_copy(moved.at[q, 8 : 8 + ROWS], result.at[q], sems.at[q]) for q in range(19)
        ]
        gathered((own, own2, chip, chip2, near, far), table)
        arrived(plan, 32, table, halo, blocks, False)
        stream(star, moved, plan, 32, table, halo, blocks, lambda q: copies[q].start())
        for copy in copies:
            copy.wait()


def swap(x, sections, members, target):
    pairs = []
    for s in range(sections):
        for m in range(members):
            t = target(s, m)
            if 0 <= t[1] < members:
                pairs.append((s * members + m, t[0] * members + t[1]))
    return lax.ppermute(x, ("section", "member"), pairs)


def exchange(exports, sections, members, last):
    me = lax.axis_index("section")

    def named(x, target):
        return swap(x, sections, members, target)

    def across(d):
        def target(s, m):
            low, high = min(s, s ^ d), max(s, s ^ d)
            needed = low >= 1 if last else (low, high) != (0, sections - 1)
            return (s ^ d, m) if needed else (s, m ^ 1)

        return target

    def beside(s, m):
        if last and s < 2:
            return (s, m ^ 1)
        t = ((m + 1) ^ 1) - 1
        return (s, t) if 0 <= t < members else (s ^ 1, m)

    parts = [exports] + [named(exports, across(d)) for d in range(1, sections)]
    first = jnp.concatenate(parts[:2], axis=0)
    if last:
        second = []
        for t in range(1, sections - 2):
            value = parts[sections - 1]
            for d in range(2, sections - 1):
                value = jnp.where(me ^ d == t, parts[d], value)
            second.append(value)
        second = jnp.concatenate(second, axis=0)
    else:
        second = jnp.concatenate(parts[2:], axis=0)
    near = named(first, beside)
    far = named(second, beside)
    chip = named(first, lambda s, m: (s, m ^ 1))
    rest = named(second, lambda s, m: (s, m ^ 1))
    return first, second, chip, rest, near, far


def packed(x):
    n, cells = x.shape[0], x.shape[-1]
    x = x.reshape(n, -1, cells // 128, 128)
    return x.transpose(1, 2, 0, 3).reshape(-1, n * cells // 128, 128)


VMEM = pl.BlockSpec(memory_space=pltpu.VMEM)
HBM = pl.BlockSpec(memory_space=pltpu.HBM)


def body(populations, fluid_mask, section_level, neighbours, interface):
    sections, members = lax.axis_size("section"), lax.axis_size("member")
    blocks, _, cells = populations.shape
    sizes = (sections, members, blocks)
    params = pltpu.CompilerParams(vmem_limit_bytes=16 << 20)
    pops = packed(populations)
    mask = packed(fluid_mask)[0]
    links = interface.transpose(0, 2, 1)
    field = jax.ShapeDtypeStruct(pops.shape, jnp.float32)
    planes = jax.ShapeDtypeStruct((blocks * PLANES, 128), jnp.float32)
    halo = pltpu.VMEM((blocks, ROWS, 128), jnp.float32)
    moved = pltpu.VMEM((19, ROWS + 16, 128), jnp.float32)

    def fixed(*values):
        return tuple(pltpu.with_memory_space_constraint(x, pltpu.HBM) for x in values)

    star, exports, mask = pl.pallas_call(
        first_kernel,
        out_shape=(field, planes, jax.ShapeDtypeStruct(mask.shape, jnp.int32)),
        in_specs=[HBM] * 3,
        out_specs=(VMEM,) * 3,
        scratch_shapes=[
            pltpu.SMEM(section_level.shape, jnp.int32),
            pltpu.VMEM(pops.shape, jnp.float32),
            pltpu.SemaphoreType.DMA((TILES + 2,)),
        ],
        compiler_params=params,
        name="first",
    )(*fixed(section_level, pops, mask))
    plan = pl.pallas_call(
        functools.partial(plan_kernel, sizes),
        out_shape=jax.ShapeDtypeStruct((16 * 38, 128), jnp.int32),
        in_specs=[HBM] * 3,
        out_specs=VMEM,
        scratch_shapes=[
            pltpu.SMEM(section_level.shape, jnp.int32),
            pltpu.VMEM(neighbours.shape, jnp.int32),
            pltpu.VMEM(links.shape, jnp.int32),
            pltpu.VMEM((16, 128), jnp.int32),
            pltpu.SemaphoreType.DMA((3,)),
        ],
        compiler_params=params,
        name="plan",
    )(*fixed(section_level, neighbours, links))
    parts = exchange(exports, sections, members, False)
    star, exports = pl.pallas_call(
        functools.partial(middle_kernel, blocks),
        out_shape=(field, planes),
        in_specs=[VMEM] * 9,
        out_specs=(VMEM, VMEM),
        scratch_shapes=[pltpu.VMEM((3 * sections * blocks, ROWS, 128), jnp.float32), halo, moved],
        compiler_params=params,
        name="middle",
    )(plan, star, mask, *parts)
    settled = pl.pallas_call(
        settle_kernel,
        out_shape=field,
        in_specs=[VMEM] * 2,
        out_specs=HBM,
        scratch_shapes=[pltpu.SemaphoreType.DMA((1,))],
        compiler_params=params,
        name="settled",
    )(plan, star)
    parts = exchange(exports, sections, members, True)
    result = pl.pallas_call(
        functools.partial(last_kernel, blocks),
        out_shape=field,
        in_specs=[VMEM] * 8 + [HBM],
        out_specs=HBM,
        input_output_aliases={8: 0},
        scratch_shapes=[
            pltpu.VMEM((3 * (sections - 1) * blocks, ROWS, 128), jnp.float32),
            halo,
            moved,
            pltpu.SemaphoreType.DMA((19,)),
        ],
        compiler_params=params,
        name="last",
    )(plan, star, *parts, settled)
    out = result.reshape(19, cells // 128, blocks, 128).transpose(2, 0, 1, 3)
    return out.reshape(blocks, 19, cells)


def solution(mesh):
    return jax.shard_map(
        body,
        mesh=mesh,
        in_specs=(
            P(("section", "member"), None, None),
            P(("section", "member"), None),
            P(),
            P(("section", "member"), None),
            P(("section", "member"), None, None),
        ),
        out_specs=P(("section", "member"), None, None),
        check_vma=False,
    )
```

```python
import functools

import jax
import jax.numpy as jnp
from jax import lax
from jax.experimental import pallas as pl
from jax.experimental.pallas import tpu as pltpu
from jax.sharding import PartitionSpec as P


VELOCITIES = (
    (0, 0, 0), (1, 0, 0), (-1, 0, 0), (0, 1, 0), (0, -1, 0), (0, 0, 1), (0, 0, -1),
    (1, 1, 0), (-1, -1, 0), (1, -1, 0), (-1, 1, 0), (1, 0, 1), (-1, 0, -1), (1, 0, -1),
    (-1, 0, 1), (0, 1, 1), (0, -1, -1), (0, 1, -1), (0, -1, 1),
)
WEIGHTS = (1.0 / 3.0,) + (1.0 / 18.0,) * 6 + (1.0 / 36.0,) * 12
OPPOSITE = (0, 2, 1, 4, 3, 6, 5, 8, 7, 10, 9, 12, 11, 14, 13, 16, 15, 18, 17)
LISTS = [
    [q for q in range(19) if sum(a * b for a, b in zip(VELOCITIES[q], VELOCITIES[1 + j])) == 1]
    for j in range(6)
]
ROWS = 64
PLANES = 60
TILES = 8


def iotas():
    sub = lax.broadcasted_iota(jnp.int32, (8, 128), 0)
    lane = lax.broadcasted_iota(jnp.int32, (8, 128), 1)
    return sub, lane


def pick(x, index):
    return jnp.take_along_axis(x, index, axis=1, mode="promise_in_bounds")


def lanes(x, shift):
    return pltpu.roll(x, shift % 128, 1)


def subs(x, shift):
    return pltpu.roll(x, shift % 8, 0)


def tile(ref, q, t, base=0):
    return ref[q, base + 8 * t : base + 8 * t + 8, :]


def bulk(ref, row):
    return jnp.broadcast_to(ref[row : row + 1, :], (8, 128))


def entry(row, lane):
    column = lane if lane < 32 else lane - 14 if lane < 64 else lane - 28
    return 16 * column + row


def number(plan, row, lane):
    return plan[entry(row, lane), 0]


def spread_rows(plan, row, lane, height):
    r = entry(row, lane)
    return jnp.broadcast_to(plan[r : r + 1, :], (height, 128))


def relax_rate(level):
    return jnp.where(
        level == 0, jnp.float32(1.0 / 0.55), jnp.where(level == 1, jnp.float32(1.0 / 0.6), jnp.float32(1.0 / 0.7))
    )


def collide(src, base, dst, mask, rate, ready):
    for t in range(TILES):
        ready(t)
        f = [tile(src, q, t, base) for q in range(19)]
        density = f[0]
        for q in range(1, 19):
            density = density + f[q]
        velocity = []
        for a in range(3):
            plus = [q for q in range(19) if VELOCITIES[q][a] > 0]
            total = f[plus[0]] - f[OPPOSITE[plus[0]]]
            for q in plus[1:]:
                total = total + (f[q] - f[OPPOSITE[q]])
            velocity.append(total / density)
        speed = velocity[0] * velocity[0] + velocity[1] * velocity[1] + velocity[2] * velocity[2]
        still = 1.0 - 1.5 * speed
        fluid = mask[8 * t : 8 * t + 8, :] == 1
        keep = 1.0 - rate
        scaled = [rate * jnp.float32(w) * density for w in (WEIGHTS[0], WEIGHTS[1], WEIGHTS[7])]
        out = keep * f[0] + scaled[0] * still
        dst[0, 8 * t : 8 * t + 8, :] = jnp.where(fluid, out, f[0])
        for q in range(1, 19, 2):
            o = OPPOSITE[q]
            along = None
            for a in range(3):
                c = VELOCITIES[q][a]
                if c:
                    term = velocity[a] if c > 0 else -velocity[a]
                    along = term if along is None else along + term
            weight = scaled[1] if q < 7 else scaled[2]
            even = still + 4.5 * along * along
            odd = 3.0 * along
            dst[q, 8 * t : 8 * t + 8, :] = jnp.where(fluid, keep * f[q] + weight * (even + odd), f[o])
            dst[o, 8 * t : 8 * t + 8, :] = jnp.where(fluid, keep * f[o] + weight * (even - odd), f[q])


def export(src, out):
    sub, lane = iotas()
    xl, yh = sub // 4, (sub // 2) % 2
    own_x = ((lane >> 4) & 1) == xl
    own_y = ((lane >> 3) & 1) == yh
    for j in range(6):
        axis, high = j // 2, j % 2 == 0
        index = (lane & 7) * 16 + (15 if high else 0)
        for i, q in enumerate(LISTS[j]):
            for h in range(2):
                r = 10 * j + 5 * h + i
                if axis == 0:
                    v = tile(src, q, TILES - 1 if high else 0)
                    first = (4 if high else 0) + 2 * h
                elif axis == 1:
                    edge = (lane & 15) + (112 if high else 0)
                    v = pick(tile(src, q, 4 * h), edge)
                    for k in range(1, 4):
                        v = jnp.where(lane >> 5 == k, pick(tile(src, q, 4 * h + k), edge), v)
                    v = jnp.where(own_x, v, subs(v, 4))
                    first = 2 if high else 0
                else:
                    v = pick(tile(src, q, 4 * h), index)
                    for k in range(1, 4):
                        v = jnp.where(lane >> 5 == k, pick(tile(src, q, 4 * h + k), index), v)
                    v = jnp.where(own_x, v, subs(v, 4))
                    v = jnp.where(own_y, v, subs(v, 2))
                    first = 0
                for b in range(2):
                    out[PLANES * b + r : PLANES * b + r + 1, :] = v[first + b : first + b + 1, :]


def divide(x, n):
    return x >> (n.bit_length() - 1) if n & (n - 1) == 0 else lax.div(x, jnp.int32(n))


def plan_rows(level_ref, near_ref, link_ref, plan, me, sizes):
    sections, members, blocks = sizes
    level = level_ref[me[0]]
    chip = jnp.where(me[1] % 2 == 0, 1, -1)

    def placed(ids):
        safe = jnp.maximum(ids, 0)
        local = divide(safe, blocks)
        within = safe - local * blocks
        section = divide(local, members)
        offset = local - section * members - me[1]
        which = jnp.where(offset == 0, 0, jnp.where(offset == chip, 1, 2))
        apart = section ^ me[0]
        one = (which * sections + apart) * blocks + within
        later = jnp.clip(section + 1, 2, max(sections - 2, 2))
        two = (which * (sections - 1) + jnp.where(apart < 2, apart, later)) * blocks + within
        source = jnp.zeros_like(ids)
        for s in range(sections):
            source = jnp.where(section == s, level_ref[s], source)
        return (one, two), source

    plan[0:1, 64:65] = jnp.full((1, 1), level, jnp.int32)
    split = jnp.zeros((1, 1), jnp.int32)
    for block in range(blocks):
        near = near_ref[block : block + 1, :]
        near_slots, _ = placed(near)
        links = link_ref[block]
        link_slots, source = placed(links)
        coarse = (links >= 0) & (source < level)
        fine = (links >= 0) & (source >= level)
        place = lax.broadcasted_iota(jnp.int32, links.shape, 0)
        quadrant = jnp.max(jnp.where(coarse, place, -1), axis=0, keepdims=True)
        any_fine = jnp.max(jnp.where(fine, 1, 0), axis=0, keepdims=True)
        kind = jnp.where(quadrant >= 0, 1, jnp.where(any_fine > 0, 2, 3))
        kind = jnp.where(near[:, :6] >= 0, 0, kind)
        split = jnp.maximum(split, jnp.max(jnp.where(kind == 2, 1, 0), axis=1, keepdims=True))
        for r in range(2):
            first = 32 * r
            plan[block : block + 1, first : first + 18] = jnp.where(near >= 0, near_slots[r], -1)
            plan[2 + 4 * block : 6 + 4 * block, first : first + 6] = jnp.where(fine, link_slots[r], -1)
            chosen = jnp.max(jnp.where(coarse, link_slots[r], -1), axis=0, keepdims=True)
            plan[10 + block : 11 + block, first : first + 6] = chosen
            plan[12 + block : 13 + block, first : first + 6] = kind
            plan[14 + block : 15 + block, first : first + 6] = quadrant
    plan[0:1, 65:66] = split


def arrived(plan, base, table, halo, blocks, fine):
    sub, lane = iotas()
    sub, lane = sub[:5], lane[:5]

    def rows(slot, j, part):
        first = 10 * (j ^ 1) + 5 * part
        return table[slot, first : first + 5, :]

    spread = (lane >> 5) * 16 + ((lane & 15) >> 1)
    for block in range(blocks):
        for j in range(6):
            kind = spread_rows(plan, 12 + block, base + j, 5)
            near = jnp.maximum(number(plan, block, base + j), 0)
            slot = jnp.maximum(number(plan, 10 + block, base + j), 0)
            quadrant = spread_rows(plan, 14 + block, base + j, 5)
            source = jnp.where(quadrant < 2, rows(slot, j, 0), rows(slot, j, 1))
            source = jnp.where((quadrant & 1) == 1, lanes(source, -8), source)
            rest = [WEIGHTS[q] for q in LISTS[j ^ 1]]
            straight = rest.index(WEIGHTS[1])
            rest = jnp.where(sub == straight, jnp.float32(WEIGHTS[1]), jnp.float32(WEIGHTS[7]))
            for h in range(2):
                coarse = pick(lanes(source, 64) if h else source, spread)
                value = jnp.where(kind == 0, rows(near, j, h), jnp.where(kind == 1, coarse, rest))
                r = 10 * j + 5 * h
                if fine:
                    value = jnp.where(kind == 2, halo[block, r : r + 5, :], value)
                halo[block, r : r + 5, :] = value


def arrived_fine(plan, base, table, halo, blocks):
    _, lane = iotas()
    lane = lane[:5]
    odd_v, odd_u = (lane & 1) == 1, ((lane >> 4) & 1) == 1
    gather = (2 * ((lane >> 4) & 3) + (lane >> 6)) * 16 + 2 * (lane & 7) + ((lane >> 3) & 1)
    for block in range(blocks):
        for j in range(6):
            first = 10 * (j ^ 1)
            for a in range(2):
                pairs = []
                for h in range(2):
                    sums = []
                    for b in range(2):
                        place = 2 + 4 * block + 2 * a + b
                        slot = jnp.maximum(number(plan, place, base + j), 0)
                        named = spread_rows(plan, place, base + j, 5) >= 0
                        scale = jnp.where(named, jnp.float32(0.25), jnp.float32(0.0))
                        v = table[slot, first + 5 * h : first + 5 * h + 5, :] * scale
                        sums.append(v + lanes(v, 1 if b else -1))
                    v = jnp.where(odd_v, sums[1], sums[0])
                    pairs.append(v + lanes(v, 16 if h else -16))
                r = 10 * j + 5 * a
                halo[block, r : r + 5, :] = pick(jnp.where(odd_u, pairs[1], pairs[0]), gather)


def stream(src, dst, plan, base, table, halo, blocks, done):
    sub, lane = iotas()
    odd = (sub & 1) == 1
    xl, yh = sub // 4, (sub // 2) % 2
    z = lane & 15

    def both(one, two):
        return jnp.where(odd, two, one)

    def plane(j, i, h):
        r = 10 * j + 5 * h + i
        return both(bulk(halo.at[0], r), bulk(halo.at[1], r))

    def edge_row(q, e, h):
        a = [n for n in range(3) if VELOCITIES[q][n]][0]
        j = 2 * a + (0 if VELOCITIES[q][a] > 0 else 1)
        r = 10 * j + 5 * h + LISTS[j].index(q)
        found = []
        for block in range(blocks):
            slot = jnp.maximum(number(plan, block, base + e), 0)
            good = spread_rows(plan, block, base + e, 8) >= 0
            found.append(jnp.where(good, bulk(table.at[slot], r), jnp.float32(WEIGHTS[q])))
        return both(*found)

    for q in range(19):
        c = VELOCITIES[q]
        moving = [a for a in range(3) if c[a]]
        e = VELOCITIES.index(tuple(-v for v in c)) - 1
        planes = {}
        for a in moving:
            j = 2 * a + (0 if c[a] < 0 else 1)
            i = LISTS[j ^ 1].index(q)
            planes[a] = [plane(j, i, h) for h in range(2)]
        if c[1]:
            up = c[1] > 0
            y_edge = lane >= 112 if up else lane < 16
            inner = yh == (1 if up else 0)
            beside = [jnp.where(xl == 0, v, lanes(v, -16)) for v in planes[1]]

            def joined(v, border):
                return jnp.where(y_edge, jnp.where(inner, subs(v, 2 * c[1]), border), v)

        if c[2]:
            z_edge = z == (0 if c[2] > 0 else 15)
            tile_of = z & 3 if c[2] > 0 else (15 - z) & 3
            index = (2 * tile_of + xl) * 16 + ((yh * 8 + (lane >> 4) - c[1]) & 15)
            columns = []
            for h in range(2):
                v = planes[2][h]
                if c[1]:
                    line = edge_row(q, e, h)
                    place, natural = (15 if c[1] > 0 else 0), (15 if c[2] > 0 else 0)
                    if place != natural:
                        line = lanes(line, place - natural)
                    v = jnp.where(z == place, line, v)
                columns.append(pick(v, index))
        shift = 16 * c[1] + c[2]
        first = 8 + 4 * c[0]
        for t in range(TILES):
            h, k = t // 4, t % 4
            v = tile(src, q, t)
            if c[1]:
                turn = (112 if c[1] > 0 else 0) - 32 * k
                v = joined(v, lanes(beside[h], turn) if turn % 128 else beside[h])
            if shift:
                v = lanes(v, shift)
            if c[2]:
                v = jnp.where(z_edge, lanes(columns[h], -k * c[2]) if k else columns[h], v)
            dst[q, first + 8 * t : first + 8 * t + 8, :] = v
        if c[0]:
            v = jnp.where(yh == 1, planes[0][1], planes[0][0])
            if c[1]:
                v = lanes(joined(v, edge_row(q, e, 1 if c[1] > 0 else 0)), shift)
            if c[2]:
                line = jnp.where(yh == 1, edge_row(q, e, 1), edge_row(q, e, 0))
                v = jnp.where(z_edge, lanes(line, -15 * c[2]), lanes(v, shift))
            r = 8 if c[0] > 0 else 68
            dst[q, r : r + 4, :] = v[:4]
        done(q)


def nothing(_):
    pass


def first_kernel(level_hbm, pops_hbm, mask_hbm, star, out, mask, level_ref, pops, sems):
    def part(t):
        here = pl.ds(64 * t, 64)
        return pltpu.make_async_copy(pops_hbm.at[:, here, :], pops.at[:, here, :], sems.at[t])

    small = [
        pltpu.make_async_copy(level_hbm, level_ref, sems.at[TILES]),
        pltpu.make_async_copy(mask_hbm, mask, sems.at[TILES + 1]),
    ]
    parts = [part(t) for t in range(1)]
    for copy in small + parts:
        copy.start()
    for copy in small:
        copy.wait()
    level = level_ref[lax.axis_index("section")]

    @pl.when(level >= 1)
    def _():
        collide(pops, 0, star, mask, relax_rate(level), lambda t: parts[t // 8].wait() if t % 8 == 0 else None)

    @pl.when(level < 1)
    def _():
        for copy in parts:
            copy.wait()
        star[...] = pops[...]

    export(star, out)


def plan_kernel(sizes, level_hbm, near_hbm, link_hbm, plan, level_ref, near, links, packed_plan, sems):
    copies = [
        pltpu.make_async_copy(level_hbm, level_ref, sems.at[0]),
        pltpu.make_async_copy(near_hbm, near, sems.at[1]),
        pltpu.make_async_copy(link_hbm, links, sems.at[2]),
    ]
    for copy in copies:
        copy.start()
    for copy in copies:
        copy.wait()
    me = (lax.axis_index("section"), lax.axis_index("member"))
    plan_rows(level_ref, near, links, packed_plan, me, sizes)
    for lane in [*range(18), *range(32, 50), 64, 65]:
        r = entry(0, lane)
        plan[r : r + 16, :] = jnp.broadcast_to(packed_plan[:, lane : lane + 1], (16, 128))


def gathered(parts, table):
    slot = 0
    for part in parts:
        for r in range(0, part.shape[0], PLANES):
            table[slot, :PLANES] = part[r : r + PLANES, :]
            slot += 1


def settle_kernel(plan, star, result, sems):
    @pl.when(number(plan, 0, 64) < 2)
    def _():
        copy = pltpu.make_async_copy(star, result, sems.at[0])
        copy.start()
        copy.wait()


def middle_kernel(blocks, plan, star, mask, own, own2, chip, near, far, dst, out, table, halo, moved):
    level = number(plan, 0, 64)

    @pl.when(level >= 1)
    def _():
        gathered((own, own2, chip, near, far), table)

        @pl.when(number(plan, 0, 65) > 0)
        def _():
            arrived_fine(plan, 0, table, halo, blocks)

        arrived(plan, 0, table, halo, blocks, True)
        stream(star, moved, plan, 0, table, halo, blocks, nothing)

    @pl.when(level < 1)
    def _():
        dst[...] = star[...]

    @pl.when(level == 1)
    def _():
        dst[...] = moved[:, 8 : 8 + ROWS, :]

    @pl.when(level == 2)
    def _():
        collide(moved, 8, dst, mask, relax_rate(level), nothing)

    export(dst, out)


def last_kernel(blocks, plan, star, own, own2, chip, near, far, settled, result, table, halo, moved, sems):
    @pl.when(number(plan, 0, 64) == 2)
    def _():
        copies = [
            pltpu.make_async_copy(moved.at[q, 8 : 8 + ROWS], result.at[q], sems.at[q]) for q in range(19)
        ]
        gathered((own, own2, chip, near, far), table)
        arrived(plan, 32, table, halo, blocks, False)
        stream(star, moved, plan, 32, table, halo, blocks, lambda q: copies[q].start())
        for copy in copies:
            copy.wait()


def swap(x, sections, members, target):
    pairs = []
    for s in range(sections):
        for m in range(members):
            t = target(s, m)
            if 0 <= t[1] < members:
                pairs.append((s * members + m, t[0] * members + t[1]))
    return lax.ppermute(x, ("section", "member"), pairs)


def exchange(exports, sections, members, last):
    me = lax.axis_index("section")

    def named(x, target):
        return swap(x, sections, members, target)

    def across(d):
        def target(s, m):
            low, high = min(s, s ^ d), max(s, s ^ d)
            needed = low >= 1 if last else (low, high) != (0, sections - 1)
            return (s ^ d, m) if needed else (s, m ^ 1)

        return target

    def beside(s, m):
        if last and s < 2:
            return (s, m ^ 1)
        t = ((m + 1) ^ 1) - 1
        return (s, t) if 0 <= t < members else (s ^ 1, m)

    parts = [exports] + [named(exports, across(d)) for d in range(1, sections)]
    first = jnp.concatenate(parts[:2], axis=0)
    if last:
        second = []
        for t in range(1, sections - 2):
            value = parts[sections - 1]
            for d in range(2, sections - 1):
                value = jnp.where(me ^ d == t, parts[d], value)
            second.append(value)
        second = jnp.concatenate(second, axis=0)
    else:
        second = jnp.concatenate(parts[2:], axis=0)
    near = named(first, beside)
    far = named(second, beside)
    chip = named(jnp.concatenate([first, second], axis=0), lambda s, m: (s, m ^ 1))
    return first, second, chip, near, far


def packed(x):
    n, cells = x.shape[0], x.shape[-1]
    x = x.reshape(n, -1, cells // 128, 128)
    return x.transpose(1, 2, 0, 3).reshape(-1, n * cells // 128, 128)


VMEM = pl.BlockSpec(memory_space=pltpu.VMEM)
HBM = pl.BlockSpec(memory_space=pltpu.HBM)


def body(populations, fluid_mask, section_level, neighbours, interface):
    sections, members = lax.axis_size("section"), lax.axis_size("member")
    blocks, _, cells = populations.shape
    sizes = (sections, members, blocks)
    params = pltpu.CompilerParams(vmem_limit_bytes=16 << 20)
    pops = packed(populations)
    mask = packed(fluid_mask)[0]
    links = interface.transpose(0, 2, 1)
    field = jax.ShapeDtypeStruct(pops.shape, jnp.float32)
    planes = jax.ShapeDtypeStruct((blocks * PLANES, 128), jnp.float32)
    halo = pltpu.VMEM((blocks, ROWS, 128), jnp.float32)
    moved = pltpu.VMEM((19, ROWS + 16, 128), jnp.float32)

    def fixed(*values):
        return tuple(pltpu.with_memory_space_constraint(x, pltpu.HBM) for x in values)

    star, exports, mask = pl.pallas_call(
        first_kernel,
        out_shape=(field, planes, jax.ShapeDtypeStruct(mask.shape, jnp.int32)),
        in_specs=[HBM] * 3,
        out_specs=(VMEM,) * 3,
        scratch_shapes=[
            pltpu.SMEM(section_level.shape, jnp.int32),
            pltpu.VMEM(pops.shape, jnp.float32),
            pltpu.SemaphoreType.DMA((TILES + 2,)),
        ],
        compiler_params=params,
        name="first",
    )(*fixed(section_level, pops, mask))
    plan = pl.pallas_call(
        functools.partial(plan_kernel, sizes),
        out_shape=jax.ShapeDtypeStruct((16 * 38, 128), jnp.int32),
        in_specs=[HBM] * 3,
        out_specs=VMEM,
        scratch_shapes=[
            pltpu.SMEM(section_level.shape, jnp.int32),
            pltpu.VMEM(neighbours.shape, jnp.int32),
            pltpu.VMEM(links.shape, jnp.int32),
            pltpu.VMEM((16, 128), jnp.int32),
            pltpu.SemaphoreType.DMA((3,)),
        ],
        compiler_params=params,
        name="plan",
    )(*fixed(section_level, neighbours, links))
    parts = exchange(exports, sections, members, False)
    star, exports = pl.pallas_call(
        functools.partial(middle_kernel, blocks),
        out_shape=(field, planes),
        in_specs=[VMEM] * 8,
        out_specs=(VMEM, VMEM),
        scratch_shapes=[pltpu.VMEM((3 * sections * blocks, ROWS, 128), jnp.float32), halo, moved],
        compiler_params=params,
        name="middle",
    )(plan, star, mask, *parts)
    settled = pl.pallas_call(
        settle_kernel,
        out_shape=field,
        in_specs=[VMEM] * 2,
        out_specs=HBM,
        scratch_shapes=[pltpu.SemaphoreType.DMA((1,))],
        compiler_params=params,
        name="settled",
    )(plan, star)
    parts = exchange(exports, sections, members, True)
    result = pl.pallas_call(
        functools.partial(last_kernel, blocks),
        out_shape=field,
        in_specs=[VMEM] * 7 + [HBM],
        out_specs=HBM,
        input_output_aliases={7: 0},
        scratch_shapes=[
            pltpu.VMEM((3 * (sections - 1) * blocks, ROWS, 128), jnp.float32),
            halo,
            moved,
            pltpu.SemaphoreType.DMA((19,)),
        ],
        compiler_params=params,
        name="last",
    )(plan, star, *parts, settled)
    out = result.reshape(19, cells // 128, blocks, 128).transpose(2, 0, 1, 3)
    return out.reshape(blocks, 19, cells)


def solution(mesh):
    return jax.shard_map(
        body,
        mesh=mesh,
        in_specs=(
            P(("section", "member"), None, None),
            P(("section", "member"), None),
            P(),
            P(("section", "member"), None),
            P(("section", "member"), None, None),
        ),
        out_specs=P(("section", "member"), None, None),
        check_vma=False,
    )
```
